32 devices in a mesh: depth: 4 (over x, core), freq: 8 (over z, y).
Axes of the slice: x: 2, y: 2, z: 4, core: 2. Of those that a mesh axis runs over, the one named last changes fastest.
Arguments:
- slowness: float32 [32, 2048], P('depth'), may hold values from 0.2 to 1
- reflect: float32 [32, 2048], P('depth'), may hold values from -0.6 to 0.6
- omega: float32 [16], P('freq'), may hold values from 1 to 6
- spread_coef: float32 [16], P('freq'), may hold values from 0.04 to 0.24
- wavelet: float32 [16, 2], P('freq'), may hold values from -4 to 4
- ray_param: float32 [8], replicated, may hold values from -0.03 to 0.03
- source_cell: int32 [8], replicated, may hold values from 0 to 2047
- aperture_tile: int32 [8], replicated, may hold values from 0 to 8
- receiver_tile: int32 [8], replicated, may hold values from 0 to 12
- observed: float32 [8, 16, 2, 2048], P(None, 'freq'), may hold values from -6 to 6
Outputs:
- image_grad: float32 [32, 32, 2048], P('depth', None, 'freq')
The draws below stay inside these ranges and needn't reach their ends.
All inputs are finite; a program needn't handle non-finite values.
Results may differ from the reference program's by a relative error of at most 0.00013.
Values sent between devices are 32-bit elements; how exact they have to be, the bound alone decides.
No kernel may reach another device: no remote copies, remote signals or barrier semaphores. Data moves between devices by JAX's collectives and lax.ppermute only.
A program may use at most 64 MiB of HBM per device.

```python
import math
import jax
import jax.numpy as jnp
from jax import lax

NXW = 2048
HOFF = 32
SHOTS = 8
FREQ = 16
NZ = 32
APT = 8
RCV = 4


def touch_ends(entries, key, low, top_value):
    extent = entries.shape
    spot = [jax.random.randint(jax.random.fold_in(key, axis), (), 0, extent[axis]) for axis in range(len(extent))]
    entries = entries.at[tuple(spot)].set(low)
    longest = extent.index(max(extent))
    spot[longest] = (spot[longest] + 1) % extent[longest]
    return entries.at[tuple(spot)].set(top_value)


def block_scale(own_key, shape, cuts, smallest, high):
    def one(axis_at, blocks):
        draws = jax.random.uniform(jax.random.fold_in(jax.random.fold_in(own_key, 6), axis_at), (blocks,), jnp.float32, smallest / len(cuts), high / len(cuts))
        return jnp.repeat(jnp.exp(draws), shape[axis_at] // blocks).reshape((-1,) + (1,) * (len(shape) - axis_at - 1))

    factor_of = one(*cuts[0])
    for cut in cuts[1:]:
        factor_of = factor_of * one(*cut)
    return factor_of


def centred(rng, dims, scale, limit, shards=(), held_as=jnp.bfloat16):
    loudness = block_scale(rng, dims, shards, -0.22, 0.18) if shards else 1.0
    result = jax.random.normal(rng, dims, jnp.float32) * scale * loudness
    return jnp.minimum(jnp.maximum(result, -limit), limit).astype(held_as)


def setup_inputs(seed: int = 0) -> dict:
    key_of = jax.random.split(jax.random.key(seed), 11)
    return {
        "slowness": jnp.clip(0.2 + 0.8 * jax.random.uniform(key_of[0], (NZ, NXW), jnp.float32) ** block_scale(key_of[0], (NZ, NXW), ((0, 4),), -0.2, 0.2), 0.2, 1.0),
        "reflect": centred(key_of[1], (NZ, NXW), 0.1, 0.6, ((0, 4),), jnp.float32),
        "omega": jnp.clip(jnp.exp(math.log(6.0) - 1.7917595 * jax.random.uniform(key_of[2], (FREQ,), jnp.float32) ** block_scale(key_of[2], (FREQ,), ((0, 8),), -0.2, 0.2)), 1.0, 6.0),
        "spread_coef": jnp.clip(jnp.exp(math.log(0.24) - 1.7917595 * jax.random.uniform(key_of[3], (FREQ,), jnp.float32) ** block_scale(key_of[3], (FREQ,), ((0, 8),), -0.2, 0.2)), 0.04, 0.24),
        "wavelet": centred(key_of[4], (FREQ, 2), 1.0, 4.0, ((0, 8),), jnp.float32),
        "ray_param": jnp.clip(jax.random.uniform(key_of[5], (SHOTS,), jnp.float32, -0.03, 0.03), -0.03, 0.03),
        "source_cell": touch_ends(jax.random.randint(key_of[6], (SHOTS,), 0, NXW), jax.random.fold_in(key_of[6], 1), 0, NXW - 1).astype(jnp.int32),
        "aperture_tile": touch_ends(jax.random.randint(key_of[7], (SHOTS,), 0, NXW // 128 - APT + 1), jax.random.fold_in(key_of[7], 1), 0, (NXW // 128 - APT + 1) - 1).astype(jnp.int32),
        "receiver_tile": touch_ends(jax.random.randint(key_of[8], (SHOTS,), 0, NXW // 128 - RCV + 1), jax.random.fold_in(key_of[8], 1), 0, (NXW // 128 - RCV + 1) - 1).astype(jnp.int32),
        "observed": centred(key_of[9], (SHOTS, FREQ, 2, NXW), 1.0, 6.0, ((1, 8),), jnp.float32),
    }


def tile_mask(start_tile, count, width):
    cells = jnp.arange(width, dtype=jnp.int32) // 128
    begin = start_tile[:, None]
    inside = (cells[None, :] >= begin) & (cells[None, :] < begin + count)
    return inside.astype(jnp.float32)[:, None, None, :]

def damping(coef):
    return 0.26 - jnp.sqrt(0.0625 - coef * coef)

def spread(field, real_coef, imag_coef):
    padded = jnp.pad(field, ((0, 0), (0, 0), (0, 0), (1, 1)))
    second = padded[..., 2:] + padded[..., :-2] - 2.0 * field
    real_c = real_coef[None, :, None]
    imag_c = imag_coef[None, :, None]
    real_part = field[:, :, 0] + real_c * second[:, :, 0] - imag_c * second[:, :, 1]
    imag_part = field[:, :, 1] + real_c * second[:, :, 1] + imag_c * second[:, :, 0]
    return jnp.stack([real_part, imag_part], axis=2)

def rotate(field, cosine, sine):
    real_part = field[:, :, 0] * cosine[None] - field[:, :, 1] * sine[None]
    imag_part = field[:, :, 0] * sine[None] + field[:, :, 1] * cosine[None]
    return jnp.stack([real_part, imag_part], axis=2)

def phases(omega, slow_row):
    angle = omega[:, None] * slow_row[None, :]
    return (jnp.cos(angle), jnp.sin(angle))

def source_field(omega, wavelet, ray_param, source_cell, mask, width):
    cells = jnp.arange(width, dtype=jnp.int32)
    dist = (cells[None, :] - source_cell[:, None]).astype(jnp.float32)
    angle = omega[None, :, None] * ray_param[:, None, None] * dist[:, None, :]
    cosine = jnp.cos(angle)
    sine = jnp.sin(angle)
    wave_re = wavelet[:, 0][None, :, None]
    wave_im = wavelet[:, 1][None, :, None]
    real_part = wave_re * cosine - wave_im * sine
    imag_part = wave_re * sine + wave_im * cosine
    return jnp.stack([real_part, imag_part], axis=2) * mask

def forward_step(source, scatter, slow_row, refl_row, omega, damp, coef, mask):
    cosine, sine = phases(omega, slow_row)
    weight = omega[None, :, None] * refl_row[None, None, :]
    born = jnp.stack([scatter[:, :, 0] - weight * source[:, :, 1], scatter[:, :, 1] + weight * source[:, :, 0]], axis=2)
    new_source = mask * rotate(spread(source, damp, coef), cosine, sine)
    new_scatter = mask * rotate(spread(born, damp, coef), cosine, sine)
    return (new_source, new_scatter)

def adjoint_step(adjoint, slow_row, omega, damp, coef, mask):
    cosine, sine = phases(omega, slow_row)
    turned = rotate(mask * adjoint, cosine, -sine)
    return spread(turned, damp, -coef)

def image_row(source, adjoint, omega, scale, offsets):
    count = source.shape[0] * source.shape[1]
    width = source.shape[-1]
    weighted = (source * (omega[None, :, None, None] / scale)).reshape(count, 2, width)
    flat_adj = adjoint.reshape(count, 2, width)
    half = offsets // 2
    src_pad = jnp.pad(weighted, ((0, 0), (0, 0), (half, half)))
    adj_pad = jnp.pad(flat_adj, ((0, 0), (0, 0), (half, half)))
    values = []
    for offset in range(offsets):
        src_seg = src_pad[:, :, offsets - offset:offsets - offset + width]
        adj_seg = adj_pad[:, :, offset:offset + width]
        values.append(lax.optimization_barrier(jnp.sum(src_seg[:, 0] * adj_seg[:, 1] - src_seg[:, 1] * adj_seg[:, 0], axis=0)))
    return jnp.stack(values, axis=0)

def reference(slowness, reflect, omega, spread_coef, wavelet, ray_param, source_cell, aperture_tile, receiver_tile, observed):
    mask = tile_mask(aperture_tile, NXW // 256, NXW)
    rmask = tile_mask(receiver_tile, max(1, NXW // 512), NXW)
    damp = damping(spread_coef)
    start = source_field(omega, wavelet, ray_param, source_cell, mask, NXW)
    scale = math.sqrt(SHOTS * FREQ)

    def down(carry, rows):
        source, scatter = carry
        new_source, new_scatter = forward_step(source, scatter, rows[0], rows[1], omega, damp, spread_coef, mask)
        return ((new_source, new_scatter), source)
    (last_source, bottom), stored = lax.scan(down, (start, jnp.zeros_like(start)), (slowness, reflect))
    adjoint_bottom = rmask * (bottom - observed)

    def up(adjoint, rows):
        new_adjoint = adjoint_step(adjoint, rows[0], omega, damp, spread_coef, mask)
        return (new_adjoint, image_row(rows[1], new_adjoint, omega, scale, HOFF))
    final_adj, image = lax.scan(up, adjoint_bottom, (slowness, stored), reverse=True)
    return image
```

```python
import functools
import math

import jax
import jax.numpy as jnp
from jax import lax
from jax.experimental import pallas as pl
from jax.experimental.pallas import tpu as pltpu
from jax.sharding import PartitionSpec as P

HOFF = 32
LANES = 128
SUBS = 8


def sincos(angle):
    turns = jnp.floor(angle * 0.6366197723675814 + 0.5)
    rem = angle - turns * 1.5703125
    rem = rem - turns * 4.837512969970703125e-4
    rem = rem - turns * 7.54978995489188216e-8
    sq = rem * rem
    sin_p = rem + rem * sq * (-1.6666654611e-1 + sq * (8.3321608736e-3 + sq * -1.9515295891e-4))
    cos_p = (1.0 - 0.5 * sq) + sq * sq * (
        4.166664568298827e-2 + sq * (-1.388731625493765e-3 + sq * 2.443315711809948e-5)
    )
    quad = turns.astype(jnp.int32)
    odd = (quad & 1) == 1
    sine = jnp.where(odd, cos_p, sin_p)
    cosine = jnp.where(odd, sin_p, cos_p)
    sine = jnp.where((quad & 2) == 2, -sine, sine)
    cosine = jnp.where(((quad + 1) & 2) == 2, -cosine, cosine)
    return cosine, sine


def pick(values, index):
    return jnp.take_along_axis(values, index, axis=1, mode="promise_in_bounds")


def split(values):
    high = values.astype(jnp.bfloat16)
    low = (values - high.astype(jnp.float32)).astype(jnp.bfloat16)
    return high, low


def migrate(
    pos, ray, cell, aper, recv, sr_ref, tab_ref, obs_ref, out_ref,
    nat, cos_c, sin_c, wgt_c, mask_s, phase_s, src_h, sct, adj, obs_n, src_n, adj_n, skew,
    *, dims,
):
    shots, nf, depth, zloc, cells, own, halo, block, scale = dims
    half = HOFF // 2
    win = own + 2 * halo
    per = LANES // shots
    zper = LANES // per
    span = own + HOFF
    f32 = jnp.float32
    group = pl.program_id(0)
    x_start = pos[0]
    dev = pos[1]
    z_first = dev * zloc

    lane = lax.broadcasted_iota(jnp.int32, (SUBS, LANES), 1)
    sub = lax.broadcasted_iota(jnp.int32, (SUBS, LANES), 0)
    lane_src = lane // (shots * nf)
    lane_shot = (lane // nf) % shots
    lane_f = lane_src * nf + lane % nf

    def row(k):
        return jnp.broadcast_to(tab_ref[k : k + 1, :], (SUBS, LANES))

    omega, coef, wave_re, wave_im = row(0), row(1), row(2), row(3)
    damp = 0.26 - jnp.sqrt(0.0625 - coef * coef)
    comp_f = lane % per
    comp_z = lane // per
    omega_c = pick(omega, (comp_f // nf) * (shots * nf) + comp_f % nf)

    def per_shot(ref, dtype):
        acc = jnp.zeros((SUBS, LANES), dtype)
        for s in range(shots):
            acc = jnp.where(lane_shot == s, ref[s], acc)
        return acc

    ray_l = per_shot(ray, f32)
    cell_l = per_shot(cell, jnp.int32)
    aper_l = per_shot(aper, jnp.int32)
    recv_l = per_shot(recv, jnp.int32)
    ntile = cells // LANES

    rows2 = 2 * depth
    for t in range(pl.cdiv(win, LANES)):
        blk = sr_ref[:, t * LANES : (t + 1) * LANES]
        blk = jnp.concatenate([blk, jnp.zeros((LANES - rows2, LANES), f32)], axis=0)
        nat[t * LANES : (t + 1) * LANES, :] = blk.T

    def rows_of(j):
        return pl.ds(j, SUBS, stride=block)

    def compact(zg, _):
        z = zg * zper + comp_z
        zrow = ((z // zloc) ^ dev) * zloc + z % zloc
        for j in range(block):
            v = nat[rows_of(j), :]
            c, s = sincos(omega_c * pick(v, zrow))
            cos_c[zg, j] = c
            sin_c[zg, j] = s
            wgt_c[zg, j] = omega_c * pick(v, zrow + depth)
        return 0

    lax.fori_loop(0, depth // zper, compact, 0)

    for j in range(block):
        x = x_start + sub * block + j
        tile = jnp.where(x < 0, -1, x // LANES)
        inside = (tile >= aper_l) & (tile < aper_l + ntile // 2) & (tile < ntile)
        m = inside.astype(f32)
        mask_s[j] = m
        dist = (x - cell_l).astype(f32)
        c, s = sincos(omega * ray_l * dist)
        src_h[0, 0, j] = (wave_re * c - wave_im * s) * m
        src_h[0, 1, j] = (wave_re * s + wave_im * c) * m
        sct[0, j] = jnp.zeros((SUBS, LANES), f32)
        sct[1, j] = jnp.zeros((SUBS, LANES), f32)

    def up_sub(v):
        return pltpu.roll(v, 1, 0)

    def down_sub(v):
        return pltpu.roll(v, SUBS - 1, 0)

    def forward(z, _):
        zg = z // zper
        idx = (z % zper) * per + lane_f

        def born(j):
            w = pick(wgt_c[zg, j], idx)
            sr, si = src_h[z, 0, j], src_h[z, 1, j]
            return sr, si, sct[0, j] - w * si, sct[1, j] + w * sr

        first = born(0)
        last = born(block - 1)
        before = [up_sub(v) for v in last]
        after = [down_sub(v) for v in first]
        now = first
        diff = [a - b for a, b in zip(now, before)]
        for j in range(block):
            nxt = after if j == block - 1 else (last if j == block - 2 else born(j + 1))
            step = [a - b for a, b in zip(nxt, now)]
            sec = [a - b for a, b in zip(step, diff)]
            m = mask_s[j]
            mc = m * pick(cos_c[zg, j], idx)
            ms = m * pick(sin_c[zg, j], idx)
            phase_s[z, 0, j] = mc
            phase_s[z, 1, j] = ms
            s_re = now[0] + (damp * sec[0] - coef * sec[1])
            s_im = now[1] + (damp * sec[1] + coef * sec[0])
            d_re = now[2] + (damp * sec[2] - coef * sec[3])
            d_im = now[3] + (damp * sec[3] + coef * sec[2])
            src_h[z + 1, 0, j] = s_re * mc - s_im * ms
            src_h[z + 1, 1, j] = s_re * ms + s_im * mc
            sct[0, j] = d_re * mc - d_im * ms
            sct[1, j] = d_re * ms + d_im * mc
            now, diff = nxt, step
        return 0

    lax.fori_loop(0, depth, forward, 0)

    for part in range(2):
        for t in range(pl.cdiv(win, LANES)):
            blk = obs_ref[:, part, :, t * LANES : (t + 1) * LANES].reshape(LANES, LANES)
            obs_n[part, t * LANES : (t + 1) * LANES, :] = blk.T
    for j in range(block):
        x = x_start + sub * block + j
        tile = jnp.where(x < 0, -1, x // LANES)
        inside = (tile >= recv_l) & (tile < recv_l + max(1, ntile // 4)) & (tile < ntile)
        m = inside.astype(f32)
        for part in range(2):
            adj[part, j] = m * (sct[part, j] - obs_n[part, rows_of(j), :])

    @pl.when(group == 0)
    def _():
        out_ref[...] = jnp.zeros(out_ref.shape, f32)

    weight = omega * scale
    nrow = span // 2
    ncol = pl.cdiv(nrow, LANES) * LANES
    lead = halo - half

    def image(z):
        zi = z - z_first
        for part in range(2):
            for j in range(block):
                src_n[part, rows_of(j), :] = src_h[z, part, j]
                adj_n[part, rows_of(j), :] = adj[part, j]
        for p in range(2):
            rows = pl.ds(lead + p, nrow, stride=2)
            y = lax.broadcasted_iota(jnp.int32, (nrow, LANES), 0) * 2 + (x_start + lead + p)
            inside = (y >= 0) & (y < cells)
            wt = jnp.broadcast_to(weight[:1], (nrow, LANES))
            left = jnp.concatenate([src_n[0, rows, :] * wt, src_n[1, rows, :] * (-wt)], axis=1)
            right = jnp.concatenate(
                [jnp.where(inside, adj_n[1, rows, :], 0.0), jnp.where(inside, adj_n[0, rows, :], 0.0)], axis=1
            )
            if ncol > nrow:
                right = jnp.concatenate([right, jnp.zeros((ncol - nrow, 2 * LANES), f32)], axis=0)
            lh, ll = split(left)
            rh, rl = split(right)
            dims_t = (((1,), (1,)), ((), ()))
            dot = functools.partial(lax.dot_general, dimension_numbers=dims_t, preferred_element_type=f32)
            prod = dot(lh, rl) + dot(ll, rh) + dot(lh, rh)
            for b in range(nrow // SUBS):
                v = prod[b * SUBS : (b + 1) * SUBS, :]
                v = pltpu.roll(v, (half - b * SUBS) % ncol, 1)[:, :LANES]
                for bit in (1, 2, 4):
                    v = jnp.where((sub & bit) != 0, pltpu.roll(v, LANES - bit, 1), v)
                skew[pl.ds(2 * b * SUBS + p, SUBS, stride=2), :] = v
        wide = pl.cdiv(span, LANES) * LANES
        turned = jnp.concatenate([skew[t * LANES : (t + 1) * LANES, :].T[:HOFF] for t in range(wide // LANES)], axis=1)
        sub_w = lax.broadcasted_iota(jnp.int32, (SUBS, wide), 0)
        for q in range(HOFF // SUBS):
            v = turned[q * SUBS : (q + 1) * SUBS, :]
            v = pltpu.roll(v, (q * SUBS - HOFF) % wide, 1)
            for bit in (1, 2, 4):
                v = jnp.where((sub_w & bit) != 0, pltpu.roll(v, bit, 1), v)
            out_ref[zi, q * SUBS : (q + 1) * SUBS, :] += v[:, :own]

    def backward(k, _):
        z = depth - 1 - k

        def turn(j):
            mc, ms = phase_s[z, 0, j], phase_s[z, 1, j]
            ar, ai = adj[0, j], adj[1, j]
            return ar * mc + ai * ms, ai * mc - ar * ms

        first = turn(0)
        last = turn(block - 1)
        before = [up_sub(v) for v in last]
        after = [down_sub(v) for v in first]
        now = first
        diff = [a - b for a, b in zip(now, before)]
        for j in range(block):
            nxt = after if j == block - 1 else (last if j == block - 2 else turn(j + 1))
            step = [a - b for a, b in zip(nxt, now)]
            sec = [a - b for a, b in zip(step, diff)]
            adj[0, j] = now[0] + (damp * sec[0] + coef * sec[1])
            adj[1, j] = now[1] + (damp * sec[1] - coef * sec[0])
            now, diff = nxt, step

        @pl.when(z < z_first + zloc)
        def _():
            image(z)

        return 0

    lax.fori_loop(0, depth - z_first, backward, 0)


def local(
    slowness, reflect, omega, spread_coef, wavelet, ray_param, source_cell, aperture_tile, receiver_tile, observed,
):
    nd = lax.axis_size("depth")
    nq = lax.axis_size("freq")
    dev = lax.axis_index("depth")
    col = lax.axis_index("freq")
    zloc, cells = slowness.shape
    depth = zloc * nd
    shots, nf, _, _ = observed.shape
    own = cells // nq
    halo = HOFF // 2 + 2 * depth
    win = own + 2 * halo
    block = win // SUBS
    wide = pl.cdiv(win, LANES) * LANES
    per = LANES // shots
    slot = shots * nf
    groups = nq * slot // LANES
    srcs = LANES // slot

    small = jnp.stack([omega, spread_coef, wavelet[:, 0], wavelet[:, 1]])
    lanes = jnp.arange(groups * LANES, dtype=jnp.int32)
    small = jnp.tile(small, (1, groups * LANES // nf))
    small = jnp.pad(jnp.where((lanes // slot == col)[None, :], small, 0.0), ((0, 4), (0, 0)))
    bit = 1
    while bit < nq:
        small = small + lax.ppermute(small, "freq", [(k, k ^ bit) for k in range(nq)])
        bit *= 2

    both = jnp.pad(jnp.stack([slowness, reflect]), ((0, 0), (0, 0), (halo, halo + wide - win)))
    both = lax.dynamic_slice_in_dim(both, col * own, wide, 2)
    bit = 1
    while bit < nd:
        both = jnp.concatenate([both, lax.ppermute(both, "depth", [(k, k ^ bit) for k in range(nd)])], axis=1)
        bit *= 2
    both = both.reshape(2 * depth, wide)

    turned = jnp.pad(observed.transpose(2, 0, 1, 3).reshape(2, slot, cells), ((0, 0), (0, 0), (halo, halo + wide - win)))
    parts = jnp.stack([turned[:, :, k * own : k * own + wide] for k in range(nq)])
    parts = lax.all_to_all(parts, "freq", 0, 0)

    pos = jnp.stack([col * own - halo, dev]).astype(jnp.int32)
    dims = (shots, nf, depth, zloc, cells, own, halo, block, 1.0 / math.sqrt(shots * nf * nq))
    smem = pl.BlockSpec(memory_space=pltpu.SMEM)
    natr = wide
    grid_spec = pltpu.PrefetchScalarGridSpec(
        num_scalar_prefetch=0,
        grid=(groups,),
        in_specs=[
            smem, smem, smem, smem, smem,
            pl.BlockSpec((2 * depth, wide), lambda g: (0, 0)),
            pl.BlockSpec((8, LANES), lambda g: (0, g)),
            pl.BlockSpec((srcs, 2, slot, wide), lambda g: (g, 0, 0, 0)),
        ],
        out_specs=pl.BlockSpec((zloc, HOFF, own), lambda g: (0, 0, 0)),
        scratch_shapes=[
            pltpu.VMEM((natr, LANES), jnp.float32),
            pltpu.VMEM((depth * per // LANES, block, SUBS, LANES), jnp.float32),
            pltpu.VMEM((depth * per // LANES, block, SUBS, LANES), jnp.float32),
            pltpu.VMEM((depth * per // LANES, block, SUBS, LANES), jnp.float32),
            pltpu.VMEM((block, SUBS, LANES), jnp.float32),
            pltpu.VMEM((depth, 2, block, SUBS, LANES), jnp.float32),
            pltpu.VMEM((depth + 1, 2, block, SUBS, LANES), jnp.float32),
            pltpu.VMEM((2, block, SUBS, LANES), jnp.float32),
            pltpu.VMEM((2, block, SUBS, LANES), jnp.float32),
            pltpu.VMEM((2, natr, LANES), jnp.float32),
            pltpu.VMEM((2, natr, LANES), jnp.float32),
            pltpu.VMEM((2, natr, LANES), jnp.float32),
            pltpu.VMEM((pl.cdiv(own + HOFF, LANES) * LANES, LANES), jnp.float32),
        ],
    )
    image = pl.pallas_call(
        functools.partial(migrate, dims=dims),
        out_shape=jax.ShapeDtypeStruct((zloc, HOFF, own), jnp.float32),
        grid_spec=grid_spec,
        compiler_params=pltpu.CompilerParams(vmem_limit_bytes=56 << 20),
    )(pos, ray_param, source_cell, aperture_tile, receiver_tile, both, small, parts)
    return image


def solution(mesh):
    return jax.shard_map(
        local,
        mesh=mesh,
        in_specs=(
            P("depth", None), P("depth", None), P("freq"), P("freq"), P("freq", None),
            P(), P(), P(), P(), P(None, "freq", None, None),
        ),
        out_specs=P("depth", None, "freq"),
        check_vma=False,
    )
```

```python
import functools
import math

import jax
import jax.numpy as jnp
from jax import lax
from jax.experimental import pallas as pl
from jax.experimental.pallas import tpu as pltpu
from jax.sharding import PartitionSpec as P

HOFF = 32
LANES = 128
SUBS = 8


def sincos(angle):
    turns = jnp.floor(angle * 0.6366197723675814 + 0.5)
    rem = angle - turns * 1.5703125
    rem = rem - turns * 4.837512969970703125e-4
    rem = rem - turns * 7.54978995489188216e-8
    sq = rem * rem
    sin_p = rem + rem * sq * (-1.6666654611e-1 + sq * (8.3321608736e-3 + sq * -1.9515295891e-4))
    cos_p = (1.0 - 0.5 * sq) + sq * sq * (
        4.166664568298827e-2 + sq * (-1.388731625493765e-3 + sq * 2.443315711809948e-5)
    )
    quad = turns.astype(jnp.int32)
    odd = (quad & 1) == 1
    sine = jnp.where(odd, cos_p, sin_p)
    cosine = jnp.where(odd, sin_p, cos_p)
    sine = jnp.where((quad & 2) == 2, -sine, sine)
    cosine = jnp.where(((quad + 1) & 2) == 2, -cosine, cosine)
    return cosine, sine


def pick(values, index):
    return jnp.take_along_axis(values, index, axis=1, mode="promise_in_bounds")


def split(values):
    high = values.astype(jnp.bfloat16)
    low = (values - high.astype(jnp.float32)).astype(jnp.bfloat16)
    return high, low


def pack(pos, omega, coef, wave, slow_ref, refl_ref, obs_ref, both_ref, *outs, dims, peers):
    shots, nf, depth, zloc, cells, own, halo, edge, wide, obsw = dims
    col = pos[0]

    def window(load, first, width):
        tiles = pl.cdiv(width, LANES) + 1
        low = first + cells * LANES
        base = low // LANES - cells
        off = low % LANES
        cut = [
            load(pl.ds(pl.multiple_of(jnp.clip(base + t, 0, cells // LANES - 1) * LANES, LANES), LANES))
            for t in range(tiles)
        ]
        full = jnp.concatenate(cut, axis=1)
        return pltpu.roll(full, (tiles * LANES - off) % (tiles * LANES), 1)[:, :width]

    first = col * own - halo
    both_ref[0] = window(lambda c: slow_ref[:, c], first, wide)
    both_ref[1] = window(lambda c: refl_ref[:, c], first, wide)
    lane = lax.broadcasted_iota(jnp.int32, (1, obsw), 1) % nf

    def spread(read):
        acc = jnp.zeros((1, obsw), jnp.float32)
        for f in range(nf):
            acc = jnp.where(lane == f, read(f), acc)
        return acc

    table = jnp.concatenate(
        [
            spread(lambda f: omega[f]),
            spread(lambda f: coef[f]),
            spread(lambda f: wave[f, 0]),
            spread(lambda f: wave[f, 1]),
            jnp.zeros((4, obsw), jnp.float32),
        ],
        axis=0,
    )
    for k, out in enumerate(outs):
        dest = peers(col, k)
        out[0, : 2 * shots * nf] = window(lambda c: obs_ref[:, c], dest * own - edge, obsw)
        out[0, 2 * shots * nf :] = table


def migrate(
    pos, ray, cell, aper, recv, *refs, dims, srcs, zsrc,
):
    sr_refs, (out_ref, nat, cos_c, sin_c, wgt_c, mask_s, phase_s, src_h, sct, adj, obs_n, src_n, adj_n, skew) = refs[: zsrc + srcs], refs[zsrc + srcs :]
    sr_refs, obs_refs = sr_refs[:zsrc], sr_refs[zsrc:]
    shots, nf, depth, zloc, cells, own, halo, edge, block, scale = dims
    half = HOFF // 2
    win = own + 2 * halo
    per = LANES // shots
    zper = LANES // per
    span = own + HOFF
    f32 = jnp.float32
    group = pl.program_id(0)
    x_start = pos[0] * own - halo
    dev = pos[1]
    z_first = dev * zloc

    lane = lax.broadcasted_iota(jnp.int32, (SUBS, LANES), 1)
    sub = lax.broadcasted_iota(jnp.int32, (SUBS, LANES), 0)
    lane_src = lane // (shots * nf)
    lane_shot = (lane // nf) % shots
    lane_f = lane_src * nf + lane % nf

    obs_rows = 2 * shots * nf
    table = jnp.zeros((SUBS, LANES), jnp.float32)
    for k in range(srcs):
        table = jnp.where(lane_src == k, obs_refs[k][obs_rows:, :LANES], table)

    def row(k):
        return jnp.broadcast_to(table[k : k + 1, :], (SUBS, LANES))

    omega, coef, wave_re, wave_im = row(0), row(1), row(2), row(3)
    damp = 0.26 - jnp.sqrt(0.0625 - coef * coef)
    comp_f = lane % per
    comp_z = lane // per
    omega_c = pick(omega, (comp_f // nf) * (shots * nf) + comp_f % nf)

    def per_shot(ref, dtype):
        acc = jnp.zeros((SUBS, LANES), dtype)
        for s in range(shots):
            acc = jnp.where(lane_shot == s, ref[s], acc)
        return acc

    ray_l = per_shot(ray, f32)
    cell_l = per_shot(cell, jnp.int32)
    aper_l = per_shot(aper, jnp.int32)
    recv_l = per_shot(recv, jnp.int32)
    ntile = cells // LANES

    rows2 = 2 * depth
    for t in range(pl.cdiv(win, LANES)):
        cut = slice(t * LANES, (t + 1) * LANES)
        blk = [r[part, :, cut] for part in range(2) for r in sr_refs]
        blk = jnp.concatenate(blk + [jnp.zeros((LANES - rows2, LANES), f32)], axis=0)
        nat[t * LANES : (t + 1) * LANES, :] = blk.T

    def rows_of(j):
        return pl.ds(j, SUBS, stride=block)

    def compact(zg, _):
        z = zg * zper + comp_z
        zrow = ((z // zloc) ^ dev) * zloc + z % zloc
        for j in range(block):
            v = nat[rows_of(j), :]
            c, s = sincos(omega_c * pick(v, zrow))
            cos_c[zg, j] = c
            sin_c[zg, j] = s
            wgt_c[zg, j] = omega_c * pick(v, zrow + depth)
        return 0

    lax.fori_loop(0, depth // zper, compact, 0)

    for j in range(block):
        x = x_start + sub * block + j
        tile = jnp.where(x < 0, -1, x // LANES)
        inside = (tile >= aper_l) & (tile < aper_l + ntile // 2) & (tile < ntile)
        m = inside.astype(f32)
        mask_s[j] = m
        dist = (x - cell_l).astype(f32)
        c, s = sincos(omega * ray_l * dist)
        src_h[0, 0, j] = (wave_re * c - wave_im * s) * m
        src_h[0, 1, j] = (wave_re * s + wave_im * c) * m
        sct[0, j] = jnp.zeros((SUBS, LANES), f32)
        sct[1, j] = jnp.zeros((SUBS, LANES), f32)

    def up_sub(v):
        return pltpu.roll(v, 1, 0)

    def down_sub(v):
        return pltpu.roll(v, SUBS - 1, 0)

    def forward(z, _):
        zg = z // zper
        idx = (z % zper) * per + lane_f

        def born(j):
            w = pick(wgt_c[zg, j], idx)
            sr, si = src_h[z, 0, j], src_h[z, 1, j]
            return sr, si, sct[0, j] - w * si, sct[1, j] + w * sr

        first = born(0)
        last = born(block - 1)
        before = [up_sub(v) for v in last]
        after = [down_sub(v) for v in first]
        now = first
        diff = [a - b for a, b in zip(now, before)]
        for j in range(block):
            nxt = after if j == block - 1 else (last if j == block - 2 else born(j + 1))
            step = [a - b for a, b in zip(nxt, now)]
            sec = [a - b for a, b in zip(step, diff)]
            m = mask_s[j]
            mc = m * pick(cos_c[zg, j], idx)
            ms = m * pick(sin_c[zg, j], idx)
            phase_s[z, 0, j] = mc
            phase_s[z, 1, j] = ms
            s_re = now[0] + (damp * sec[0] - coef * sec[1])
            s_im = now[1] + (damp * sec[1] + coef * sec[0])
            d_re = now[2] + (damp * sec[2] - coef * sec[3])
            d_im = now[3] + (damp * sec[3] + coef * sec[2])
            src_h[z + 1, 0, j] = s_re * mc - s_im * ms
            src_h[z + 1, 1, j] = s_re * ms + s_im * mc
            sct[0, j] = d_re * mc - d_im * ms
            sct[1, j] = d_re * ms + d_im * mc
            now, diff = nxt, step
        return 0

    lax.fori_loop(0, depth, forward, 0)

    pad = halo - edge
    for part in range(2):
        obs_n[part, : pad + SUBS, :] = jnp.zeros((pad + SUBS, LANES), f32)
        obs_n[part, win - pad - SUBS : win, :] = jnp.zeros((pad + SUBS, LANES), f32)
    per_blk = LANES // obs_rows
    where_in = (lane_src % per_blk) * obs_rows + (lane % (shots * nf)) * 2
    for t in range(pl.cdiv(own + 2 * edge, LANES)):
        cut = slice(t * LANES, (t + 1) * LANES)
        turned = [
            jnp.concatenate([r[:obs_rows, cut] for r in obs_refs[q * per_blk : (q + 1) * per_blk]], axis=0).T
            for q in range(srcs // per_blk)
        ]
        rows_t = min(LANES, own + 2 * edge - t * LANES)
        for r in range(0, rows_t, SUBS):
            for part in range(2):
                v = pick(turned[0][r : r + SUBS], where_in + part)
                for q in range(1, srcs // per_blk):
                    v = jnp.where(lane_src // per_blk == q, pick(turned[q][r : r + SUBS], where_in + part), v)
                obs_n[part, pad + t * LANES + r : pad + t * LANES + r + SUBS, :] = v
    for j in range(block):
        x = x_start + sub * block + j
        tile = jnp.where(x < 0, -1, x // LANES)
        inside = (tile >= recv_l) & (tile < recv_l + max(1, ntile // 4)) & (tile < ntile)
        m = inside.astype(f32)
        for part in range(2):
            adj[part, j] = m * (sct[part, j] - obs_n[part, rows_of(j), :])

    @pl.when(group == 0)
    def _():
        out_ref[...] = jnp.zeros(out_ref.shape, f32)

    weight = omega * scale
    nrow = span // 2
    ncol = pl.cdiv(nrow, LANES) * LANES
    lead = halo - half

    def image(z):
        zi = z - z_first
        for part in range(2):
            for j in range(block):
                src_n[part, rows_of(j), :] = src_h[z, part, j]
                adj_n[part, rows_of(j), :] = adj[part, j]
        for p in range(2):
            rows = pl.ds(lead + p, nrow, stride=2)
            y = lax.broadcasted_iota(jnp.int32, (nrow, LANES), 0) * 2 + (x_start + lead + p)
            inside = (y >= 0) & (y < cells)
            wt = jnp.broadcast_to(weight[:1], (nrow, LANES))
            left = jnp.concatenate([src_n[0, rows, :] * wt, src_n[1, rows, :] * (-wt)], axis=1)
            right = jnp.concatenate(
                [jnp.where(inside, adj_n[1, rows, :], 0.0), jnp.where(inside, adj_n[0, rows, :], 0.0)], axis=1
            )
            if ncol > nrow:
                right = jnp.concatenate([right, jnp.zeros((ncol - nrow, 2 * LANES), f32)], axis=0)
            lh, ll = split(left)
            rh, rl = split(right)
            dims_t = (((1,), (1,)), ((), ()))
            dot = functools.partial(lax.dot_general, dimension_numbers=dims_t, preferred_element_type=f32)
            prod = dot(lh, rl) + dot(ll, rh) + dot(lh, rh)
            for b in range(nrow // SUBS):
                v = prod[b * SUBS : (b + 1) * SUBS, :]
                v = pltpu.roll(v, (half - b * SUBS) % ncol, 1)[:, :LANES]
                for bit in (1, 2, 4):
                    v = jnp.where((sub & bit) != 0, pltpu.roll(v, LANES - bit, 1), v)
                skew[pl.ds(2 * b * SUBS + p, SUBS, stride=2), :] = v
        wide = pl.cdiv(span, LANES) * LANES
        turned = jnp.concatenate([skew[t * LANES : (t + 1) * LANES, :].T[:HOFF] for t in range(wide // LANES)], axis=1)
        sub_w = lax.broadcasted_iota(jnp.int32, (SUBS, wide), 0)
        for q in range(HOFF // SUBS):
            v = turned[q * SUBS : (q + 1) * SUBS, :]
            v = pltpu.roll(v, (q * SUBS - HOFF) % wide, 1)
            for bit in (1, 2, 4):
                v = jnp.where((sub_w & bit) != 0, pltpu.roll(v, bit, 1), v)
            out_ref[zi, q * SUBS : (q + 1) * SUBS, :] += v[:, :own]

    def backward(k, _):
        z = depth - 1 - k

        def turn(j):
            mc, ms = phase_s[z, 0, j], phase_s[z, 1, j]
            ar, ai = adj[0, j], adj[1, j]
            return ar * mc + ai * ms, ai * mc - ar * ms

        first = turn(0)
        last = turn(block - 1)
        before = [up_sub(v) for v in last]
        after = [down_sub(v) for v in first]
        now = first
        diff = [a - b for a, b in zip(now, before)]
        for j in range(block):
            nxt = after if j == block - 1 else (last if j == block - 2 else turn(j + 1))
            step = [a - b for a, b in zip(nxt, now)]
            sec = [a - b for a, b in zip(step, diff)]
            adj[0, j] = now[0] + (damp * sec[0] + coef * sec[1])
            adj[1, j] = now[1] + (damp * sec[1] - coef * sec[0])
            now, diff = nxt, step

        @pl.when(z < z_first + zloc)
        def _():
            image(z)

        return 0

    lax.fori_loop(0, depth - z_first, backward, 0)


def local(
    slowness, reflect, omega, spread_coef, wavelet, ray_param, source_cell, aperture_tile, receiver_tile, observed,
):
    nd = lax.axis_size("depth")
    nq = lax.axis_size("freq")
    dev = lax.axis_index("depth")
    col = lax.axis_index("freq")
    zloc, cells = slowness.shape
    depth = zloc * nd
    shots, nf, _, _ = observed.shape
    own = cells // nq
    halo = HOFF // 2 + 2 * depth
    win = own + 2 * halo
    block = win // SUBS
    wide = pl.cdiv(win, LANES) * LANES
    per = LANES // shots
    slot = shots * nf
    groups = nq * slot // LANES
    srcs = LANES // slot
    half = HOFF // 2
    edge = half + depth + half
    obsw = pl.cdiv(own + 2 * edge, LANES) * LANES
    direct = groups == 1
    smem = pl.BlockSpec(memory_space=pltpu.SMEM)
    rows = 2 * slot + SUBS
    pos = jnp.stack([col, dev]).astype(jnp.int32)

    packed = pl.pallas_call(
        functools.partial(
            pack,
            dims=(shots, nf, depth, zloc, cells, own, halo, edge, wide, obsw),
            peers=(lambda c, k: c ^ k) if direct else (lambda c, k: k),
        ),
        in_specs=[smem] * 4 + [pl.BlockSpec(memory_space=pltpu.VMEM)] * 3,
        out_shape=[jax.ShapeDtypeStruct((2, zloc, wide), jnp.float32)]
        + [jax.ShapeDtypeStruct((1, rows, obsw), jnp.float32)] * nq,
    )(pos, omega, spread_coef, wavelet, slowness, reflect, observed.reshape(2 * slot, cells))
    both, parts = packed[0], packed[1:]
    if direct:
        parts = [parts[0]] + [
            lax.ppermute(parts[k], "freq", [(i, i ^ k) for i in range(nq)]) for k in range(1, nq)
        ]
    else:
        parts = lax.all_to_all(jnp.stack(parts), "freq", 0, 0).reshape(groups, srcs, rows, obsw)
        parts = [parts[:, k] for k in range(srcs)]
    both = [both] + [lax.ppermute(both, "depth", [(i, i ^ k) for i in range(nd)]) for k in range(1, nd)]

    dims = (shots, nf, depth, zloc, cells, own, halo, edge, block, 1.0 / math.sqrt(shots * nf * nq))
    natr = wide
    grid_spec = pltpu.PrefetchScalarGridSpec(
        num_scalar_prefetch=0,
        grid=(groups,),
        in_specs=[
            smem, smem, smem, smem, smem,
        ]
        + [pl.BlockSpec((2, zloc, wide), lambda g: (0, 0, 0))] * nd
        + [pl.BlockSpec((None, rows, obsw), lambda g: (g, 0, 0))] * srcs,
        out_specs=pl.BlockSpec((zloc, HOFF, own), lambda g: (0, 0, 0)),
        scratch_shapes=[
            pltpu.VMEM((natr, LANES), jnp.float32),
            pltpu.VMEM((depth * per // LANES, block, SUBS, LANES), jnp.float32),
            pltpu.VMEM((depth * per // LANES, block, SUBS, LANES), jnp.float32),
            pltpu.VMEM((depth * per // LANES, block, SUBS, LANES), jnp.float32),
            pltpu.VMEM((block, SUBS, LANES), jnp.float32),
            pltpu.VMEM((depth, 2, block, SUBS, LANES), jnp.float32),
            pltpu.VMEM((depth + 1, 2, block, SUBS, LANES), jnp.float32),
            pltpu.VMEM((2, block, SUBS, LANES), jnp.float32),
            pltpu.VMEM((2, block, SUBS, LANES), jnp.float32),
            pltpu.VMEM((2, natr, LANES), jnp.float32),
            pltpu.VMEM((2, natr, LANES), jnp.float32),
            pltpu.VMEM((2, natr, LANES), jnp.float32),
            pltpu.VMEM((pl.cdiv(own + HOFF, LANES) * LANES, LANES), jnp.float32),
        ],
    )
    image = pl.pallas_call(
        functools.partial(migrate, dims=dims, srcs=srcs, zsrc=nd),
        out_shape=jax.ShapeDtypeStruct((zloc, HOFF, own), jnp.float32),
        grid_spec=grid_spec,
        compiler_params=pltpu.CompilerParams(vmem_limit_bytes=56 << 20),
    )(pos, ray_param, source_cell, aperture_tile, receiver_tile, *both, *parts)
    return image


def solution(mesh):
    return jax.shard_map(
        local,
        mesh=mesh,
        in_specs=(
            P("depth", None), P("depth", None), P("freq"), P("freq"), P("freq", None),
            P(), P(), P(), P(), P(None, "freq", None, None),
        ),
        out_specs=P("depth", None, "freq"),
        check_vma=False,
    )
```

```python
import functools
import math

import jax
import jax.numpy as jnp
from jax import lax
from jax.experimental import pallas as pl
from jax.experimental.pallas import tpu as pltpu
from jax.sharding import PartitionSpec as P

HOFF = 32
LANES = 128
SUBS = 8


def sincos(angle):
    turns = jnp.floor(angle * 0.6366197723675814 + 0.5)
    rem = angle - turns * 1.5703125
    rem = rem - turns * 4.837512969970703125e-4
    rem = rem - turns * 7.54978995489188216e-8
    sq = rem * rem
    sin_p = rem + rem * sq * (-1.6666654611e-1 + sq * (8.3321608736e-3 + sq * -1.9515295891e-4))
    cos_p = (1.0 - 0.5 * sq) + sq * sq * (
        4.166664568298827e-2 + sq * (-1.388731625493765e-3 + sq * 2.443315711809948e-5)
    )
    quad = turns.astype(jnp.int32)
    odd = (quad & 1) == 1
    sine = jnp.where(odd, cos_p, sin_p)
    cosine = jnp.where(odd, sin_p, cos_p)
    sine = jnp.where((quad & 2) == 2, -sine, sine)
    cosine = jnp.where(((quad + 1) & 2) == 2, -cosine, cosine)
    return cosine, sine


def pick(values, index):
    return jnp.take_along_axis(values, index, axis=1, mode="promise_in_bounds")


def split(values):
    high = values.astype(jnp.bfloat16)
    low = (values - high.astype(jnp.float32)).astype(jnp.bfloat16)
    return high, low


def pack(pos, omega, coef, wave, slow_ref, refl_ref, obs_ref, both_ref, *outs, dims, peers):
    shots, nf, depth, zloc, cells, own, halo, edge, wide, obsw = dims
    col = pos[0]

    def window(load, first, width):
        tiles = pl.cdiv(width, LANES) + 1
        low = first + cells * LANES
        base = low // LANES - cells
        off = low % LANES
        cut = [
            load(pl.ds(pl.multiple_of(jnp.clip(base + t, 0, cells // LANES - 1) * LANES, LANES), LANES))
            for t in range(tiles)
        ]
        full = jnp.concatenate(cut, axis=1)
        return pltpu.roll(full, (tiles * LANES - off) % (tiles * LANES), 1)[:, :width]

    first = col * own - halo
    both_ref[0] = window(lambda c: slow_ref[:, c], first, wide)
    both_ref[1] = window(lambda c: refl_ref[:, c], first, wide)
    lane = lax.broadcasted_iota(jnp.int32, (1, obsw), 1) % nf

    def spread(read):
        acc = jnp.zeros((1, obsw), jnp.float32)
        for f in range(nf):
            acc = jnp.where(lane == f, read(f), acc)
        return acc

    table = jnp.concatenate(
        [
            spread(lambda f: omega[f]),
            spread(lambda f: coef[f]),
            spread(lambda f: wave[f, 0]),
            spread(lambda f: wave[f, 1]),
            jnp.zeros((4, obsw), jnp.float32),
        ],
        axis=0,
    )
    for k, out in enumerate(outs):
        dest = peers(col, k)
        out[0, : 2 * shots * nf] = window(lambda c: obs_ref[:, c], dest * own - edge, obsw)
        out[0, 2 * shots * nf :] = table


def migrate(
    pos, ray, cell, aper, recv, *refs, dims, srcs, zsrc,
):
    sr_refs, (out_ref, nat, cos_c, sin_c, wgt_c, mask_s, phase_s, src_h, sct, adj, obs_n, src_n, adj_n, prod, skew) = refs[: zsrc + srcs], refs[zsrc + srcs :]
    sr_refs, obs_refs = sr_refs[:zsrc], sr_refs[zsrc:]
    shots, nf, depth, zloc, cells, own, halo, edge, block, scale = dims
    half = HOFF // 2
    win = own + 2 * halo
    per = LANES // shots
    zper = LANES // per
    span = own + HOFF
    f32 = jnp.float32
    group = pl.program_id(0)
    x_start = pos[0] * own - halo
    dev = pos[1]
    z_first = dev * zloc

    lane = lax.broadcasted_iota(jnp.int32, (SUBS, LANES), 1)
    sub = lax.broadcasted_iota(jnp.int32, (SUBS, LANES), 0)
    lane_src = lane // (shots * nf)
    lane_shot = (lane // nf) % shots
    lane_f = lane_src * nf + lane % nf

    obs_rows = 2 * shots * nf
    table = jnp.zeros((SUBS, LANES), jnp.float32)
    for k in range(srcs):
        table = jnp.where(lane_src == k, obs_refs[k][obs_rows:, :LANES], table)

    def row(k):
        return jnp.broadcast_to(table[k : k + 1, :], (SUBS, LANES))

    omega, coef, wave_re, wave_im = row(0), row(1), row(2), row(3)
    damp = 0.26 - jnp.sqrt(0.0625 - coef * coef)
    comp_f = lane % per
    comp_z = lane // per
    omega_c = pick(omega, (comp_f // nf) * (shots * nf) + comp_f % nf)

    def per_shot(ref, dtype):
        acc = jnp.zeros((SUBS, LANES), dtype)
        for s in range(shots):
            acc = jnp.where(lane_shot == s, ref[s], acc)
        return acc

    ray_l = per_shot(ray, f32)
    cell_l = per_shot(cell, jnp.int32)
    aper_l = per_shot(aper, jnp.int32)
    recv_l = per_shot(recv, jnp.int32)
    ntile = cells // LANES

    rows2 = 2 * depth
    for t in range(pl.cdiv(win, LANES)):
        cut = slice(t * LANES, (t + 1) * LANES)
        blk = [r[part, :, cut] for part in range(2) for r in sr_refs]
        blk = jnp.concatenate(blk + [jnp.zeros((LANES - rows2, LANES), f32)], axis=0)
        nat[t * LANES : (t + 1) * LANES, :] = blk.T

    def rows_of(j):
        return pl.ds(j, SUBS, stride=block)

    def compact(zg, _):
        z = zg * zper + comp_z
        zrow = ((z // zloc) ^ dev) * zloc + z % zloc
        for j in range(block):
            v = nat[rows_of(j), :]
            c, s = sincos(omega_c * pick(v, zrow))
            cos_c[zg, j] = c
            sin_c[zg, j] = s
            wgt_c[zg, j] = omega_c * pick(v, zrow + depth)
        return 0

    lax.fori_loop(0, depth // zper, compact, 0)

    for j in range(block):
        x = x_start + sub * block + j
        tile = jnp.where(x < 0, -1, x // LANES)
        inside = (tile >= aper_l) & (tile < aper_l + ntile // 2) & (tile < ntile)
        m = inside.astype(f32)
        mask_s[j] = m
        dist = (x - cell_l).astype(f32)
        c, s = sincos(omega * ray_l * dist)
        src_h[0, 0, j] = (wave_re * c - wave_im * s) * m
        src_h[0, 1, j] = (wave_re * s + wave_im * c) * m
        sct[0, j] = jnp.zeros((SUBS, LANES), f32)
        sct[1, j] = jnp.zeros((SUBS, LANES), f32)

    def up_sub(v):
        return pltpu.roll(v, 1, 0)

    def down_sub(v):
        return pltpu.roll(v, SUBS - 1, 0)

    def forward(z, _):
        zg = z // zper
        idx = (z % zper) * per + lane_f

        def born(j):
            w = pick(wgt_c[zg, j], idx)
            sr, si = src_h[z, 0, j], src_h[z, 1, j]
            return sr, si, sct[0, j] - w * si, sct[1, j] + w * sr

        first = born(0)
        last = born(block - 1)
        before = [up_sub(v) for v in last]
        after = [down_sub(v) for v in first]
        now = first
        diff = [a - b for a, b in zip(now, before)]
        for j in range(block):
            nxt = after if j == block - 1 else (last if j == block - 2 else born(j + 1))
            step = [a - b for a, b in zip(nxt, now)]
            sec = [a - b for a, b in zip(step, diff)]
            m = mask_s[j]
            mc = m * pick(cos_c[zg, j], idx)
            ms = m * pick(sin_c[zg, j], idx)
            phase_s[z, 0, j] = mc
            phase_s[z, 1, j] = ms
            s_re = now[0] + (damp * sec[0] - coef * sec[1])
            s_im = now[1] + (damp * sec[1] + coef * sec[0])
            d_re = now[2] + (damp * sec[2] - coef * sec[3])
            d_im = now[3] + (damp * sec[3] + coef * sec[2])
            src_h[z + 1, 0, j] = s_re * mc - s_im * ms
            src_h[z + 1, 1, j] = s_re * ms + s_im * mc
            sct[0, j] = d_re * mc - d_im * ms
            sct[1, j] = d_re * ms + d_im * mc
            now, diff = nxt, step
        return 0

    lax.fori_loop(0, depth, forward, 0)

    pad = halo - edge
    for part in range(2):
        obs_n[part, : pad + SUBS, :] = jnp.zeros((pad + SUBS, LANES), f32)
        obs_n[part, win - pad - SUBS : win, :] = jnp.zeros((pad + SUBS, LANES), f32)
    per_blk = LANES // obs_rows
    where_in = (lane_src % per_blk) * obs_rows + (lane % (shots * nf)) * 2
    for t in range(pl.cdiv(own + 2 * edge, LANES)):
        cut = slice(t * LANES, (t + 1) * LANES)
        turned = [
            jnp.concatenate([r[:obs_rows, cut] for r in obs_refs[q * per_blk : (q + 1) * per_blk]], axis=0).T
            for q in range(srcs // per_blk)
        ]
        rows_t = min(LANES, own + 2 * edge - t * LANES)
        for r in range(0, rows_t, SUBS):
            for part in range(2):
                v = pick(turned[0][r : r + SUBS], where_in + part)
                for q in range(1, srcs // per_blk):
                    v = jnp.where(lane_src // per_blk == q, pick(turned[q][r : r + SUBS], where_in + part), v)
                obs_n[part, pad + t * LANES + r : pad + t * LANES + r + SUBS, :] = v
    for j in range(block):
        x = x_start + sub * block + j
        tile = jnp.where(x < 0, -1, x // LANES)
        inside = (tile >= recv_l) & (tile < recv_l + max(1, ntile // 4)) & (tile < ntile)
        m = inside.astype(f32)
        for part in range(2):
            adj[part, j] = m * (sct[part, j] - obs_n[part, rows_of(j), :])

    @pl.when(group == 0)
    def _():
        out_ref[...] = jnp.zeros(out_ref.shape, f32)

    weight = omega * scale
    nrow = span // 2
    ncol = pl.cdiv(nrow, LANES) * LANES
    lead = halo - half
    rows_in = slice(lead // 2, lead // 2 + nrow)

    def products(z):
        zi = z - z_first
        for j in range(block):
            rows = pl.ds(j // 2, SUBS, stride=block // 2)
            src_n[0, j % 2, rows, :] = src_h[z, 0, j] * weight
            src_n[1, j % 2, rows, :] = src_h[z, 1, j] * -weight
            adj_n[0, j % 2, rows, :] = adj[0, j]
            adj_n[1, j % 2, rows, :] = adj[1, j]
        for p in range(2):
            y = lax.broadcasted_iota(jnp.int32, (nrow, 2 * LANES), 0) * 2 + (x_start + lead + p)
            left = jnp.concatenate([src_n[0, p, rows_in, :], src_n[1, p, rows_in, :]], axis=1)
            right = jnp.concatenate([adj_n[1, p, rows_in, :], adj_n[0, p, rows_in, :]], axis=1)
            right = jnp.where((y >= 0) & (y < cells), right, 0.0)
            if ncol > nrow:
                right = jnp.concatenate([right, jnp.zeros((ncol - nrow, 2 * LANES), f32)], axis=0)
            lh, ll = split(left)
            rh, rl = split(right)
            dims_t = (((1,), (1,)), ((), ()))
            dot = functools.partial(lax.dot_general, dimension_numbers=dims_t, preferred_element_type=f32)
            prod[zi, p] = dot(lh, rl) + dot(ll, rh) + dot(lh, rh)

    slots = LANES // HOFF

    def extract(zg, _):
        for p in range(2):
            for b in range(nrow // SUBS):
                acc = None
                column = lane % HOFF + sub + (b * SUBS - half)
                for q in range(slots):
                    z = zg * slots + q
                    lo = max(0, b * SUBS - half) // LANES
                    hi = min(b * SUBS + SUBS - 1 + half - 1, ncol - 1) // LANES
                    v = None
                    for t in range(lo, hi + 1):
                        part = prod[z, p, b * SUBS : (b + 1) * SUBS, t * LANES : (t + 1) * LANES]
                        part = pick(part, (column + LANES) & (LANES - 1))
                        if v is None:
                            v = part
                        else:
                            v = jnp.where(column >= t * LANES, part, v)
                    acc = v if acc is None else jnp.where(lane >= q * HOFF, v, acc)
                skew[pl.ds(2 * b * SUBS + p, SUBS, stride=2), :] = acc
        tiles = pl.cdiv(span, LANES)
        turned = [skew[t * LANES : (t + 1) * LANES, :].T for t in range(tiles)]
        for q in range(slots):
            for hq in range(HOFF // SUBS):
                rows = slice(q * HOFF + hq * SUBS, q * HOFF + (hq + 1) * SUBS)
                column = lane - sub + (HOFF - hq * SUBS)
                moved = [pick(turned[t][rows], column & (LANES - 1)) for t in range(tiles)]
                for t in range(pl.cdiv(own, LANES)):
                    v = moved[t]
                    if t + 1 < tiles:
                        v = jnp.where(column < LANES, v, moved[t + 1])
                    width = min(LANES, own - t * LANES)
                    out_ref[zg * slots + q, hq * SUBS : (hq + 1) * SUBS, t * LANES : t * LANES + width] += v[:, :width]
        return 0

    def backward(k, _):
        z = depth - 1 - k

        def turn(j):
            mc, ms = phase_s[z, 0, j], phase_s[z, 1, j]
            ar, ai = adj[0, j], adj[1, j]
            return ar * mc + ai * ms, ai * mc - ar * ms

        first = turn(0)
        last = turn(block - 1)
        before = [up_sub(v) for v in last]
        after = [down_sub(v) for v in first]
        now = first
        diff = [a - b for a, b in zip(now, before)]
        for j in range(block):
            nxt = after if j == block - 1 else (last if j == block - 2 else turn(j + 1))
            step = [a - b for a, b in zip(nxt, now)]
            sec = [a - b for a, b in zip(step, diff)]
            adj[0, j] = now[0] + (damp * sec[0] + coef * sec[1])
            adj[1, j] = now[1] + (damp * sec[1] - coef * sec[0])
            now, diff = nxt, step

        return 0

    def backward_slab(k, _):
        backward(k, 0)
        products(depth - 1 - k)
        return 0

    ahead = depth - z_first - zloc
    lax.fori_loop(0, ahead, backward, 0)
    lax.fori_loop(ahead, ahead + zloc, backward_slab, 0)
    lax.fori_loop(0, zloc // slots, extract, 0)


def local(
    slowness, reflect, omega, spread_coef, wavelet, ray_param, source_cell, aperture_tile, receiver_tile, observed,
):
    nd = lax.axis_size("depth")
    nq = lax.axis_size("freq")
    dev = lax.axis_index("depth")
    col = lax.axis_index("freq")
    zloc, cells = slowness.shape
    depth = zloc * nd
    shots, nf, _, _ = observed.shape
    own = cells // nq
    halo = HOFF // 2 + 2 * depth
    win = own + 2 * halo
    block = win // SUBS
    wide = pl.cdiv(win, LANES) * LANES
    per = LANES // shots
    slot = shots * nf
    groups = nq * slot // LANES
    srcs = LANES // slot
    half = HOFF // 2
    edge = half + depth + half
    obsw = pl.cdiv(own + 2 * edge, LANES) * LANES
    direct = groups == 1
    smem = pl.BlockSpec(memory_space=pltpu.SMEM)
    rows = 2 * slot + SUBS
    pos = jnp.stack([col, dev]).astype(jnp.int32)

    packed = pl.pallas_call(
        functools.partial(
            pack,
            dims=(shots, nf, depth, zloc, cells, own, halo, edge, wide, obsw),
            peers=(lambda c, k: c ^ k) if direct else (lambda c, k: k),
        ),
        in_specs=[smem] * 4 + [pl.BlockSpec(memory_space=pltpu.VMEM)] * 3,
        out_shape=[jax.ShapeDtypeStruct((2, zloc, wide), jnp.float32)]
        + [jax.ShapeDtypeStruct((1, rows, obsw), jnp.float32)] * nq,
    )(pos, omega, spread_coef, wavelet, slowness, reflect, observed.reshape(2 * slot, cells))
    both, parts = packed[0], packed[1:]
    if direct:
        parts = [parts[0]] + [
            lax.ppermute(parts[k], "freq", [(i, i ^ k) for i in range(nq)]) for k in range(1, nq)
        ]
    else:
        parts = lax.all_to_all(jnp.stack(parts), "freq", 0, 0).reshape(groups, srcs, rows, obsw)
        parts = [parts[:, k] for k in range(srcs)]
    both = [both] + [lax.ppermute(both, "depth", [(i, i ^ k) for i in range(nd)]) for k in range(1, nd)]

    dims = (shots, nf, depth, zloc, cells, own, halo, edge, block, 1.0 / math.sqrt(shots * nf * nq))
    natr = wide
    grid_spec = pltpu.PrefetchScalarGridSpec(
        num_scalar_prefetch=0,
        grid=(groups,),
        in_specs=[
            smem, smem, smem, smem, smem,
        ]
        + [pl.BlockSpec((2, zloc, wide), lambda g: (0, 0, 0))] * nd
        + [pl.BlockSpec((None, rows, obsw), lambda g: (g, 0, 0))] * srcs,
        out_specs=pl.BlockSpec((zloc, HOFF, own), lambda g: (0, 0, 0)),
        scratch_shapes=[
            pltpu.VMEM((natr, LANES), jnp.float32),
            pltpu.VMEM((depth * per // LANES, block, SUBS, LANES), jnp.float32),
            pltpu.VMEM((depth * per // LANES, block, SUBS, LANES), jnp.float32),
            pltpu.VMEM((depth * per // LANES, block, SUBS, LANES), jnp.float32),
            pltpu.VMEM((block, SUBS, LANES), jnp.float32),
            pltpu.VMEM((depth, 2, block, SUBS, LANES), jnp.float32),
            pltpu.VMEM((depth + 1, 2, block, SUBS, LANES), jnp.float32),
            pltpu.VMEM((2, block, SUBS, LANES), jnp.float32),
            pltpu.VMEM((2, block, SUBS, LANES), jnp.float32),
            pltpu.VMEM((2, natr, LANES), jnp.float32),
            pltpu.VMEM((2, 2, win // 2, LANES), jnp.float32),
            pltpu.VMEM((2, 2, win // 2, LANES), jnp.float32),
            pltpu.VMEM((zloc, 2, (own + HOFF) // 2, pl.cdiv((own + HOFF) // 2, LANES) * LANES), jnp.float32),
            pltpu.VMEM((pl.cdiv(own + HOFF, LANES) * LANES, LANES), jnp.float32),
        ],
    )
    image = pl.pallas_call(
        functools.partial(migrate, dims=dims, srcs=srcs, zsrc=nd),
        out_shape=jax.ShapeDtypeStruct((zloc, HOFF, own), jnp.float32),
        grid_spec=grid_spec,
        compiler_params=pltpu.CompilerParams(vmem_limit_bytes=56 << 20),
    )(pos, ray_param, source_cell, aperture_tile, receiver_tile, *both, *parts)
    return image


def solution(mesh):
    return jax.shard_map(
        local,
        mesh=mesh,
        in_specs=(
            P("depth", None), P("depth", None), P("freq"), P("freq"), P("freq", None),
            P(), P(), P(), P(), P(None, "freq", None, None),
        ),
        out_specs=P("depth", None, "freq"),
        check_vma=False,
    )
```

```python
import functools
import math

import jax
import jax.numpy as jnp
from jax import lax
from jax.experimental import pallas as pl
from jax.experimental.pallas import tpu as pltpu
from jax.sharding import PartitionSpec as P

HOFF = 32
LANES = 128
SUBS = 8


def sincos(angle):
    turns = jnp.floor(angle * 0.6366197723675814 + 0.5)
    rem = angle - turns * 1.5703125
    rem = rem - turns * 4.837512969970703125e-4
    rem = rem - turns * 7.54978995489188216e-8
    sq = rem * rem
    sin_p = rem + rem * sq * (-1.6666654611e-1 + sq * (8.3321608736e-3 + sq * -1.9515295891e-4))
    cos_p = (1.0 - 0.5 * sq) + sq * sq * (
        4.166664568298827e-2 + sq * (-1.388731625493765e-3 + sq * 2.443315711809948e-5)
    )
    quad = turns.astype(jnp.int32)
    odd = (quad & 1) == 1
    sine = jnp.where(odd, cos_p, sin_p)
    cosine = jnp.where(odd, sin_p, cos_p)
    sine = jnp.where((quad & 2) == 2, -sine, sine)
    cosine = jnp.where(((quad + 1) & 2) == 2, -cosine, cosine)
    return cosine, sine


def pick(values, index):
    return jnp.take_along_axis(values, index, axis=1, mode="promise_in_bounds")


def split(values):
    high = values.astype(jnp.bfloat16)
    low = (values - high.astype(jnp.float32)).astype(jnp.bfloat16)
    return high, low


def pack(omega, coef, wave, slow_ref, refl_ref, obs_ref, both_ref, *outs, dims, peers):
    shots, nf, depth, zloc, cells, own, halo, edge, wide, obsw = dims
    col = lax.axis_index("freq")
    dev = lax.axis_index("depth")

    def window(load, first, width):
        tiles = pl.cdiv(width, LANES) + 1
        low = first + cells * LANES
        base = low // LANES - cells
        off = low % LANES
        cut = [
            load(pl.ds(pl.multiple_of(jnp.clip(base + t, 0, cells // LANES - 1) * LANES, LANES), LANES))
            for t in range(tiles)
        ]
        full = jnp.concatenate(cut, axis=1)
        return pltpu.roll(full, (tiles * LANES - off) % (tiles * LANES), 1)[:, :width]

    first = col * own - halo
    both_ref[0] = window(lambda c: slow_ref[:, c], first, wide)
    both_ref[1] = window(lambda c: refl_ref[:, c], first, wide)
    lane = lax.broadcasted_iota(jnp.int32, (1, obsw), 1) % nf

    def spread(read):
        acc = jnp.zeros((1, obsw), jnp.float32)
        for f in range(nf):
            acc = jnp.where(lane == f, read(f), acc)
        return acc

    table = jnp.concatenate(
        [
            spread(lambda f: omega[f]),
            spread(lambda f: coef[f]),
            spread(lambda f: wave[f, 0]),
            spread(lambda f: wave[f, 1]),
            jnp.zeros((4, obsw), jnp.float32),
        ],
        axis=0,
    )
    for k, out in enumerate(outs):
        dest = peers(col, dev, k)
        out[0, : 2 * shots * nf] = window(lambda c: obs_ref[:, c], dest * own - edge, obsw)
        out[0, 2 * shots * nf :] = table


def migrate(
    ray, cell, aper, recv, *refs, dims, srcs, zsrc,
):
    sr_refs, (out_ref, nat, cos_c, sin_c, wgt_c, mask_s, phase_s, src_h, sct, adj, obs_n, src_n, adj_n, prod, skew) = refs[: zsrc + srcs], refs[zsrc + srcs :]
    sr_refs, obs_refs = sr_refs[:zsrc], sr_refs[zsrc:]
    shots, nf, depth, zloc, cells, own, halo, edge, block, scale = dims
    half = HOFF // 2
    win = own + 2 * halo
    per = LANES // shots
    zper = LANES // per
    span = own + HOFF
    f32 = jnp.float32
    group = pl.program_id(0)
    x_start = lax.axis_index("freq") * own - halo
    dev = lax.axis_index("depth")
    z_first = dev * zloc

    lane = lax.broadcasted_iota(jnp.int32, (SUBS, LANES), 1)
    sub = lax.broadcasted_iota(jnp.int32, (SUBS, LANES), 0)
    lane_src = lane // (shots * nf)
    lane_shot = (lane // nf) % shots
    lane_f = lane_src * nf + lane % nf

    obs_rows = 2 * shots * nf
    table = jnp.zeros((SUBS, LANES), jnp.float32)
    for k in range(srcs):
        table = jnp.where(lane_src == k, obs_refs[k][obs_rows:, :LANES], table)

    def row(k):
        return jnp.broadcast_to(table[k : k + 1, :], (SUBS, LANES))

    omega, coef, wave_re, wave_im = row(0), row(1), row(2), row(3)
    damp = 0.26 - jnp.sqrt(0.0625 - coef * coef)
    comp_f = lane % per
    comp_z = lane // per
    omega_c = pick(omega, (comp_f // nf) * (shots * nf) + comp_f % nf)

    def per_shot(ref, dtype):
        acc = jnp.zeros((SUBS, LANES), dtype)
        for s in range(shots):
            acc = jnp.where(lane_shot == s, ref[s], acc)
        return acc

    ray_l = per_shot(ray, f32)
    cell_l = per_shot(cell, jnp.int32)
    aper_l = per_shot(aper, jnp.int32)
    recv_l = per_shot(recv, jnp.int32)
    ntile = cells // LANES

    rows2 = 2 * depth
    for t in range(pl.cdiv(win, LANES)):
        cut = slice(t * LANES, (t + 1) * LANES)
        blk = [r[part, :, cut] for part in range(2) for r in sr_refs]
        blk = jnp.concatenate(blk + [jnp.zeros((LANES - rows2, LANES), f32)], axis=0)
        nat[t * LANES : (t + 1) * LANES, :] = blk.T

    def rows_of(j):
        return pl.ds(j, SUBS, stride=block)

    def compact(zg, _):
        z = zg * zper + comp_z
        zrow = ((z // zloc) ^ dev) * zloc + z % zloc
        for j in range(block):
            v = nat[rows_of(j), :]
            c, s = sincos(omega_c * pick(v, zrow))
            cos_c[zg, j] = c
            sin_c[zg, j] = s
            wgt_c[zg, j] = omega_c * pick(v, zrow + depth)
        return 0

    lax.fori_loop(0, depth // zper, compact, 0)

    for j in range(block):
        x = x_start + sub * block + j
        tile = jnp.where(x < 0, -1, x // LANES)
        inside = (tile >= aper_l) & (tile < aper_l + ntile // 2) & (tile < ntile)
        m = inside.astype(f32)
        mask_s[j] = m
        dist = (x - cell_l).astype(f32)
        c, s = sincos(omega * ray_l * dist)
        src_h[0, 0, j] = (wave_re * c - wave_im * s) * m
        src_h[0, 1, j] = (wave_re * s + wave_im * c) * m
        sct[0, j] = jnp.zeros((SUBS, LANES), f32)
        sct[1, j] = jnp.zeros((SUBS, LANES), f32)

    def up_sub(v):
        return pltpu.roll(v, 1, 0)

    def down_sub(v):
        return pltpu.roll(v, SUBS - 1, 0)

    def forward(z, _):
        zg = z // zper
        idx = (z % zper) * per + lane_f

        def born(j):
            w = pick(wgt_c[zg, j], idx)
            sr, si = src_h[z, 0, j], src_h[z, 1, j]
            return sr, si, sct[0, j] - w * si, sct[1, j] + w * sr

        first = born(0)
        last = born(block - 1)
        before = [up_sub(v) for v in last]
        after = [down_sub(v) for v in first]
        now = first
        diff = [a - b for a, b in zip(now, before)]
        for j in range(block):
            nxt = after if j == block - 1 else (last if j == block - 2 else born(j + 1))
            step = [a - b for a, b in zip(nxt, now)]
            sec = [a - b for a, b in zip(step, diff)]
            m = mask_s[j]
            mc = m * pick(cos_c[zg, j], idx)
            ms = m * pick(sin_c[zg, j], idx)
            phase_s[z, 0, j] = mc
            phase_s[z, 1, j] = ms
            s_re = now[0] + (damp * sec[0] - coef * sec[1])
            s_im = now[1] + (damp * sec[1] + coef * sec[0])
            d_re = now[2] + (damp * sec[2] - coef * sec[3])
            d_im = now[3] + (damp * sec[3] + coef * sec[2])
            src_h[z + 1, 0, j] = s_re * mc - s_im * ms
            src_h[z + 1, 1, j] = s_re * ms + s_im * mc
            sct[0, j] = d_re * mc - d_im * ms
            sct[1, j] = d_re * ms + d_im * mc
            now, diff = nxt, step
        return 0

    lax.fori_loop(0, depth, forward, 0)

    pad = halo - edge
    for part in range(2):
        obs_n[part, : pad + SUBS, :] = jnp.zeros((pad + SUBS, LANES), f32)
        obs_n[part, win - pad - SUBS : win, :] = jnp.zeros((pad + SUBS, LANES), f32)
    per_blk = LANES // obs_rows
    where_in = (lane_src % per_blk) * obs_rows + (lane % (shots * nf)) * 2
    for t in range(pl.cdiv(own + 2 * edge, LANES)):
        cut = slice(t * LANES, (t + 1) * LANES)
        turned = [
            jnp.concatenate([r[:obs_rows, cut] for r in obs_refs[q * per_blk : (q + 1) * per_blk]], axis=0).T
            for q in range(srcs // per_blk)
        ]
        rows_t = min(LANES, own + 2 * edge - t * LANES)
        for r in range(0, rows_t, SUBS):
            for part in range(2):
                v = pick(turned[0][r : r + SUBS], where_in + part)
                for q in range(1, srcs // per_blk):
                    v = jnp.where(lane_src // per_blk == q, pick(turned[q][r : r + SUBS], where_in + part), v)
                obs_n[part, pad + t * LANES + r : pad + t * LANES + r + SUBS, :] = v
    for j in range(block):
        x = x_start + sub * block + j
        tile = jnp.where(x < 0, -1, x // LANES)
        inside = (tile >= recv_l) & (tile < recv_l + max(1, ntile // 4)) & (tile < ntile)
        m = inside.astype(f32)
        for part in range(2):
            adj[part, j] = m * (sct[part, j] - obs_n[part, rows_of(j), :])

    @pl.when(group == 0)
    def _():
        out_ref[...] = jnp.zeros(out_ref.shape, f32)

    weight = omega * scale
    nrow = span // 2
    ncol = pl.cdiv(nrow, LANES) * LANES
    lead = halo - half
    rows_in = slice(lead // 2, lead // 2 + nrow)

    def products(z):
        zi = z - z_first
        for j in range(block):
            rows = pl.ds(j // 2, SUBS, stride=block // 2)
            src_n[0, j % 2, rows, :] = src_h[z, 0, j] * weight
            src_n[1, j % 2, rows, :] = src_h[z, 1, j] * -weight
            adj_n[0, j % 2, rows, :] = adj[0, j]
            adj_n[1, j % 2, rows, :] = adj[1, j]
        for p in range(2):
            y = lax.broadcasted_iota(jnp.int32, (nrow, 2 * LANES), 0) * 2 + (x_start + lead + p)
            left = jnp.concatenate([src_n[0, p, rows_in, :], src_n[1, p, rows_in, :]], axis=1)
            right = jnp.concatenate([adj_n[1, p, rows_in, :], adj_n[0, p, rows_in, :]], axis=1)
            right = jnp.where((y >= 0) & (y < cells), right, 0.0)
            if ncol > nrow:
                right = jnp.concatenate([right, jnp.zeros((ncol - nrow, 2 * LANES), f32)], axis=0)
            lh, ll = split(left)
            rh, rl = split(right)
            dims_t = (((1,), (1,)), ((), ()))
            dot = functools.partial(lax.dot_general, dimension_numbers=dims_t, preferred_element_type=f32)
            prod[zi, p] = dot(lh, rl) + dot(ll, rh) + dot(lh, rh)

    slots = LANES // HOFF

    def extract(zg, _):
        for p in range(2):
            for b in range(nrow // SUBS):
                acc = None
                column = lane % HOFF + sub + (b * SUBS - half)
                for q in range(slots):
                    z = zg * slots + q
                    lo = max(0, b * SUBS - half) // LANES
                    hi = min(b * SUBS + SUBS - 1 + half - 1, ncol - 1) // LANES
                    v = None
                    for t in range(lo, hi + 1):
                        part = prod[z, p, b * SUBS : (b + 1) * SUBS, t * LANES : (t + 1) * LANES]
                        part = pick(part, (column + LANES) & (LANES - 1))
                        if v is None:
                            v = part
                        else:
                            v = jnp.where(column >= t * LANES, part, v)
                    acc = v if acc is None else jnp.where(lane >= q * HOFF, v, acc)
                skew[pl.ds(2 * b * SUBS + p, SUBS, stride=2), :] = acc
        tiles = pl.cdiv(span, LANES)
        turned = [skew[t * LANES : (t + 1) * LANES, :].T for t in range(tiles)]
        for q in range(slots):
            for hq in range(HOFF // SUBS):
                rows = slice(q * HOFF + hq * SUBS, q * HOFF + (hq + 1) * SUBS)
                column = lane - sub + (HOFF - hq * SUBS)
                moved = [pick(turned[t][rows], column & (LANES - 1)) for t in range(tiles)]
                for t in range(pl.cdiv(own, LANES)):
                    v = moved[t]
                    if t + 1 < tiles:
                        v = jnp.where(column < LANES, v, moved[t + 1])
                    width = min(LANES, own - t * LANES)
                    out_ref[zg * slots + q, hq * SUBS : (hq + 1) * SUBS, t * LANES : t * LANES + width] += v[:, :width]
        return 0

    def backward(k, _):
        z = depth - 1 - k

        def turn(j):
            mc, ms = phase_s[z, 0, j], phase_s[z, 1, j]
            ar, ai = adj[0, j], adj[1, j]
            return ar * mc + ai * ms, ai * mc - ar * ms

        first = turn(0)
        last = turn(block - 1)
        before = [up_sub(v) for v in last]
        after = [down_sub(v) for v in first]
        now = first
        diff = [a - b for a, b in zip(now, before)]
        for j in range(block):
            nxt = after if j == block - 1 else (last if j == block - 2 else turn(j + 1))
            step = [a - b for a, b in zip(nxt, now)]
            sec = [a - b for a, b in zip(step, diff)]
            adj[0, j] = now[0] + (damp * sec[0] + coef * sec[1])
            adj[1, j] = now[1] + (damp * sec[1] - coef * sec[0])
            now, diff = nxt, step

        return 0

    def backward_slab(k, _):
        backward(k, 0)
        products(depth - 1 - k)
        return 0

    ahead = depth - z_first - zloc
    lax.fori_loop(0, ahead, backward, 0)
    lax.fori_loop(ahead, ahead + zloc, backward_slab, 0)
    lax.fori_loop(0, zloc // slots, extract, 0)


def local(
    slowness, reflect, omega, spread_coef, wavelet, ray_param, source_cell, aperture_tile, receiver_tile, observed,
):
    nd = lax.axis_size("depth")
    nq = lax.axis_size("freq")
    zloc, cells = slowness.shape
    depth = zloc * nd
    shots, nf, _, _ = observed.shape
    own = cells // nq
    halo = HOFF // 2 + 2 * depth
    win = own + 2 * halo
    block = win // SUBS
    wide = pl.cdiv(win, LANES) * LANES
    per = LANES // shots
    slot = shots * nf
    groups = nq * slot // LANES
    srcs = LANES // slot
    half = HOFF // 2
    edge = half + depth + half
    obsw = pl.cdiv(own + 2 * edge, LANES) * LANES
    direct = groups == 1 and nq == 8
    smem = pl.BlockSpec(memory_space=pltpu.SMEM)
    rows = 2 * slot + SUBS

    fetch = ((7, 4, 3, 0), (6, 5, 2, 1))
    if direct:
        count = nq // 2
        peers = lambda c, d, k: c ^ jnp.where(d % 2 == 0, fetch[0][k], fetch[1][k])
    else:
        count = nq
        peers = lambda c, d, k: k

    packed = pl.pallas_call(
        functools.partial(
            pack,
            dims=(shots, nf, depth, zloc, cells, own, halo, edge, wide, obsw),
            peers=peers,
        ),
        in_specs=[smem] * 3 + [pl.BlockSpec(memory_space=pltpu.VMEM)] * 3,
        out_shape=[jax.ShapeDtypeStruct((2, zloc, wide), jnp.float32)]
        + [jax.ShapeDtypeStruct((1, rows, obsw), jnp.float32)] * count,
    )(omega, spread_coef, wavelet, slowness, reflect, observed.reshape(2 * slot, cells))
    both, parts = {0: packed[0]}, packed[1:]

    def swap(value, bit):
        return lax.ppermute(value, "depth", [(i, i ^ bit) for i in range(nd)])

    bit = nd // 2
    while bit > 1:
        both.update({k ^ bit: swap(v, bit) for k, v in list(both.items())})
        bit //= 2
    if direct:
        parts = [
            lax.ppermute(
                part,
                ("depth", "freq"),
                [(d * nq + i, d * nq + (i ^ fetch[d % 2][k])) for d in range(nd) for i in range(nq)],
            )
            for k, part in enumerate(parts)
        ]
        parts = parts + [swap(part, 1) for part in parts]
    else:
        parts = lax.all_to_all(jnp.stack(parts), "freq", 0, 0).reshape(groups, srcs, rows, obsw)
        parts = [parts[:, k] for k in range(srcs)]
    both.update({k ^ 1: swap(v, 1) for k, v in list(both.items())})
    both = [both[k] for k in range(nd)]

    dims = (shots, nf, depth, zloc, cells, own, halo, edge, block, 1.0 / math.sqrt(shots * nf * nq))
    natr = wide
    grid_spec = pltpu.PrefetchScalarGridSpec(
        num_scalar_prefetch=0,
        grid=(groups,),
        in_specs=[
            smem, smem, smem, smem,
        ]
        + [pl.BlockSpec((2, zloc, wide), lambda g: (0, 0, 0))] * nd
        + [pl.BlockSpec((None, rows, obsw), lambda g: (g, 0, 0))] * srcs,
        out_specs=pl.BlockSpec((zloc, HOFF, own), lambda g: (0, 0, 0)),
        scratch_shapes=[
            pltpu.VMEM((natr, LANES), jnp.float32),
            pltpu.VMEM((depth * per // LANES, block, SUBS, LANES), jnp.float32),
            pltpu.VMEM((depth * per // LANES, block, SUBS, LANES), jnp.float32),
            pltpu.VMEM((depth * per // LANES, block, SUBS, LANES), jnp.float32),
            pltpu.VMEM((block, SUBS, LANES), jnp.float32),
            pltpu.VMEM((depth, 2, block, SUBS, LANES), jnp.float32),
            pltpu.VMEM((depth + 1, 2, block, SUBS, LANES), jnp.float32),
            pltpu.VMEM((2, block, SUBS, LANES), jnp.float32),
            pltpu.VMEM((2, block, SUBS, LANES), jnp.float32),
            pltpu.VMEM((2, natr, LANES), jnp.float32),
            pltpu.VMEM((2, 2, win // 2, LANES), jnp.float32),
            pltpu.VMEM((2, 2, win // 2, LANES), jnp.float32),
            pltpu.VMEM((zloc, 2, (own + HOFF) // 2, pl.cdiv((own + HOFF) // 2, LANES) * LANES), jnp.float32),
            pltpu.VMEM((pl.cdiv(own + HOFF, LANES) * LANES, LANES), jnp.float32),
        ],
    )
    image = pl.pallas_call(
        functools.partial(migrate, dims=dims, srcs=srcs, zsrc=nd),
        out_shape=jax.ShapeDtypeStruct((zloc, HOFF, own), jnp.float32),
        grid_spec=grid_spec,
        compiler_params=pltpu.CompilerParams(vmem_limit_bytes=56 << 20),
    )(ray_param, source_cell, aperture_tile, receiver_tile, *both, *parts)
    return image


def solution(mesh):
    return jax.shard_map(
        local,
        mesh=mesh,
        in_specs=(
            P("depth", None), P("depth", None), P("freq"), P("freq"), P("freq", None),
            P(), P(), P(), P(), P(None, "freq", None, None),
        ),
        out_specs=P("depth", None, "freq"),
        check_vma=False,
    )
```

```python
import functools
import math

import jax
import jax.numpy as jnp
from jax import lax
from jax.experimental import pallas as pl
from jax.experimental.pallas import tpu as pltpu
from jax.sharding import PartitionSpec as P

HOFF = 32
LANES = 128
SUBS = 8


def sincos(angle):
    turns = jnp.floor(angle * 0.6366197723675814 + 0.5)
    rem = angle - turns * 1.5703125
    rem = rem - turns * 4.837512969970703125e-4
    rem = rem - turns * 7.54978995489188216e-8
    sq = rem * rem
    sin_p = rem + rem * sq * (-1.6666654611e-1 + sq * (8.3321608736e-3 + sq * -1.9515295891e-4))
    cos_p = (1.0 - 0.5 * sq) + sq * sq * (
        4.166664568298827e-2 + sq * (-1.388731625493765e-3 + sq * 2.443315711809948e-5)
    )
    quad = turns.astype(jnp.int32)
    odd = (quad & 1) == 1
    sine = jnp.where(odd, cos_p, sin_p)
    cosine = jnp.where(odd, sin_p, cos_p)
    sine = jnp.where((quad & 2) == 2, -sine, sine)
    cosine = jnp.where(((quad + 1) & 2) == 2, -cosine, cosine)
    return cosine, sine


def pick(values, index):
    return jnp.take_along_axis(values, index, axis=1, mode="promise_in_bounds")


def split(values):
    high = values.astype(jnp.bfloat16)
    low = (values - high.astype(jnp.float32)).astype(jnp.bfloat16)
    return high, low


def pack(omega, coef, wave, slow_ref, refl_ref, obs_ref, both_ref, *outs, dims, peers):
    shots, nf, depth, zloc, cells, own, halo, edge, wide, obsw = dims
    col = lax.axis_index("freq")
    dev = lax.axis_index("depth")

    def window(load, first, width):
        tiles = pl.cdiv(width, LANES) + 1
        low = first + cells * LANES
        base = low // LANES - cells
        off = low % LANES
        cut = [
            load(pl.ds(pl.multiple_of(jnp.clip(base + t, 0, cells // LANES - 1) * LANES, LANES), LANES))
            for t in range(tiles)
        ]
        full = jnp.concatenate(cut, axis=1)
        return pltpu.roll(full, (tiles * LANES - off) % (tiles * LANES), 1)[:, :width]

    first = col * own - halo
    both_ref[0] = window(lambda c: slow_ref[:, c], first, wide)
    both_ref[1] = window(lambda c: refl_ref[:, c], first, wide)
    lane = lax.broadcasted_iota(jnp.int32, (1, obsw), 1) % nf

    def spread(read):
        acc = jnp.zeros((1, obsw), jnp.float32)
        for f in range(nf):
            acc = jnp.where(lane == f, read(f), acc)
        return acc

    table = jnp.concatenate(
        [
            spread(lambda f: omega[f]),
            spread(lambda f: coef[f]),
            spread(lambda f: wave[f, 0]),
            spread(lambda f: wave[f, 1]),
            jnp.zeros((4, obsw), jnp.float32),
        ],
        axis=0,
    )
    for k, out in enumerate(outs):
        dest = peers(col, dev, k)
        out[0, : 2 * shots * nf] = window(lambda c: obs_ref[:, :, :, c].reshape(2 * shots * nf, LANES), dest * own - edge, obsw)
        out[0, 2 * shots * nf :] = table


def migrate(
    ray, cell, aper, recv, *refs, dims, srcs, zsrc,
):
    sr_refs, (out_mine, out_other, nat, cos_c, sin_c, wgt_c, mask_s, phase_s, src_h, sct, adj, obs_n, src_n, adj_n, prod, skew) = refs[: zsrc + srcs], refs[zsrc + srcs :]
    sr_refs, obs_refs = sr_refs[:zsrc], sr_refs[zsrc:]
    shots, nf, depth, zloc, cells, own, halo, edge, block, scale = dims
    half = HOFF // 2
    win = own + 2 * halo
    pairs = LANES // 2
    nfc = nf // 2
    per = pairs // shots
    zper = pairs // per
    span = own + HOFF
    f32 = jnp.float32
    group = pl.program_id(0)
    x_start = lax.axis_index("freq") * own - halo
    dev = lax.axis_index("depth")
    core = dev % 2
    z_first = (dev - core) * zloc
    slab = 2 * zloc

    lane = lax.broadcasted_iota(jnp.int32, (SUBS, LANES), 1)
    sub = lax.broadcasted_iota(jnp.int32, (SUBS, LANES), 0)
    upper = lane >= pairs
    pair = lane % pairs
    lane_src = pair // (shots * nfc)
    lane_shot = (pair // nfc) % shots
    lane_f = lane_src * nfc + pair % nfc
    lane_own = core * nfc + pair % nfc

    obs_rows = 2 * shots * nf
    table = jnp.zeros((SUBS, LANES), jnp.float32)
    for k in range(srcs):
        table = jnp.where(lane_src == k, obs_refs[k][obs_rows:, :LANES], table)

    table = pick(table, lane_src * (shots * nfc) + lane_own)

    def row(k):
        return jnp.broadcast_to(table[k : k + 1, :], (SUBS, LANES))

    omega, coef, wave_re, wave_im = row(0), row(1), row(2), row(3)
    damp = 0.26 - jnp.sqrt(0.0625 - coef * coef)
    comp_f = lane % per
    comp_z = pair // per
    omega_c = pick(omega, (comp_f // nfc) * (shots * nfc) + comp_f % nfc)

    def per_shot(ref, dtype):
        acc = jnp.zeros((SUBS, LANES), dtype)
        for s in range(shots):
            acc = jnp.where(lane_shot == s, ref[s], acc)
        return acc

    ray_l = per_shot(ray, f32)
    cell_l = per_shot(cell, jnp.int32)
    aper_l = per_shot(aper, jnp.int32)
    recv_l = per_shot(recv, jnp.int32)
    ntile = cells // LANES

    rows2 = 2 * depth
    for t in range(pl.cdiv(win, LANES)):
        cut = slice(t * LANES, (t + 1) * LANES)
        blk = [r[part, :, cut] for part in range(2) for r in sr_refs]
        blk = jnp.concatenate(blk + [jnp.zeros((LANES - rows2, LANES), f32)], axis=0)
        nat[t * LANES : (t + 1) * LANES, :] = blk.T

    def halves(j):
        return pl.ds(j, SUBS, stride=block), pl.ds(win // 2 + j, SUBS, stride=block)

    def cell_of(j):
        return x_start + (sub + jnp.where(upper, SUBS, 0)) * block + j

    def compact(zg, _):
        z = zg * zper + comp_z
        zrow = ((z // zloc) ^ dev) * zloc + z % zloc
        for j in range(block):
            low, high = (nat[rows, :] for rows in halves(j))
            c, s = sincos(omega_c * jnp.where(upper, pick(high, zrow), pick(low, zrow)))
            cos_c[zg, j] = c
            sin_c[zg, j] = s
            wgt_c[zg, j] = omega_c * jnp.where(upper, pick(high, zrow + depth), pick(low, zrow + depth))
        return 0

    lax.fori_loop(0, depth // zper, compact, 0)

    for j in range(block):
        x = cell_of(j)
        tile = jnp.where(x < 0, -1, x // LANES)
        inside = (tile >= aper_l) & (tile < aper_l + ntile // 2) & (tile < ntile)
        m = inside.astype(f32)
        mask_s[j] = m
        dist = (x - cell_l).astype(f32)
        c, s = sincos(omega * ray_l * dist)
        src_h[0, 0, j] = (wave_re * c - wave_im * s) * m
        src_h[0, 1, j] = (wave_re * s + wave_im * c) * m
        sct[0, j] = jnp.zeros((SUBS, LANES), f32)
        sct[1, j] = jnp.zeros((SUBS, LANES), f32)

    def up_sub(v):
        v = pltpu.roll(v, 1, 0)
        return jnp.where(sub == 0, pltpu.roll(v, pairs, 1), v)

    def down_sub(v):
        v = pltpu.roll(v, SUBS - 1, 0)
        return jnp.where(sub == SUBS - 1, pltpu.roll(v, pairs, 1), v)

    def forward(z, _):
        zg = z // zper
        idx = (z % zper) * per + lane_f + jnp.where(upper, pairs, 0)

        def born(j):
            w = pick(wgt_c[zg, j], idx)
            sr, si = src_h[z, 0, j], src_h[z, 1, j]
            return sr, si, sct[0, j] - w * si, sct[1, j] + w * sr

        first = born(0)
        last = born(block - 1)
        before = [up_sub(v) for v in last]
        after = [down_sub(v) for v in first]
        now = first
        diff = [a - b for a, b in zip(now, before)]
        for j in range(block):
            nxt = after if j == block - 1 else (last if j == block - 2 else born(j + 1))
            step = [a - b for a, b in zip(nxt, now)]
            sec = [a - b for a, b in zip(step, diff)]
            m = mask_s[j]
            mc = m * pick(cos_c[zg, j], idx)
            ms = m * pick(sin_c[zg, j], idx)
            phase_s[z, 0, j] = mc
            phase_s[z, 1, j] = ms
            s_re = now[0] + (damp * sec[0] - coef * sec[1])
            s_im = now[1] + (damp * sec[1] + coef * sec[0])
            d_re = now[2] + (damp * sec[2] - coef * sec[3])
            d_im = now[3] + (damp * sec[3] + coef * sec[2])
            src_h[z + 1, 0, j] = s_re * mc - s_im * ms
            src_h[z + 1, 1, j] = s_re * ms + s_im * mc
            sct[0, j] = d_re * mc - d_im * ms
            sct[1, j] = d_re * ms + d_im * mc
            now, diff = nxt, step
        return 0

    lax.fori_loop(0, depth, forward, 0)

    pad = halo - edge
    for part in range(2):
        obs_n[part, : pad + SUBS, :] = jnp.zeros((pad + SUBS, LANES), f32)
        obs_n[part, win - pad - SUBS : win, :] = jnp.zeros((pad + SUBS, LANES), f32)
    per_blk = LANES // obs_rows
    where_in = (lane_src % per_blk) * obs_rows + (lane_shot * nf + lane_own) * 2
    for t in range(pl.cdiv(own + 2 * edge, LANES)):
        cut = slice(t * LANES, (t + 1) * LANES)
        turned = [
            jnp.concatenate([r[:obs_rows, cut] for r in obs_refs[q * per_blk : (q + 1) * per_blk]], axis=0).T
            for q in range(srcs // per_blk)
        ]
        rows_t = min(LANES, own + 2 * edge - t * LANES)
        for r in range(0, rows_t, SUBS):
            for part in range(2):
                v = pick(turned[0][r : r + SUBS], where_in + part)
                for q in range(1, srcs // per_blk):
                    v = jnp.where(lane_src // per_blk == q, pick(turned[q][r : r + SUBS], where_in + part), v)
                obs_n[part, pad + t * LANES + r : pad + t * LANES + r + SUBS, :] = v
    for j in range(block):
        x = cell_of(j)
        tile = jnp.where(x < 0, -1, x // LANES)
        inside = (tile >= recv_l) & (tile < recv_l + max(1, ntile // 4)) & (tile < ntile)
        m = inside.astype(f32)
        for part in range(2):
            low, high = (obs_n[part, rows, :] for rows in halves(j))
            adj[part, j] = m * (sct[part, j] - jnp.where(upper, high, low))

    @pl.when(group == 0)
    def _():
        out_mine[...] = jnp.zeros(out_mine.shape, f32)
        out_other[...] = jnp.zeros(out_other.shape, f32)

    weight = omega * scale
    nrow = span // 2
    ncol = pl.cdiv(nrow, LANES) * LANES
    lead = halo - half
    rows_in = slice(lead // 2, lead // 2 + nrow)

    def products(z):
        zi = z - z_first
        for j in range(block):
            for out, a, b in (
                (src_n, src_h[z, 0, j] * weight, src_h[z, 1, j] * -weight),
                (adj_n, adj[1, j], adj[0, j]),
            ):
                low = jnp.where(upper, pltpu.roll(b, pairs, 1), a)
                high = jnp.where(upper, b, pltpu.roll(a, pairs, 1))
                out[j % 2, pl.ds(j // 2, SUBS, stride=block // 2), :] = low
                out[j % 2, pl.ds(win // 4 + j // 2, SUBS, stride=block // 2), :] = high
        for p in range(2):
            y = lax.broadcasted_iota(jnp.int32, (nrow, LANES), 0) * 2 + (x_start + lead + p)
            left = src_n[p, rows_in, :]
            right = jnp.where((y >= 0) & (y < cells), adj_n[p, rows_in, :], 0.0)
            if ncol > nrow:
                right = jnp.concatenate([right, jnp.zeros((ncol - nrow, LANES), f32)], axis=0)
            lh, ll = split(left)
            rh, rl = split(right)
            dims_t = (((1,), (1,)), ((), ()))
            dot = functools.partial(lax.dot_general, dimension_numbers=dims_t, preferred_element_type=f32)
            prod[zi, p] = dot(lh, rl) + dot(
                jnp.concatenate([lh, ll], axis=1), jnp.concatenate([rh, rh], axis=1)
            )

    slots = LANES // HOFF

    def extract(zg, slab_at, out_ref):
        for p in range(2):
            for b in range(nrow // SUBS):
                acc = None
                column = lane % HOFF + sub + (b * SUBS - half)
                for q in range(slots):
                    z = slab_at + zg * slots + q
                    lo = max(0, b * SUBS - half) // LANES
                    hi = min(b * SUBS + SUBS - 1 + half - 1, ncol - 1) // LANES
                    v = None
                    for t in range(lo, hi + 1):
                        part = prod[z, p, b * SUBS : (b + 1) * SUBS, t * LANES : (t + 1) * LANES]
                        part = pick(part, (column + LANES) & (LANES - 1))
                        if v is None:
                            v = part
                        else:
                            v = jnp.where(column >= t * LANES, part, v)
                    acc = v if acc is None else jnp.where(lane >= q * HOFF, v, acc)
                skew[pl.ds(2 * b * SUBS + p, SUBS, stride=2), :] = acc
        tiles = pl.cdiv(span, LANES)
        turned = [skew[t * LANES : (t + 1) * LANES, :].T for t in range(tiles)]
        for q in range(slots):
            for hq in range(HOFF // SUBS):
                rows = slice(q * HOFF + hq * SUBS, q * HOFF + (hq + 1) * SUBS)
                column = lane - sub + (HOFF - hq * SUBS)
                moved = [pick(turned[t][rows], column & (LANES - 1)) for t in range(tiles)]
                for t in range(pl.cdiv(own, LANES)):
                    v = moved[t]
                    if t + 1 < tiles:
                        v = jnp.where(column < LANES, v, moved[t + 1])
                    width = min(LANES, own - t * LANES)
                    out_ref[zg * slots + q, hq * SUBS : (hq + 1) * SUBS, t * LANES : t * LANES + width] += v[:, :width]

    def backward(k, _):
        z = depth - 1 - k

        def turn(j):
            mc, ms = phase_s[z, 0, j], phase_s[z, 1, j]
            ar, ai = adj[0, j], adj[1, j]
            return ar * mc + ai * ms, ai * mc - ar * ms

        first = turn(0)
        last = turn(block - 1)
        before = [up_sub(v) for v in last]
        after = [down_sub(v) for v in first]
        now = first
        diff = [a - b for a, b in zip(now, before)]
        for j in range(block):
            nxt = after if j == block - 1 else (last if j == block - 2 else turn(j + 1))
            step = [a - b for a, b in zip(nxt, now)]
            sec = [a - b for a, b in zip(step, diff)]
            adj[0, j] = now[0] + (damp * sec[0] + coef * sec[1])
            adj[1, j] = now[1] + (damp * sec[1] - coef * sec[0])
            now, diff = nxt, step

        return 0

    def backward_slab(k, _):
        backward(k, 0)
        products(depth - 1 - k)
        return 0

    ahead = depth - z_first - slab
    lax.fori_loop(0, ahead, backward, 0)
    lax.fori_loop(ahead, ahead + slab, backward_slab, 0)

    @pl.loop(0, zloc // slots)
    def _(zg):
        extract(zg, core * zloc, out_mine)
        extract(zg, (1 - core) * zloc, out_other)


def local(
    slowness, reflect, omega, spread_coef, wavelet, ray_param, source_cell, aperture_tile, receiver_tile, observed,
):
    nd = lax.axis_size("depth")
    nq = lax.axis_size("freq")
    zloc, cells = slowness.shape
    depth = zloc * nd
    shots, nf, _, _ = observed.shape
    own = cells // nq
    halo = HOFF // 2 + 2 * depth
    win = own + 2 * halo
    block = win // (2 * SUBS)
    wide = pl.cdiv(win, LANES) * LANES
    per = LANES // (2 * shots)
    slot = shots * nf
    groups = nq * slot // LANES
    srcs = LANES // slot
    half = HOFF // 2
    edge = half + depth + half
    obsw = pl.cdiv(own + 2 * edge, LANES) * LANES
    direct = groups == 1 and nq == 8
    smem = pl.BlockSpec(memory_space=pltpu.SMEM)
    rows = 2 * slot + SUBS

    fetch = ((7, 4, 3, 0), (6, 5, 2, 1))
    if direct:
        count = nq // 2
        peers = lambda c, d, k: c ^ jnp.where(d % 2 == 0, fetch[0][k], fetch[1][k])
    else:
        count = nq
        peers = lambda c, d, k: k

    packed = pl.pallas_call(
        functools.partial(
            pack,
            dims=(shots, nf, depth, zloc, cells, own, halo, edge, wide, obsw),
            peers=peers,
        ),
        in_specs=[smem] * 3 + [pl.BlockSpec(memory_space=pltpu.VMEM)] * 3,
        out_shape=[jax.ShapeDtypeStruct((2, zloc, wide), jnp.float32)]
        + [jax.ShapeDtypeStruct((1, rows, obsw), jnp.float32)] * count,
    )(omega, spread_coef, wavelet, slowness, reflect, observed)
    both, parts = {0: packed[0]}, packed[1:]

    def swap(value, bit):
        return lax.ppermute(value, "depth", [(i, i ^ bit) for i in range(nd)])

    bit = nd // 2
    while bit > 1:
        both.update({k ^ bit: swap(v, bit) for k, v in list(both.items())})
        bit //= 2
    if direct:
        parts = [
            lax.ppermute(
                part,
                ("depth", "freq"),
                [(d * nq + i, d * nq + (i ^ fetch[d % 2][k])) for d in range(nd) for i in range(nq)],
            )
            for k, part in enumerate(parts)
        ]
        parts = parts + [swap(part, 1) for part in parts]
    else:
        parts = lax.all_to_all(jnp.stack(parts), "freq", 0, 0).reshape(groups, srcs, rows, obsw)
        parts = [parts[:, k] for k in range(srcs)]
    both.update({k ^ 1: swap(v, 1) for k, v in list(both.items())})
    both = [both[k] for k in range(nd)]

    dims = (shots, nf, depth, zloc, cells, own, halo, edge, block, 1.0 / math.sqrt(shots * nf * nq))
    natr = wide
    grid_spec = pltpu.PrefetchScalarGridSpec(
        num_scalar_prefetch=0,
        grid=(groups,),
        in_specs=[
            smem, smem, smem, smem,
        ]
        + [pl.BlockSpec((2, zloc, wide), lambda g: (0, 0, 0))] * nd
        + [pl.BlockSpec((None, rows, obsw), lambda g: (g, 0, 0))] * srcs,
        out_specs=[pl.BlockSpec((zloc, HOFF, own), lambda g: (0, 0, 0))] * 2,
        scratch_shapes=[
            pltpu.VMEM((natr, LANES), jnp.float32),
            pltpu.VMEM((2 * depth * per // LANES, block, SUBS, LANES), jnp.float32),
            pltpu.VMEM((2 * depth * per // LANES, block, SUBS, LANES), jnp.float32),
            pltpu.VMEM((2 * depth * per // LANES, block, SUBS, LANES), jnp.float32),
            pltpu.VMEM((block, SUBS, LANES), jnp.float32),
            pltpu.VMEM((depth, 2, block, SUBS, LANES), jnp.float32),
            pltpu.VMEM((depth + 1, 2, block, SUBS, LANES), jnp.float32),
            pltpu.VMEM((2, block, SUBS, LANES), jnp.float32),
            pltpu.VMEM((2, block, SUBS, LANES), jnp.float32),
            pltpu.VMEM((2, natr, LANES), jnp.float32),
            pltpu.VMEM((2, win // 2, LANES), jnp.float32),
            pltpu.VMEM((2, win // 2, LANES), jnp.float32),
            pltpu.VMEM((2 * zloc, 2, (own + HOFF) // 2, pl.cdiv((own + HOFF) // 2, LANES) * LANES), jnp.float32),
            pltpu.VMEM((pl.cdiv(own + HOFF, LANES) * LANES, LANES), jnp.float32),
        ],
    )
    mine, other = pl.pallas_call(
        functools.partial(migrate, dims=dims, srcs=srcs, zsrc=nd),
        out_shape=[jax.ShapeDtypeStruct((zloc, HOFF, own), jnp.float32)] * 2,
        grid_spec=grid_spec,
        compiler_params=pltpu.CompilerParams(vmem_limit_bytes=56 << 20),
    )(ray_param, source_cell, aperture_tile, receiver_tile, *both, *parts)
    return mine + swap(other, 1)


def solution(mesh):
    return jax.shard_map(
        local,
        mesh=mesh,
        in_specs=(
            P("depth", None), P("depth", None), P("freq"), P("freq"), P("freq", None),
            P(), P(), P(), P(), P(None, "freq", None, None),
        ),
        out_specs=P("depth", None, "freq"),
        check_vma=False,
    )
```

```python
import functools
import math

import jax
import jax.numpy as jnp
from jax import lax
from jax.experimental import pallas as pl
from jax.experimental.pallas import tpu as pltpu
from jax.sharding import PartitionSpec as P

HOFF = 32
LANES = 128
SUBS = 8
UNROLL = 8


def sincos(angle):
    turns = jnp.floor(angle * 0.6366197723675814 + 0.5)
    rem = angle - turns * 1.5703125
    rem = rem - turns * 4.837512969970703125e-4
    rem = rem - turns * 7.54978995489188216e-8
    sq = rem * rem
    sin_p = rem + rem * sq * (-1.6666654611e-1 + sq * (8.3321608736e-3 + sq * -1.9515295891e-4))
    cos_p = (1.0 - 0.5 * sq) + sq * sq * (
        4.166664568298827e-2 + sq * (-1.388731625493765e-3 + sq * 2.443315711809948e-5)
    )
    quad = turns.astype(jnp.int32)
    odd = (quad & 1) == 1
    sine = jnp.where(odd, cos_p, sin_p)
    cosine = jnp.where(odd, sin_p, cos_p)
    sine = jnp.where((quad & 2) == 2, -sine, sine)
    cosine = jnp.where(((quad + 1) & 2) == 2, -cosine, cosine)
    return cosine, sine


def pick(values, index):
    return jnp.take_along_axis(values, index, axis=1, mode="promise_in_bounds")


def split(values):
    high = values.astype(jnp.bfloat16)
    low = (values - high.astype(jnp.float32)).astype(jnp.bfloat16)
    return high, low


def pack(omega, coef, wave, slow_ref, refl_ref, obs_ref, both_ref, *outs, dims, peers):
    shots, nf, depth, zloc, cells, own, halo, edge, wide, obsw = dims
    col = lax.axis_index("freq")
    dev = lax.axis_index("depth")

    def window(load, first, width):
        tiles = pl.cdiv(width, LANES) + 1
        low = first + cells * LANES
        base = low // LANES - cells
        off = low % LANES
        cut = [
            load(pl.ds(pl.multiple_of(jnp.clip(base + t, 0, cells // LANES - 1) * LANES, LANES), LANES))
            for t in range(tiles)
        ]
        full = jnp.concatenate(cut, axis=1)
        return pltpu.roll(full, (tiles * LANES - off) % (tiles * LANES), 1)[:, :width]

    first = col * own - halo
    both_ref[0] = window(lambda c: slow_ref[:, c], first, wide)
    both_ref[1] = window(lambda c: refl_ref[:, c], first, wide)
    lane = lax.broadcasted_iota(jnp.int32, (1, obsw), 1) % nf

    def spread(read):
        acc = jnp.zeros((1, obsw), jnp.float32)
        for f in range(nf):
            acc = jnp.where(lane == f, read(f), acc)
        return acc

    table = jnp.concatenate(
        [
            spread(lambda f: omega[f]),
            spread(lambda f: coef[f]),
            spread(lambda f: wave[f, 0]),
            spread(lambda f: wave[f, 1]),
            jnp.zeros((4, obsw), jnp.float32),
        ],
        axis=0,
    )
    for k, out in enumerate(outs):
        dest = peers(col, dev, k)
        out[0, : 2 * shots * nf] = window(lambda c: obs_ref[:, :, :, c].reshape(2 * shots * nf, LANES), dest * own - edge, obsw)
        out[0, 2 * shots * nf :] = table


def migrate(
    ray, cell, aper, recv, *refs, dims, srcs, zsrc,
):
    sr_refs, (out_mine, out_other, nat, cos_c, sin_c, wgt_c, mask_s, phase_s, src_h, sct, adj, obs_n, src_n, adj_n, prod, skew) = refs[: zsrc + srcs], refs[zsrc + srcs :]
    sr_refs, obs_refs = sr_refs[:zsrc], sr_refs[zsrc:]
    shots, nf, depth, zloc, cells, own, halo, edge, block, scale = dims
    half = HOFF // 2
    win = own + 2 * halo
    pairs = LANES // 2
    nfc = nf // 2
    per = pairs // shots
    zper = pairs // per
    span = own + HOFF
    f32 = jnp.float32
    group = pl.program_id(0)
    x_start = lax.axis_index("freq") * own - halo
    dev = lax.axis_index("depth")
    core = dev % 2
    z_first = (dev - core) * zloc
    slab = 2 * zloc

    lane = lax.broadcasted_iota(jnp.int32, (SUBS, LANES), 1)
    sub = lax.broadcasted_iota(jnp.int32, (SUBS, LANES), 0)
    upper = lane >= pairs
    pair = lane % pairs
    lane_src = pair // (shots * nfc)
    lane_shot = (pair // nfc) % shots
    lane_f = lane_src * nfc + pair % nfc
    lane_own = core * nfc + pair % nfc

    obs_rows = 2 * shots * nf
    table = jnp.zeros((SUBS, LANES), jnp.float32)
    for k in range(srcs):
        table = jnp.where(lane_src == k, obs_refs[k][obs_rows:, :LANES], table)

    table = pick(table, lane_src * (shots * nfc) + lane_own)

    def row(k):
        return jnp.broadcast_to(table[k : k + 1, :], (SUBS, LANES))

    omega, coef, wave_re, wave_im = row(0), row(1), row(2), row(3)
    damp = 0.26 - jnp.sqrt(0.0625 - coef * coef)
    comp_f = lane % per
    comp_z = pair // per
    omega_c = pick(omega, (comp_f // nfc) * (shots * nfc) + comp_f % nfc)

    def per_shot(ref, dtype):
        acc = jnp.zeros((SUBS, LANES), dtype)
        for s in range(shots):
            acc = jnp.where(lane_shot == s, ref[s], acc)
        return acc

    ray_l = per_shot(ray, f32)
    cell_l = per_shot(cell, jnp.int32)
    aper_l = per_shot(aper, jnp.int32)
    recv_l = per_shot(recv, jnp.int32)
    ntile = cells // LANES

    rows2 = 2 * depth
    for t in range(pl.cdiv(win, LANES)):
        cut = slice(t * LANES, (t + 1) * LANES)
        blk = [r[part, :, cut] for part in range(2) for r in sr_refs]
        blk = jnp.concatenate(blk + [jnp.zeros((LANES - rows2, LANES), f32)], axis=0)
        nat[t * LANES : (t + 1) * LANES, :] = blk.T

    def halves(j):
        return pl.ds(j, SUBS, stride=block), pl.ds(win // 2 + j, SUBS, stride=block)

    def cell_of(j):
        return x_start + (sub + jnp.where(upper, SUBS, 0)) * block + j

    def compact(zg, _):
        z = zg * zper + comp_z
        zrow = ((z // zloc) ^ dev) * zloc + z % zloc
        for j in range(block):
            low, high = (nat[rows, :] for rows in halves(j))
            c, s = sincos(omega_c * jnp.where(upper, pick(high, zrow), pick(low, zrow)))
            cos_c[zg, j] = c
            sin_c[zg, j] = s
            wgt_c[zg, j] = omega_c * jnp.where(upper, pick(high, zrow + depth), pick(low, zrow + depth))
        return 0

    lax.fori_loop(0, depth // zper, compact, 0)

    for j in range(block):
        x = cell_of(j)
        tile = jnp.where(x < 0, -1, x // LANES)
        inside = (tile >= aper_l) & (tile < aper_l + ntile // 2) & (tile < ntile)
        m = inside.astype(f32)
        mask_s[j] = m
        dist = (x - cell_l).astype(f32)
        c, s = sincos(omega * ray_l * dist)
        src_h[0, 0, j] = (wave_re * c - wave_im * s) * m
        src_h[0, 1, j] = (wave_re * s + wave_im * c) * m
        sct[0, j] = jnp.zeros((SUBS, LANES), f32)
        sct[1, j] = jnp.zeros((SUBS, LANES), f32)

    def up_sub(v):
        v = pltpu.roll(v, 1, 0)
        return jnp.where(sub == 0, pltpu.roll(v, pairs, 1), v)

    def down_sub(v):
        v = pltpu.roll(v, SUBS - 1, 0)
        return jnp.where(sub == SUBS - 1, pltpu.roll(v, pairs, 1), v)

    def forward(z, _):
        zg = z // zper
        idx = (z % zper) * per + lane_f + jnp.where(upper, pairs, 0)

        def born(j):
            w = pick(wgt_c[zg, j], idx)
            sr, si = src_h[z, 0, j], src_h[z, 1, j]
            return sr, si, sct[0, j] - w * si, sct[1, j] + w * sr

        first = born(0)
        last = born(block - 1)
        before = [up_sub(v) for v in last]
        after = [down_sub(v) for v in first]
        now = first
        diff = [a - b for a, b in zip(now, before)]
        for j in range(block):
            nxt = after if j == block - 1 else (last if j == block - 2 else born(j + 1))
            step = [a - b for a, b in zip(nxt, now)]
            sec = [a - b for a, b in zip(step, diff)]
            m = mask_s[j]
            mc = m * pick(cos_c[zg, j], idx)
            ms = m * pick(sin_c[zg, j], idx)
            phase_s[z, 0, j] = mc
            phase_s[z, 1, j] = ms
            s_re = now[0] + (damp * sec[0] - coef * sec[1])
            s_im = now[1] + (damp * sec[1] + coef * sec[0])
            d_re = now[2] + (damp * sec[2] - coef * sec[3])
            d_im = now[3] + (damp * sec[3] + coef * sec[2])
            src_h[z + 1, 0, j] = s_re * mc - s_im * ms
            src_h[z + 1, 1, j] = s_re * ms + s_im * mc
            sct[0, j] = d_re * mc - d_im * ms
            sct[1, j] = d_re * ms + d_im * mc
            now, diff = nxt, step
        return 0

    lax.fori_loop(0, depth, forward, 0)

    pad = halo - edge
    for part in range(2):
        obs_n[part, : pad + SUBS, :] = jnp.zeros((pad + SUBS, LANES), f32)
        obs_n[part, win - pad - SUBS : win, :] = jnp.zeros((pad + SUBS, LANES), f32)
    per_blk = LANES // obs_rows
    where_in = (lane_src % per_blk) * obs_rows + (lane_shot * nf + lane_own) * 2
    for t in range(pl.cdiv(own + 2 * edge, LANES)):
        cut = slice(t * LANES, (t + 1) * LANES)
        turned = [
            jnp.concatenate([r[:obs_rows, cut] for r in obs_refs[q * per_blk : (q + 1) * per_blk]], axis=0).T
            for q in range(srcs // per_blk)
        ]
        rows_t = min(LANES, own + 2 * edge - t * LANES)
        for r in range(0, rows_t, SUBS):
            for part in range(2):
                v = pick(turned[0][r : r + SUBS], where_in + part)
                for q in range(1, srcs // per_blk):
                    v = jnp.where(lane_src // per_blk == q, pick(turned[q][r : r + SUBS], where_in + part), v)
                obs_n[part, pad + t * LANES + r : pad + t * LANES + r + SUBS, :] = v
    for j in range(block):
        x = cell_of(j)
        tile = jnp.where(x < 0, -1, x // LANES)
        inside = (tile >= recv_l) & (tile < recv_l + max(1, ntile // 4)) & (tile < ntile)
        m = inside.astype(f32)
        for part in range(2):
            low, high = (obs_n[part, rows, :] for rows in halves(j))
            adj[part, j] = m * (sct[part, j] - jnp.where(upper, high, low))

    @pl.when(group == 0)
    def _():
        out_mine[...] = jnp.zeros(out_mine.shape, f32)
        out_other[...] = jnp.zeros(out_other.shape, f32)

    weight = omega * scale
    nrow = span // 2
    ncol = pl.cdiv(nrow, LANES) * LANES
    lead = halo - half
    rows_in = slice(lead // 2, lead // 2 + nrow)

    def products(z, odd):
        zi = z - z_first
        for j in range(block):
            for out, a, b in (
                (src_n, src_h[z, 0, j] * weight, src_h[z, 1, j] * -weight),
                (adj_n, adj[1, j], adj[0, j]),
            ):
                turn = pltpu.roll(jnp.where(upper, a, b), pairs, 1)
                low = jnp.where(upper, turn, a)
                high = jnp.where(upper, b, turn)
                out[j % 2, pl.ds(j // 2, SUBS, stride=block // 2), :] = low
                out[j % 2, pl.ds(win // 4 + j // 2, SUBS, stride=block // 2), :] = high
        for p in range(2):
            y = lax.broadcasted_iota(jnp.int32, (nrow, LANES), 0) * 2 + (x_start + lead + p)
            left = src_n[p, rows_in, :]
            right = jnp.where((y >= 0) & (y < cells), adj_n[p, rows_in, :], 0.0)
            if ncol > nrow:
                right = jnp.concatenate([right, jnp.zeros((ncol - nrow, LANES), f32)], axis=0)
            if odd:
                cuts = [right[i : i + pairs] for i in range(0, ncol, pairs)]
                right = jnp.concatenate([cuts[i ^ 1] for i in range(len(cuts))], axis=0)
            lh, ll = split(left)
            rh, rl = split(right)
            dims_t = (((1,), (1,)), ((), ()))
            dot = functools.partial(lax.dot_general, dimension_numbers=dims_t, preferred_element_type=f32)
            prod[zi, p] = dot(lh, rl) + dot(
                jnp.concatenate([lh, ll], axis=1), jnp.concatenate([rh, rh], axis=1)
            )

    slots = LANES // HOFF

    def extract(zg, slab_at, out_ref):
        for p in range(2):
            for b in range(nrow // SUBS):
                rows = slice(b * SUBS, (b + 1) * SUBS)
                first = b * SUBS - half
                near = ((lane - first) & (LANES - 1)) < pairs
                index = (lane % HOFF + sub + first + (lane // HOFF) * pairs) & (LANES - 1)

                def window(z, start):
                    at = max(first, 0)
                    v = prod[z, p, rows, at // LANES * LANES : (at // LANES + 1) * LANES]
                    end = min(b * SUBS + SUBS + half - 1, nrow)
                    if at // LANES < (end - 1) // LANES:
                        v2 = prod[z, p, rows, (at // LANES + 1) * LANES : (at // LANES + 2) * LANES]
                        v = jnp.where(((lane - start) & (LANES - 1)) < at % LANES - SUBS, v2, v)
                    return v

                acc = None
                for q in range(0, slots, 2):
                    z = slab_at + zg * slots + q
                    v = jnp.where(near, window(z, 0), window(z + 1, pairs))
                    v = pick(v, index)
                    acc = v if acc is None else jnp.where(lane >= q * HOFF, v, acc)
                skew[pl.ds(2 * b * SUBS + p, SUBS, stride=2), :] = acc
        tiles = pl.cdiv(span, LANES)
        turned = [skew[t * LANES : (t + 1) * LANES, :].T for t in range(tiles)]
        for q in range(slots):
            for hq in range(HOFF // SUBS):
                rows = slice(q * HOFF + hq * SUBS, q * HOFF + (hq + 1) * SUBS)
                for t in range(pl.cdiv(own, LANES)):
                    v = turned[t][rows]
                    if t + 1 < tiles:
                        v = jnp.where(lane < HOFF - hq * SUBS - sub, turned[t + 1][rows], v)
                    v = pltpu.roll(v, (hq * SUBS - HOFF) % LANES, 1, stride=1, stride_axis=0)
                    width = min(LANES, own - t * LANES)
                    out_ref[zg * slots + q, hq * SUBS : (hq + 1) * SUBS, t * LANES : t * LANES + width] += v[:, :width]

    def backward(k, _):
        z = depth - 1 - k

        def turn(j):
            mc, ms = phase_s[z, 0, j], phase_s[z, 1, j]
            ar, ai = adj[0, j], adj[1, j]
            return ar * mc + ai * ms, ai * mc - ar * ms

        first = turn(0)
        last = turn(block - 1)
        before = [up_sub(v) for v in last]
        after = [down_sub(v) for v in first]
        now = first
        diff = [a - b for a, b in zip(now, before)]
        for j in range(block):
            nxt = after if j == block - 1 else (last if j == block - 2 else turn(j + 1))
            step = [a - b for a, b in zip(nxt, now)]
            sec = [a - b for a, b in zip(step, diff)]
            adj[0, j] = now[0] + (damp * sec[0] + coef * sec[1])
            adj[1, j] = now[1] + (damp * sec[1] - coef * sec[0])
            now, diff = nxt, step

        return 0

    def backward_slab(k, i):
        backward(k, 0)
        products(depth - 1 - k, (i + 1) % 2)
        return 0

    ahead = depth - z_first - slab
    lax.fori_loop(0, ahead, backward, 0)

    def several(k, _):
        for i in range(UNROLL):
            backward_slab(ahead + UNROLL * k + i, i)
        return 0

    lax.fori_loop(0, slab // UNROLL, several, 0)

    @pl.loop(0, zloc // slots)
    def _(zg):
        extract(zg, core * zloc, out_mine)
        extract(zg, (1 - core) * zloc, out_other)


def local(
    slowness, reflect, omega, spread_coef, wavelet, ray_param, source_cell, aperture_tile, receiver_tile, observed,
):
    nd = lax.axis_size("depth")
    nq = lax.axis_size("freq")
    zloc, cells = slowness.shape
    depth = zloc * nd
    shots, nf, _, _ = observed.shape
    own = cells // nq
    halo = HOFF // 2 + 2 * depth
    win = own + 2 * halo
    block = win // (2 * SUBS)
    wide = pl.cdiv(win, LANES) * LANES
    per = LANES // (2 * shots)
    slot = shots * nf
    groups = nq * slot // LANES
    srcs = LANES // slot
    half = HOFF // 2
    edge = half + depth + half
    obsw = pl.cdiv(own + 2 * edge, LANES) * LANES
    direct = groups == 1 and nq == 8
    smem = pl.BlockSpec(memory_space=pltpu.SMEM)
    rows = 2 * slot + SUBS

    fetch = ((7, 4, 3, 0), (6, 5, 2, 1))
    if direct:
        count = nq // 2
        peers = lambda c, d, k: c ^ jnp.where(d % 2 == 0, fetch[0][k], fetch[1][k])
    else:
        count = nq
        peers = lambda c, d, k: k

    packed = pl.pallas_call(
        functools.partial(
            pack,
            dims=(shots, nf, depth, zloc, cells, own, halo, edge, wide, obsw),
            peers=peers,
        ),
        in_specs=[smem] * 3 + [pl.BlockSpec(memory_space=pltpu.VMEM)] * 3,
        out_shape=[jax.ShapeDtypeStruct((2, zloc, wide), jnp.float32)]
        + [jax.ShapeDtypeStruct((1, rows, obsw), jnp.float32)] * count,
    )(omega, spread_coef, wavelet, slowness, reflect, observed)
    both, parts = {0: packed[0]}, packed[1:]

    def swap(value, bit):
        return lax.ppermute(value, "depth", [(i, i ^ bit) for i in range(nd)])

    bit = nd // 2
    while bit > 1:
        both.update({k ^ bit: swap(v, bit) for k, v in list(both.items())})
        bit //= 2
    if direct:
        parts = [
            lax.ppermute(
                part,
                ("depth", "freq"),
                [(d * nq + i, d * nq + (i ^ fetch[d % 2][k])) for d in range(nd) for i in range(nq)],
            )
            for k, part in enumerate(parts)
        ]
        parts = parts + [swap(part, 1) for part in parts]
    else:
        parts = lax.all_to_all(jnp.stack(parts), "freq", 0, 0).reshape(groups, srcs, rows, obsw)
        parts = [parts[:, k] for k in range(srcs)]
    both.update({k ^ 1: swap(v, 1) for k, v in list(both.items())})
    both = [both[k] for k in range(nd)]

    dims = (shots, nf, depth, zloc, cells, own, halo, edge, block, 1.0 / math.sqrt(shots * nf * nq))
    natr = wide
    grid_spec = pltpu.PrefetchScalarGridSpec(
        num_scalar_prefetch=0,
        grid=(groups,),
        in_specs=[
            smem, smem, smem, smem,
        ]
        + [pl.BlockSpec((2, zloc, wide), lambda g: (0, 0, 0))] * nd
        + [pl.BlockSpec((None, rows, obsw), lambda g: (g, 0, 0))] * srcs,
        out_specs=[pl.BlockSpec((zloc, HOFF, own), lambda g: (0, 0, 0))] * 2,
        scratch_shapes=[
            pltpu.VMEM((natr, LANES), jnp.float32),
            pltpu.VMEM((2 * depth * per // LANES, block, SUBS, LANES), jnp.float32),
            pltpu.VMEM((2 * depth * per // LANES, block, SUBS, LANES), jnp.float32),
            pltpu.VMEM((2 * depth * per // LANES, block, SUBS, LANES), jnp.float32),
            pltpu.VMEM((block, SUBS, LANES), jnp.float32),
            pltpu.VMEM((depth, 2, block, SUBS, LANES), jnp.float32),
            pltpu.VMEM((depth + 1, 2, block, SUBS, LANES), jnp.float32),
            pltpu.VMEM((2, block, SUBS, LANES), jnp.float32),
            pltpu.VMEM((2, block, SUBS, LANES), jnp.float32),
            pltpu.VMEM((2, natr, LANES), jnp.float32),
            pltpu.VMEM((2, win // 2, LANES), jnp.float32),
            pltpu.VMEM((2, win // 2, LANES), jnp.float32),
            pltpu.VMEM((2 * zloc, 2, (own + HOFF) // 2, pl.cdiv((own + HOFF) // 2, LANES) * LANES), jnp.float32),
            pltpu.VMEM((pl.cdiv(own + HOFF, LANES) * LANES, LANES), jnp.float32),
        ],
    )
    mine, other = pl.pallas_call(
        functools.partial(migrate, dims=dims, srcs=srcs, zsrc=nd),
        out_shape=[jax.ShapeDtypeStruct((zloc, HOFF, own), jnp.float32)] * 2,
        grid_spec=grid_spec,
        compiler_params=pltpu.CompilerParams(vmem_limit_bytes=56 << 20),
    )(ray_param, source_cell, aperture_tile, receiver_tile, *both, *parts)
    return mine + swap(other, 1)


def solution(mesh):
    return jax.shard_map(
        local,
        mesh=mesh,
        in_specs=(
            P("depth", None), P("depth", None), P("freq"), P("freq"), P("freq", None),
            P(), P(), P(), P(), P(None, "freq", None, None),
        ),
        out_specs=P("depth", None, "freq"),
        check_vma=False,
    )
```

```python
import functools
import math

import jax
import jax.numpy as jnp
from jax import lax
from jax.experimental import pallas as pl
from jax.experimental.pallas import tpu as pltpu
from jax.sharding import PartitionSpec as P

HOFF = 32
LANES = 128
SUBS = 8
UNROLL = 8


def sincos(angle):
    turns = jnp.floor(angle * 0.6366197723675814 + 0.5)
    rem = angle - turns * 1.5703125
    rem = rem - turns * 4.837512969970703125e-4
    rem = rem - turns * 7.54978995489188216e-8
    sq = rem * rem
    sin_p = rem + rem * sq * (-1.6666654611e-1 + sq * (8.3321608736e-3 + sq * -1.9515295891e-4))
    cos_p = (1.0 - 0.5 * sq) + sq * sq * (
        4.166664568298827e-2 + sq * (-1.388731625493765e-3 + sq * 2.443315711809948e-5)
    )
    quad = turns.astype(jnp.int32)
    odd = (quad & 1) == 1
    sine = jnp.where(odd, cos_p, sin_p)
    cosine = jnp.where(odd, sin_p, cos_p)
    sine = jnp.where((quad & 2) == 2, -sine, sine)
    cosine = jnp.where(((quad + 1) & 2) == 2, -cosine, cosine)
    return cosine, sine


def pick(values, index):
    return jnp.take_along_axis(values, index, axis=1, mode="promise_in_bounds")


def split(values):
    high = values.astype(jnp.bfloat16)
    low = (values - high.astype(jnp.float32)).astype(jnp.bfloat16)
    return high, low


def pack(omega, coef, wave, slow_ref, refl_ref, obs_ref, both_ref, *outs, dims, peers):
    shots, nf, depth, zloc, cells, own, halo, edge, wide, obsw = dims
    col = lax.axis_index("freq")
    dev = lax.axis_index("depth")

    def window(load, first, width):
        tiles = pl.cdiv(width, LANES) + 1
        low = first + cells * LANES
        base = low // LANES - cells
        off = low % LANES
        cut = [
            load(pl.ds(pl.multiple_of(jnp.clip(base + t, 0, cells // LANES - 1) * LANES, LANES), LANES))
            for t in range(tiles)
        ]
        full = jnp.concatenate(cut, axis=1)
        return pltpu.roll(full, (tiles * LANES - off) % (tiles * LANES), 1)[:, :width]

    first = col * own - halo
    both_ref[0] = window(lambda c: slow_ref[:, c], first, wide)
    both_ref[1] = window(lambda c: refl_ref[:, c], first, wide)
    lane = lax.broadcasted_iota(jnp.int32, (1, obsw), 1) % nf

    def spread(read):
        acc = jnp.zeros((1, obsw), jnp.float32)
        for f in range(nf):
            acc = jnp.where(lane == f, read(f), acc)
        return acc

    table = jnp.concatenate(
        [
            spread(lambda f: omega[f]),
            spread(lambda f: coef[f]),
            spread(lambda f: wave[f, 0]),
            spread(lambda f: wave[f, 1]),
            jnp.zeros((4, obsw), jnp.float32),
        ],
        axis=0,
    )
    for k, out in enumerate(outs):
        dest = peers(col, dev, k)
        out[0, : 2 * shots * nf] = window(lambda c: obs_ref[:, :, :, c].reshape(2 * shots * nf, LANES), dest * own - edge, obsw)
        out[0, 2 * shots * nf :] = table


def migrate(
    ray, cell, aper, recv, *refs, dims, srcs, zsrc,
):
    sr_refs, (out_mine, out_other, nat, cos_c, sin_c, wgt_c, mask_s, phase_s, src_h, sct, adj, obs_n, src_n, adj_n, prod, skew) = refs[: zsrc + srcs], refs[zsrc + srcs :]
    sr_refs, obs_refs = sr_refs[:zsrc], sr_refs[zsrc:]
    shots, nf, depth, zloc, cells, own, halo, edge, block, scale = dims
    half = HOFF // 2
    win = own + 2 * halo
    pairs = LANES // 2
    nfc = nf // 2
    per = pairs // shots
    zper = pairs // per
    span = own + HOFF
    f32 = jnp.float32
    group = pl.program_id(0)
    x_start = lax.axis_index("freq") * own - halo
    dev = lax.axis_index("depth")
    core = dev % 2
    z_first = (dev - core) * zloc
    slab = 2 * zloc

    lane = lax.broadcasted_iota(jnp.int32, (SUBS, LANES), 1)
    sub = lax.broadcasted_iota(jnp.int32, (SUBS, LANES), 0)
    upper = lane >= pairs
    pair = lane % pairs
    lane_src = pair // (shots * nfc)
    lane_shot = (pair // nfc) % shots
    lane_f = lane_src * nfc + pair % nfc
    lane_own = core * nfc + pair % nfc

    obs_rows = 2 * shots * nf
    table = jnp.zeros((SUBS, LANES), jnp.float32)
    for k in range(srcs):
        table = jnp.where(lane_src == k, obs_refs[k][obs_rows:, :LANES], table)

    table = pick(table, lane_src * (shots * nfc) + lane_own)

    def row(k):
        return jnp.broadcast_to(table[k : k + 1, :], (SUBS, LANES))

    omega, coef, wave_re, wave_im = row(0), row(1), row(2), row(3)
    damp = 0.26 - jnp.sqrt(0.0625 - coef * coef)
    comp_f = lane % per
    comp_z = pair // per
    omega_c = pick(omega, (comp_f // nfc) * (shots * nfc) + comp_f % nfc)

    def per_shot(ref, dtype):
        acc = jnp.zeros((SUBS, LANES), dtype)
        for s in range(shots):
            acc = jnp.where(lane_shot == s, ref[s], acc)
        return acc

    ray_l = per_shot(ray, f32)
    cell_l = per_shot(cell, jnp.int32)
    aper_l = per_shot(aper, jnp.int32)
    recv_l = per_shot(recv, jnp.int32)
    ntile = cells // LANES

    rows2 = 2 * depth
    for t in range(pl.cdiv(win, LANES)):
        cut = slice(t * LANES, (t + 1) * LANES)
        blk = [r[part, :, cut] for part in range(2) for r in sr_refs]
        blk = jnp.concatenate(blk + [jnp.zeros((LANES - rows2, LANES), f32)], axis=0)
        nat[t * LANES : (t + 1) * LANES, :] = blk.T

    def halves(j):
        return pl.ds(j, SUBS, stride=block), pl.ds(win // 2 + j, SUBS, stride=block)

    def cell_of(j):
        return x_start + (sub + jnp.where(upper, SUBS, 0)) * block + j

    def compact(zg, _):
        z = zg * zper + comp_z
        zrow = ((z // zloc) ^ dev) * zloc + z % zloc
        for j in range(block):
            low, high = (nat[rows, :] for rows in halves(j))
            c, s = sincos(omega_c * jnp.where(upper, pick(high, zrow), pick(low, zrow)))
            cos_c[zg, j] = c
            sin_c[zg, j] = s
            wgt_c[zg, j] = omega_c * jnp.where(upper, pick(high, zrow + depth), pick(low, zrow + depth))
        return 0

    lax.fori_loop(0, depth // zper, compact, 0)

    for j in range(block):
        x = cell_of(j)
        tile = jnp.where(x < 0, -1, x // LANES)
        inside = (tile >= aper_l) & (tile < aper_l + ntile // 2) & (tile < ntile)
        m = inside.astype(f32)
        mask_s[j] = m
        dist = (x - cell_l).astype(f32)
        c, s = sincos(omega * ray_l * dist)
        src_h[0, 0, j] = (wave_re * c - wave_im * s) * m
        src_h[0, 1, j] = (wave_re * s + wave_im * c) * m
        sct[0, j] = jnp.zeros((SUBS, LANES), f32)
        sct[1, j] = jnp.zeros((SUBS, LANES), f32)

    def up_sub(v):
        v = pltpu.roll(v, 1, 0)
        return jnp.where(sub == 0, pltpu.roll(v, pairs, 1), v)

    def down_sub(v):
        v = pltpu.roll(v, SUBS - 1, 0)
        return jnp.where(sub == SUBS - 1, pltpu.roll(v, pairs, 1), v)

    def forward(z, _):
        zg = z // zper
        idx = (z % zper) * per + lane_f + jnp.where(upper, pairs, 0)

        def born(j):
            w = pick(wgt_c[zg, j], idx)
            sr, si = src_h[z, 0, j], src_h[z, 1, j]
            return sr, si, sct[0, j] - w * si, sct[1, j] + w * sr

        first = born(0)
        last = born(block - 1)
        before = [up_sub(v) for v in last]
        after = [down_sub(v) for v in first]
        now = first
        diff = [a - b for a, b in zip(now, before)]
        for j in range(block):
            nxt = after if j == block - 1 else (last if j == block - 2 else born(j + 1))
            step = [a - b for a, b in zip(nxt, now)]
            sec = [a - b for a, b in zip(step, diff)]
            m = mask_s[j]
            mc = m * pick(cos_c[zg, j], idx)
            ms = m * pick(sin_c[zg, j], idx)
            phase_s[z, 0, j] = mc
            phase_s[z, 1, j] = ms
            s_re = now[0] + (damp * sec[0] - coef * sec[1])
            s_im = now[1] + (damp * sec[1] + coef * sec[0])
            d_re = now[2] + (damp * sec[2] - coef * sec[3])
            d_im = now[3] + (damp * sec[3] + coef * sec[2])
            src_h[z + 1, 0, j] = s_re * mc - s_im * ms
            src_h[z + 1, 1, j] = s_re * ms + s_im * mc
            sct[0, j] = d_re * mc - d_im * ms
            sct[1, j] = d_re * ms + d_im * mc
            now, diff = nxt, step
        return 0

    lax.fori_loop(0, depth, forward, 0)

    pad = halo - edge
    for part in range(2):
        obs_n[part, : pad + SUBS, :] = jnp.zeros((pad + SUBS, LANES), f32)
        obs_n[part, win - pad - SUBS : win, :] = jnp.zeros((pad + SUBS, LANES), f32)
    per_blk = LANES // obs_rows
    where_in = (lane_src % per_blk) * obs_rows + (lane_shot * nf + lane_own) * 2
    for t in range(pl.cdiv(own + 2 * edge, LANES)):
        cut = slice(t * LANES, (t + 1) * LANES)
        turned = [
            jnp.concatenate([r[:obs_rows, cut] for r in obs_refs[q * per_blk : (q + 1) * per_blk]], axis=0).T
            for q in range(srcs // per_blk)
        ]
        rows_t = min(LANES, own + 2 * edge - t * LANES)
        for r in range(0, rows_t, SUBS):
            for part in range(2):
                v = pick(turned[0][r : r + SUBS], where_in + part)
                for q in range(1, srcs // per_blk):
                    v = jnp.where(lane_src // per_blk == q, pick(turned[q][r : r + SUBS], where_in + part), v)
                obs_n[part, pad + t * LANES + r : pad + t * LANES + r + SUBS, :] = v
    for j in range(block):
        x = cell_of(j)
        tile = jnp.where(x < 0, -1, x // LANES)
        inside = (tile >= recv_l) & (tile < recv_l + max(1, ntile // 4)) & (tile < ntile)
        m = inside.astype(f32)
        for part in range(2):
            low, high = (obs_n[part, rows, :] for rows in halves(j))
            adj[part, j] = m * (sct[part, j] - jnp.where(upper, high, low))

    @pl.when(group == 0)
    def _():
        out_mine[...] = jnp.zeros(out_mine.shape, f32)
        out_other[...] = jnp.zeros(out_other.shape, f32)

    weight = omega * scale
    nrow = span // 2
    ncol = pl.cdiv(nrow, LANES) * LANES
    lead = halo - half
    rows_in = slice(lead // 2, lead // 2 + nrow)

    def products(z, odd):
        zi = z - z_first
        for j in range(block):
            for out, a, b in (
                (src_n, src_h[z, 0, j] * weight, src_h[z, 1, j] * -weight),
                (adj_n, adj[1, j], adj[0, j]),
            ):
                turn = pltpu.roll(jnp.where(upper, a, b), pairs, 1)
                low = jnp.where(upper, turn, a)
                high = jnp.where(upper, b, turn)
                out[j % 2, pl.ds(j // 2, SUBS, stride=block // 2), :] = low
                out[j % 2, pl.ds(win // 4 + j // 2, SUBS, stride=block // 2), :] = high
        for p in range(2):
            y = lax.broadcasted_iota(jnp.int32, (nrow, LANES), 0) * 2 + (x_start + lead + p)
            left = src_n[p, rows_in, :]
            right = jnp.where((y >= 0) & (y < cells), adj_n[p, rows_in, :], 0.0)
            if ncol > nrow:
                right = jnp.concatenate([right, jnp.zeros((ncol - nrow, LANES), f32)], axis=0)
            if odd:
                cuts = [right[i : i + pairs] for i in range(0, ncol, pairs)]
                right = jnp.concatenate([cuts[i ^ 1] for i in range(len(cuts))], axis=0)
            lh, ll = split(left)
            rh, rl = split(right)
            dims_t = (((1,), (1,)), ((), ()))
            dot = functools.partial(lax.dot_general, dimension_numbers=dims_t, preferred_element_type=f32)
            prod[zi, p] = dot(lh, rl) + dot(
                jnp.concatenate([lh, ll], axis=1), jnp.concatenate([rh, rh], axis=1)
            )

    slots = LANES // HOFF

    def extract(zg, slab_at, out_ref):
        for b in range(nrow // SUBS):
            for p in range(2):
                rows = slice(b * SUBS, (b + 1) * SUBS)
                first = b * SUBS - half
                near = ((lane - first) & (LANES - 1)) < pairs
                index = (lane % HOFF + sub + first + (lane // HOFF) * pairs) & (LANES - 1)

                def window(z, start):
                    at = max(first, 0)
                    v = prod[z, p, rows, at // LANES * LANES : (at // LANES + 1) * LANES]
                    end = min(b * SUBS + SUBS + half - 1, nrow)
                    if at // LANES < (end - 1) // LANES:
                        v2 = prod[z, p, rows, (at // LANES + 1) * LANES : (at // LANES + 2) * LANES]
                        v = jnp.where(((lane - start) & (LANES - 1)) < at % LANES - SUBS, v2, v)
                    return v

                acc = None
                for q in range(0, slots, 2):
                    z = slab_at + zg * slots + q
                    v = jnp.where(near, window(z, 0), window(z + 1, pairs))
                    v = pick(v, index)
                    acc = v if acc is None else jnp.where(lane >= q * HOFF, v, acc)
                skew[pl.ds(2 * b * SUBS + p, SUBS, stride=2), :] = acc
        tiles = pl.cdiv(span, LANES)
        turned = [skew[t * LANES : (t + 1) * LANES, :].T for t in range(tiles)]
        for q in range(slots):
            for hq in range(HOFF // SUBS):
                rows = slice(q * HOFF + hq * SUBS, q * HOFF + (hq + 1) * SUBS)
                for t in range(pl.cdiv(own, LANES)):
                    v = turned[t][rows]
                    if t + 1 < tiles:
                        v = jnp.where(lane < HOFF - hq * SUBS - sub, turned[t + 1][rows], v)
                    v = pltpu.roll(v, (hq * SUBS - HOFF) % LANES, 1, stride=1, stride_axis=0)
                    width = min(LANES, own - t * LANES)
                    out_ref[zg * slots + q, hq * SUBS : (hq + 1) * SUBS, t * LANES : t * LANES + width] += v[:, :width]

    def backward(k, _):
        z = depth - 1 - k

        def turn(j):
            mc, ms = phase_s[z, 0, j], phase_s[z, 1, j]
            ar, ai = adj[0, j], adj[1, j]
            return ar * mc + ai * ms, ai * mc - ar * ms

        first = turn(0)
        last = turn(block - 1)
        before = [up_sub(v) for v in last]
        after = [down_sub(v) for v in first]
        now = first
        diff = [a - b for a, b in zip(now, before)]
        for j in range(block):
            nxt = after if j == block - 1 else (last if j == block - 2 else turn(j + 1))
            step = [a - b for a, b in zip(nxt, now)]
            sec = [a - b for a, b in zip(step, diff)]
            adj[0, j] = now[0] + (damp * sec[0] + coef * sec[1])
            adj[1, j] = now[1] + (damp * sec[1] - coef * sec[0])
            now, diff = nxt, step

        return 0

    def backward_slab(k, i):
        backward(k, 0)
        products(depth - 1 - k, (i + 1) % 2)
        return 0

    ahead = depth - z_first - slab
    lax.fori_loop(0, ahead, backward, 0)

    def several(k, _):
        for i in range(UNROLL):
            backward_slab(ahead + UNROLL * k + i, i)
        return 0

    lax.fori_loop(0, slab // UNROLL, several, 0)

    @pl.loop(0, zloc // slots)
    def _(zg):
        extract(zg, core * zloc, out_mine)
        extract(zg, (1 - core) * zloc, out_other)


def local(
    slowness, reflect, omega, spread_coef, wavelet, ray_param, source_cell, aperture_tile, receiver_tile, observed,
):
    nd = lax.axis_size("depth")
    nq = lax.axis_size("freq")
    zloc, cells = slowness.shape
    depth = zloc * nd
    shots, nf, _, _ = observed.shape
    own = cells // nq
    halo = HOFF // 2 + 2 * depth
    win = own + 2 * halo
    block = win // (2 * SUBS)
    wide = pl.cdiv(win, LANES) * LANES
    per = LANES // (2 * shots)
    slot = shots * nf
    groups = nq * slot // LANES
    srcs = LANES // slot
    half = HOFF // 2
    edge = half + depth + half
    obsw = pl.cdiv(own + 2 * edge, LANES) * LANES
    direct = groups == 1 and nq == 8
    smem = pl.BlockSpec(memory_space=pltpu.SMEM)
    rows = 2 * slot + SUBS

    fetch = ((7, 4, 3, 0), (6, 5, 2, 1))
    if direct:
        count = nq // 2
        peers = lambda c, d, k: c ^ jnp.where(d % 2 == 0, fetch[0][k], fetch[1][k])
    else:
        count = nq
        peers = lambda c, d, k: k

    packed = pl.pallas_call(
        functools.partial(
            pack,
            dims=(shots, nf, depth, zloc, cells, own, halo, edge, wide, obsw),
            peers=peers,
        ),
        in_specs=[smem] * 3 + [pl.BlockSpec(memory_space=pltpu.VMEM)] * 3,
        out_shape=[jax.ShapeDtypeStruct((2, zloc, wide), jnp.float32)]
        + [jax.ShapeDtypeStruct((1, rows, obsw), jnp.float32)] * count,
    )(omega, spread_coef, wavelet, slowness, reflect, observed)
    both, parts = {0: packed[0]}, packed[1:]

    def swap(value, bit):
        return lax.ppermute(value, "depth", [(i, i ^ bit) for i in range(nd)])

    bit = nd // 2
    while bit > 1:
        both.update({k ^ bit: swap(v, bit) for k, v in list(both.items())})
        bit //= 2
    if direct:
        parts = [
            lax.ppermute(
                part,
                ("depth", "freq"),
                [(d * nq + i, d * nq + (i ^ fetch[d % 2][k])) for d in range(nd) for i in range(nq)],
            )
            for k, part in enumerate(parts)
        ]
        parts = parts + [swap(part, 1) for part in parts]
    else:
        parts = lax.all_to_all(jnp.stack(parts), "freq", 0, 0).reshape(groups, srcs, rows, obsw)
        parts = [parts[:, k] for k in range(srcs)]
    both.update({k ^ 1: swap(v, 1) for k, v in list(both.items())})
    both = [both[k] for k in range(nd)]

    dims = (shots, nf, depth, zloc, cells, own, halo, edge, block, 1.0 / math.sqrt(shots * nf * nq))
    natr = wide
    grid_spec = pltpu.PrefetchScalarGridSpec(
        num_scalar_prefetch=0,
        grid=(groups,),
        in_specs=[
            smem, smem, smem, smem,
        ]
        + [pl.BlockSpec((2, zloc, wide), lambda g: (0, 0, 0))] * nd
        + [pl.BlockSpec((None, rows, obsw), lambda g: (g, 0, 0))] * srcs,
        out_specs=[pl.BlockSpec((zloc, HOFF, own), lambda g: (0, 0, 0))] * 2,
        scratch_shapes=[
            pltpu.VMEM((natr, LANES), jnp.float32),
            pltpu.VMEM((2 * depth * per // LANES, block, SUBS, LANES), jnp.float32),
            pltpu.VMEM((2 * depth * per // LANES, block, SUBS, LANES), jnp.float32),
            pltpu.VMEM((2 * depth * per // LANES, block, SUBS, LANES), jnp.float32),
            pltpu.VMEM((block, SUBS, LANES), jnp.float32),
            pltpu.VMEM((depth, 2, block, SUBS, LANES), jnp.float32),
            pltpu.VMEM((depth + 1, 2, block, SUBS, LANES), jnp.float32),
            pltpu.VMEM((2, block, SUBS, LANES), jnp.float32),
            pltpu.VMEM((2, block, SUBS, LANES), jnp.float32),
            pltpu.VMEM((2, natr, LANES), jnp.float32),
            pltpu.VMEM((2, win // 2, LANES), jnp.float32),
            pltpu.VMEM((2, win // 2, LANES), jnp.float32),
            pltpu.VMEM((2 * zloc, 2, (own + HOFF) // 2, pl.cdiv((own + HOFF) // 2, LANES) * LANES), jnp.float32),
            pltpu.VMEM((pl.cdiv(own + HOFF, LANES) * LANES, LANES), jnp.float32),
        ],
    )
    mine, other = pl.pallas_call(
        functools.partial(migrate, dims=dims, srcs=srcs, zsrc=nd),
        out_shape=[jax.ShapeDtypeStruct((zloc, HOFF, own), jnp.float32)] * 2,
        grid_spec=grid_spec,
        compiler_params=pltpu.CompilerParams(vmem_limit_bytes=36 << 20),
    )(ray_param, source_cell, aperture_tile, receiver_tile, *both, *parts)
    return mine + swap(other, 1)


def solution(mesh):
    return jax.shard_map(
        local,
        mesh=mesh,
        in_specs=(
            P("depth", None), P("depth", None), P("freq"), P("freq"), P("freq", None),
            P(), P(), P(), P(), P(None, "freq", None, None),
        ),
        out_specs=P("depth", None, "freq"),
        check_vma=False,
    )
```

```python
import functools
import math

import jax
import jax.numpy as jnp
from jax import lax
from jax.experimental import pallas as pl
from jax.experimental.pallas import tpu as pltpu
from jax.sharding import PartitionSpec as P

HOFF = 32
LANES = 128
SUBS = 8
UNROLL = 16


def sincos(angle):
    turns = jnp.floor(angle * 0.6366197723675814 + 0.5)
    rem = angle - turns * 1.5703125
    rem = rem - turns * 4.837512969970703125e-4
    rem = rem - turns * 7.54978995489188216e-8
    sq = rem * rem
    sin_p = rem + rem * sq * (-1.6666654611e-1 + sq * (8.3321608736e-3 + sq * -1.9515295891e-4))
    cos_p = (1.0 - 0.5 * sq) + sq * sq * (
        4.166664568298827e-2 + sq * (-1.388731625493765e-3 + sq * 2.443315711809948e-5)
    )
    quad = turns.astype(jnp.int32)
    odd = (quad & 1) == 1
    sine = jnp.where(odd, cos_p, sin_p)
    cosine = jnp.where(odd, sin_p, cos_p)
    sine = jnp.where((quad & 2) == 2, -sine, sine)
    cosine = jnp.where(((quad + 1) & 2) == 2, -cosine, cosine)
    return cosine, sine


def pick(values, index):
    return jnp.take_along_axis(values, index, axis=1, mode="promise_in_bounds")


def split(values):
    high = values.astype(jnp.bfloat16)
    low = (values - high.astype(jnp.float32)).astype(jnp.bfloat16)
    return high, low


def pack(omega, coef, wave, slow_ref, refl_ref, obs_ref, both_ref, *outs, dims, peers):
    shots, nf, depth, zloc, cells, own, halo, edge, wide, obsw = dims
    col = lax.axis_index("freq")
    dev = lax.axis_index("depth")

    def window(load, first, width):
        tiles = pl.cdiv(width, LANES) + 1
        low = first + cells * LANES
        base = low // LANES - cells
        off = low % LANES
        cut = [
            load(pl.ds(pl.multiple_of(jnp.clip(base + t, 0, cells // LANES - 1) * LANES, LANES), LANES))
            for t in range(tiles)
        ]
        full = jnp.concatenate(cut, axis=1)
        return pltpu.roll(full, (tiles * LANES - off) % (tiles * LANES), 1)[:, :width]

    first = col * own - halo
    both_ref[0] = window(lambda c: slow_ref[:, c], first, wide)
    both_ref[1] = window(lambda c: refl_ref[:, c], first, wide)
    lane = lax.broadcasted_iota(jnp.int32, (1, obsw), 1) % nf

    def spread(read):
        acc = jnp.zeros((1, obsw), jnp.float32)
        for f in range(nf):
            acc = jnp.where(lane == f, read(f), acc)
        return acc

    table = jnp.concatenate(
        [
            spread(lambda f: omega[f]),
            spread(lambda f: coef[f]),
            spread(lambda f: wave[f, 0]),
            spread(lambda f: wave[f, 1]),
            jnp.zeros((4, obsw), jnp.float32),
        ],
        axis=0,
    )
    def observed_rows(c):
        return jnp.concatenate([obs_ref[:, f, part, c] for f in range(nf) for part in range(2)], axis=0)

    for k, out in enumerate(outs):
        dest = peers(col, dev, k)
        out[0, : 2 * shots * nf] = window(observed_rows, dest * own - edge, obsw)
        out[0, 2 * shots * nf :] = table


def migrate(
    ray, cell, aper, recv, *refs, dims, srcs, zsrc,
):
    sr_refs, (out_mine, out_other, nat, rows_s, rows_b, cos_c, sin_c, wgt, mask_s, phase_s, src_h, sct, adj, obs_n, src_n, adj_n, prod, skew) = refs[: zsrc + srcs], refs[zsrc + srcs :]
    sr_refs, obs_refs = sr_refs[:zsrc], sr_refs[zsrc:]
    shots, nf, depth, zloc, cells, own, halo, edge, block, scale = dims
    half = HOFF // 2
    win = own + 2 * halo
    pairs = LANES // 2
    nfc = nf // 2
    per = pairs // shots
    zper = pairs // per
    span = own + HOFF
    f32 = jnp.float32
    group = pl.program_id(0)
    x_start = lax.axis_index("freq") * own - halo
    dev = lax.axis_index("depth")
    core = dev % 2
    z_first = (dev - core) * zloc
    slab = 2 * zloc

    lane = lax.broadcasted_iota(jnp.int32, (SUBS, LANES), 1)
    sub = lax.broadcasted_iota(jnp.int32, (SUBS, LANES), 0)
    upper = lane >= pairs
    pair = lane % pairs
    lane_src = pair // (shots * nfc)
    lane_shot = pair % shots
    lane_f2 = (pair // shots) % nfc
    lane_f = lane_src * nfc + lane_f2
    lane_own = core * nfc + lane_f2

    obs_rows = 2 * shots * nf
    table = jnp.zeros((SUBS, LANES), jnp.float32)
    for k in range(srcs):
        table = jnp.where(lane_src == k, obs_refs[k][obs_rows:, :LANES], table)

    table = pick(table, lane_src * (shots * nfc) + lane_own)

    def row(k):
        return jnp.broadcast_to(table[k : k + 1, :], (SUBS, LANES))

    omega, coef, wave_re, wave_im = row(0), row(1), row(2), row(3)
    damp = 0.26 - jnp.sqrt(0.0625 - coef * coef)
    comp_f = lane % per
    comp_z = pair // per
    omega_c = pick(omega, (comp_f // nfc) * (shots * nfc) + (comp_f % nfc) * shots)

    def per_shot(ref, dtype):
        acc = jnp.zeros((SUBS, LANES), dtype)
        for s in range(shots):
            acc = jnp.where(lane_shot == s, ref[s], acc)
        return acc

    ray_l = per_shot(ray, f32)
    cell_l = per_shot(cell, jnp.int32)
    aper_l = per_shot(aper, jnp.int32)
    recv_l = per_shot(recv, jnp.int32)
    ntile = cells // LANES

    rows2 = 2 * depth
    for t in range(pl.cdiv(win, LANES)):
        cut = slice(t * LANES, (t + 1) * LANES)
        blk = [r[part, :, cut] for part in range(2) for r in sr_refs]
        blk = jnp.concatenate(blk + [jnp.zeros((LANES - rows2, LANES), f32)], axis=0)
        nat[t * LANES : (t + 1) * LANES, :] = blk.T

    def halves(j):
        return pl.ds(j, SUBS, stride=block), pl.ds(win // 2 + j, SUBS, stride=block)

    def cell_of(j):
        return x_start + (sub + jnp.where(upper, SUBS, 0)) * block + j

    def compact(zg, _):
        z = zg * zper + comp_z
        zrow = ((z // zloc) ^ dev) * zloc + z % zloc + jnp.where(upper, pairs, 0)
        for j in range(block):
            c, s = sincos(omega_c * pick(rows_s[j], zrow))
            cos_c[zg, j] = c
            sin_c[zg, j] = s
        for i in range(0, zper, 2):
            z0 = zg * zper + i
            chosen = [depth + ((z // zloc) ^ dev) * zloc + z % zloc for z in (z0, z0 + 1)]
            col = lax.broadcasted_iota(jnp.int32, (1, 2 * LANES), 1)
            at = jnp.where(col >= LANES, chosen[1], chosen[0]) + jnp.where(col % LANES >= pairs, pairs, 0)
            hot = jnp.where(lax.broadcasted_iota(jnp.int32, (LANES, 2 * LANES), 0) == at, 1.0, 0.0)
            hot = hot.astype(jnp.bfloat16)
            value = jnp.dot(rows_b[...], jnp.concatenate([hot, hot], axis=0), preferred_element_type=f32)
            for k in range(2):
                wgt[z0 + k] = value[:, k * LANES : (k + 1) * LANES].reshape(block, SUBS, LANES) * omega
        return 0

    for j in range(block):
        low, high = (nat[rows, :] for rows in halves(j))
        rows_s[j] = jnp.where(upper, pltpu.roll(high, pairs, 1), low)
    rows_b[...] = jnp.concatenate(split(rows_s[...].reshape(block * SUBS, LANES)), axis=1)
    lax.fori_loop(0, depth // zper, compact, 0)

    for j in range(block):
        x = cell_of(j)
        tile = jnp.where(x < 0, -1, x // LANES)
        inside = (tile >= aper_l) & (tile < aper_l + ntile // 2) & (tile < ntile)
        m = inside.astype(f32)
        mask_s[j] = m
        dist = (x - cell_l).astype(f32)
        c, s = sincos(omega * ray_l * dist)
        src_h[0, 0, j] = (wave_re * c - wave_im * s) * m
        src_h[0, 1, j] = (wave_re * s + wave_im * c) * m
        sct[0, j] = jnp.zeros((SUBS, LANES), f32)
        sct[1, j] = jnp.zeros((SUBS, LANES), f32)

    def up_sub(v):
        v = pltpu.roll(v, 1, 0)
        return jnp.where(sub == 0, pltpu.roll(v, pairs, 1), v)

    def down_sub(v):
        v = pltpu.roll(v, SUBS - 1, 0)
        return jnp.where(sub == SUBS - 1, pltpu.roll(v, pairs, 1), v)

    def forward(z, _):
        zg = z // zper
        idx = (z % zper) * per + lane_f + jnp.where(upper, pairs, 0)

        def born(j):
            w = wgt[z, j]
            sr, si = src_h[z, 0, j], src_h[z, 1, j]
            return sr, si, sct[0, j] - w * si, sct[1, j] + w * sr

        first = born(0)
        last = born(block - 1)
        before = [up_sub(v) for v in last]
        after = [down_sub(v) for v in first]
        now = first
        diff = [a - b for a, b in zip(now, before)]
        for j in range(block):
            nxt = after if j == block - 1 else (last if j == block - 2 else born(j + 1))
            step = [a - b for a, b in zip(nxt, now)]
            sec = [a - b for a, b in zip(step, diff)]
            m = mask_s[j]
            mc = m * pick(cos_c[zg, j], idx)
            ms = m * pick(sin_c[zg, j], idx)
            phase_s[z, 0, j] = mc
            phase_s[z, 1, j] = ms
            s_re = now[0] + (damp * sec[0] - coef * sec[1])
            s_im = now[1] + (damp * sec[1] + coef * sec[0])
            d_re = now[2] + (damp * sec[2] - coef * sec[3])
            d_im = now[3] + (damp * sec[3] + coef * sec[2])
            src_h[z + 1, 0, j] = s_re * mc - s_im * ms
            src_h[z + 1, 1, j] = s_re * ms + s_im * mc
            sct[0, j] = d_re * mc - d_im * ms
            sct[1, j] = d_re * ms + d_im * mc
            now, diff = nxt, step
        return 0

    lax.fori_loop(0, depth, forward, 0)

    pad = halo - edge
    obs_n[: pad + SUBS, :] = jnp.zeros((pad + SUBS, LANES), f32)
    obs_n[win - pad - SUBS : win, :] = jnp.zeros((pad + SUBS, LANES), f32)
    for t in range(pl.cdiv(own + 2 * edge, LANES)):
        rows_t = min(LANES, own + 2 * edge - t * LANES)
        blk = [
            r[pl.ds(pl.multiple_of(((core * nfc + f) * 2 + part) * shots, SUBS), shots), t * LANES : (t + 1) * LANES]
            for part in range(2)
            for r in obs_refs
            for f in range(nfc)
        ]
        obs_n[pad + t * LANES : pad + t * LANES + rows_t, :] = jnp.concatenate(blk, axis=0).T[:rows_t]
    for j in range(block):
        x = cell_of(j)
        tile = jnp.where(x < 0, -1, x // LANES)
        inside = (tile >= recv_l) & (tile < recv_l + max(1, ntile // 4)) & (tile < ntile)
        m = inside.astype(f32)
        low, high = (obs_n[rows, :] for rows in halves(j))
        turn = pltpu.roll(jnp.where(upper, low, high), pairs, 1)
        adj[0, j] = m * (sct[0, j] - jnp.where(upper, turn, low))
        adj[1, j] = m * (sct[1, j] - jnp.where(upper, high, turn))

    @pl.when(group == 0)
    def _():
        out_mine[...] = jnp.zeros(out_mine.shape, f32)
        out_other[...] = jnp.zeros(out_other.shape, f32)

    weight = omega * scale
    nrow = span // 2
    ncol = pl.cdiv(nrow, LANES) * LANES
    lead = halo - half
    rows_in = slice(lead // 2, lead // 2 + nrow)

    def products(z, odd):
        zi = z - z_first
        for j in range(block):
            for out, a, b in (
                (src_n, src_h[z, 0, j] * weight, src_h[z, 1, j] * -weight),
                (adj_n, adj[1, j], adj[0, j]),
            ):
                turn = pltpu.roll(jnp.where(upper, a, b), pairs, 1)
                low = jnp.where(upper, turn, a)
                high = jnp.where(upper, b, turn)
                out[j % 2, pl.ds(j // 2, SUBS, stride=block // 2), :] = low
                out[j % 2, pl.ds(win // 4 + j // 2, SUBS, stride=block // 2), :] = high
        for p in range(2):
            y = lax.broadcasted_iota(jnp.int32, (nrow, LANES), 0) * 2 + (x_start + lead + p)
            left = src_n[p, rows_in, :]
            right = jnp.where((y >= 0) & (y < cells), adj_n[p, rows_in, :], 0.0)
            if ncol > nrow:
                right = jnp.concatenate([right, jnp.zeros((ncol - nrow, LANES), f32)], axis=0)
            if odd:
                cuts = [right[i : i + pairs] for i in range(0, ncol, pairs)]
                right = jnp.concatenate([cuts[i ^ 1] for i in range(len(cuts))], axis=0)
            lh, ll = split(left)
            rh, rl = split(right)
            dims_t = (((1,), (1,)), ((), ()))
            dot = functools.partial(lax.dot_general, dimension_numbers=dims_t, preferred_element_type=f32)
            prod[zi, p] = dot(lh, rl) + dot(
                jnp.concatenate([lh, ll], axis=1), jnp.concatenate([rh, rh], axis=1)
            )

    slots = LANES // HOFF

    def extract(zg, slab_at, out_ref):
        for b in range(nrow // SUBS):
            for p in range(2):
                rows = slice(b * SUBS, (b + 1) * SUBS)
                first = b * SUBS - half
                near = ((lane - first) & (LANES - 1)) < pairs
                index = (lane % HOFF + sub + first + (lane // HOFF) * pairs) & (LANES - 1)

                def window(z, start):
                    at = max(first, 0)
                    v = prod[z, p, rows, at // LANES * LANES : (at // LANES + 1) * LANES]
                    end = min(b * SUBS + SUBS + half - 1, nrow)
                    if at // LANES < (end - 1) // LANES:
                        v2 = prod[z, p, rows, (at // LANES + 1) * LANES : (at // LANES + 2) * LANES]
                        v = jnp.where(((lane - start) & (LANES - 1)) < at % LANES - SUBS, v2, v)
                    return v

                acc = None
                for q in range(0, slots, 2):
                    z = slab_at + zg * slots + q
                    v = jnp.where(near, window(z, 0), window(z + 1, pairs))
                    v = pick(v, index)
                    acc = v if acc is None else jnp.where(lane >= q * HOFF, v, acc)
                skew[pl.ds(2 * b * SUBS + p, SUBS, stride=2), :] = acc
        tiles = pl.cdiv(span, LANES)
        turned = [skew[t * LANES : (t + 1) * LANES, :].T for t in range(tiles)]
        for q in range(slots):
            for hq in range(HOFF // SUBS):
                rows = slice(q * HOFF + hq * SUBS, q * HOFF + (hq + 1) * SUBS)
                for t in range(pl.cdiv(own, LANES)):
                    v = turned[t][rows]
                    if t + 1 < tiles:
                        v = jnp.where(lane < HOFF - hq * SUBS - sub, turned[t + 1][rows], v)
                    v = pltpu.roll(v, (hq * SUBS - HOFF) % LANES, 1, stride=1, stride_axis=0)
                    width = min(LANES, own - t * LANES)
                    out_ref[zg * slots + q, hq * SUBS : (hq + 1) * SUBS, t * LANES : t * LANES + width] += v[:, :width]

    def backward(k, _):
        z = depth - 1 - k

        def turn(j):
            mc, ms = phase_s[z, 0, j], phase_s[z, 1, j]
            ar, ai = adj[0, j], adj[1, j]
            return ar * mc + ai * ms, ai * mc - ar * ms

        first = turn(0)
        last = turn(block - 1)
        before = [up_sub(v) for v in last]
        after = [down_sub(v) for v in first]
        now = first
        diff = [a - b for a, b in zip(now, before)]
        for j in range(block):
            nxt = after if j == block - 1 else (last if j == block - 2 else turn(j + 1))
            step = [a - b for a, b in zip(nxt, now)]
            sec = [a - b for a, b in zip(step, diff)]
            adj[0, j] = now[0] + (damp * sec[0] + coef * sec[1])
            adj[1, j] = now[1] + (damp * sec[1] - coef * sec[0])
            now, diff = nxt, step

        return 0

    def backward_slab(k, i):
        backward(k, 0)
        products(depth - 1 - k, (i + 1) % 2)
        return 0

    ahead = depth - z_first - slab
    lax.fori_loop(0, ahead, backward, 0)

    def several(k, _):
        for i in range(UNROLL):
            backward_slab(ahead + UNROLL * k + i, i)
        return 0

    lax.fori_loop(0, slab // UNROLL, several, 0)

    @pl.loop(0, zloc // slots)
    def _(zg):
        extract(zg, core * zloc, out_mine)
        extract(zg, (1 - core) * zloc, out_other)


def local(
    slowness, reflect, omega, spread_coef, wavelet, ray_param, source_cell, aperture_tile, receiver_tile, observed,
):
    nd = lax.axis_size("depth")
    nq = lax.axis_size("freq")
    zloc, cells = slowness.shape
    depth = zloc * nd
    shots, nf, _, _ = observed.shape
    own = cells // nq
    halo = HOFF // 2 + 2 * depth
    win = own + 2 * halo
    block = win // (2 * SUBS)
    wide = pl.cdiv(win, LANES) * LANES
    per = LANES // (2 * shots)
    slot = shots * nf
    groups = nq * slot // LANES
    srcs = LANES // slot
    half = HOFF // 2
    edge = half + depth + half
    obsw = pl.cdiv(own + 2 * edge, LANES) * LANES
    direct = groups == 1 and nq == 8
    smem = pl.BlockSpec(memory_space=pltpu.SMEM)
    rows = 2 * slot + SUBS

    fetch = ((7, 4, 3, 0), (6, 5, 2, 1))
    if direct:
        count = nq // 2
        peers = lambda c, d, k: c ^ jnp.where(d % 2 == 0, fetch[0][k], fetch[1][k])
    else:
        count = nq
        peers = lambda c, d, k: k

    packed = pl.pallas_call(
        functools.partial(
            pack,
            dims=(shots, nf, depth, zloc, cells, own, halo, edge, wide, obsw),
            peers=peers,
        ),
        in_specs=[smem] * 3 + [pl.BlockSpec(memory_space=pltpu.VMEM)] * 3,
        out_shape=[jax.ShapeDtypeStruct((2, zloc, wide), jnp.float32)]
        + [jax.ShapeDtypeStruct((1, rows, obsw), jnp.float32)] * count,
    )(omega, spread_coef, wavelet, slowness, reflect, observed)
    both, parts = {0: packed[0]}, packed[1:]

    def swap(value, bit):
        return lax.ppermute(value, "depth", [(i, i ^ bit) for i in range(nd)])

    bit = nd // 2
    while bit > 1:
        both.update({k ^ bit: swap(v, bit) for k, v in list(both.items())})
        bit //= 2
    if direct:
        parts = [
            lax.ppermute(
                part,
                ("depth", "freq"),
                [(d * nq + i, d * nq + (i ^ fetch[d % 2][k])) for d in range(nd) for i in range(nq)],
            )
            for k, part in enumerate(parts)
        ]
        parts = parts + [swap(part, 1) for part in parts]
    else:
        parts = lax.all_to_all(jnp.stack(parts), "freq", 0, 0).reshape(groups, srcs, rows, obsw)
        parts = [parts[:, k] for k in range(srcs)]
    both.update({k ^ 1: swap(v, 1) for k, v in list(both.items())})
    both = [both[k] for k in range(nd)]

    dims = (shots, nf, depth, zloc, cells, own, halo, edge, block, 1.0 / math.sqrt(shots * nf * nq))
    natr = wide
    grid_spec = pltpu.PrefetchScalarGridSpec(
        num_scalar_prefetch=0,
        grid=(groups,),
        in_specs=[
            smem, smem, smem, smem,
        ]
        + [pl.BlockSpec((2, zloc, wide), lambda g: (0, 0, 0))] * nd
        + [pl.BlockSpec((None, rows, obsw), lambda g: (g, 0, 0))] * srcs,
        out_specs=[pl.BlockSpec((zloc, HOFF, own), lambda g: (0, 0, 0))] * 2,
        scratch_shapes=[
            pltpu.VMEM((natr, LANES), jnp.float32),
            pltpu.VMEM((block, SUBS, LANES), jnp.float32),
            pltpu.VMEM((block * SUBS, 2 * LANES), jnp.bfloat16),
            pltpu.VMEM((2 * depth * per // LANES, block, SUBS, LANES), jnp.float32),
            pltpu.VMEM((2 * depth * per // LANES, block, SUBS, LANES), jnp.float32),
            pltpu.VMEM((depth, block, SUBS, LANES), jnp.float32),
            pltpu.VMEM((block, SUBS, LANES), jnp.float32),
            pltpu.VMEM((depth, 2, block, SUBS, LANES), jnp.float32),
            pltpu.VMEM((depth + 1, 2, block, SUBS, LANES), jnp.float32),
            pltpu.VMEM((2, block, SUBS, LANES), jnp.float32),
            pltpu.VMEM((2, block, SUBS, LANES), jnp.float32),
            pltpu.VMEM((natr, LANES), jnp.float32),
            pltpu.VMEM((2, win // 2, LANES), jnp.float32),
            pltpu.VMEM((2, win // 2, LANES), jnp.float32),
            pltpu.VMEM((2 * zloc, 2, (own + HOFF) // 2, pl.cdiv((own + HOFF) // 2, LANES) * LANES), jnp.float32),
            pltpu.VMEM((pl.cdiv(own + HOFF, LANES) * LANES, LANES), jnp.float32),
        ],
    )
    mine, other = pl.pallas_call(
        functools.partial(migrate, dims=dims, srcs=srcs, zsrc=nd),
        out_shape=[jax.ShapeDtypeStruct((zloc, HOFF, own), jnp.float32)] * 2,
        grid_spec=grid_spec,
        compiler_params=pltpu.CompilerParams(vmem_limit_bytes=36 << 20),
    )(ray_param, source_cell, aperture_tile, receiver_tile, *both, *parts)
    return mine + swap(other, 1)


def solution(mesh):
    return jax.shard_map(
        local,
        mesh=mesh,
        in_specs=(
            P("depth", None), P("depth", None), P("freq"), P("freq"), P("freq", None),
            P(), P(), P(), P(), P(None, "freq", None, None),
        ),
        out_specs=P("depth", None, "freq"),
        check_vma=False,
    )
```

```python
import functools
import math

import jax
import jax.numpy as jnp
from jax import lax
from jax.experimental import pallas as pl
from jax.experimental.pallas import tpu as pltpu
from jax.sharding import PartitionSpec as P

HOFF = 32
LANES = 128
SUBS = 8
UNROLL = 16


def sincos(angle):
    turns = jnp.floor(angle * 0.6366197723675814 + 0.5)
    rem = angle - turns * 1.5703125
    rem = rem - turns * 4.837512969970703125e-4
    rem = rem - turns * 7.54978995489188216e-8
    sq = rem * rem
    sin_p = rem + rem * sq * (-1.6666654611e-1 + sq * (8.3321608736e-3 + sq * -1.9515295891e-4))
    cos_p = (1.0 - 0.5 * sq) + sq * sq * (
        4.166664568298827e-2 + sq * (-1.388731625493765e-3 + sq * 2.443315711809948e-5)
    )
    quad = turns.astype(jnp.int32)
    odd = (quad & 1) == 1
    sine = jnp.where(odd, cos_p, sin_p)
    cosine = jnp.where(odd, sin_p, cos_p)
    sine = jnp.where((quad & 2) == 2, -sine, sine)
    cosine = jnp.where(((quad + 1) & 2) == 2, -cosine, cosine)
    return cosine, sine


def pick(values, index):
    return jnp.take_along_axis(values, index, axis=1, mode="promise_in_bounds")


def split(values):
    high = values.astype(jnp.bfloat16)
    low = (values - high.astype(jnp.float32)).astype(jnp.bfloat16)
    return high, low


def cut_out(load, first, width, cells):
    tiles = pl.cdiv(width, LANES) + 1
    low = first + cells * LANES
    base = low // LANES - cells
    off = low % LANES
    cut = [
        load(pl.ds(pl.multiple_of(jnp.clip(base + t, 0, cells // LANES - 1) * LANES, LANES), LANES))
        for t in range(tiles)
    ]
    full = jnp.concatenate(cut, axis=1)
    return pltpu.roll(full, (tiles * LANES - off) % (tiles * LANES), 1)[:, :width]


def pack(omega, coef, wave, slow_ref, refl_ref, obs_ref, both_ref, *outs, dims, peers):
    shots, nf, depth, zloc, cells, own, halo, edge, wide, obsw = dims
    col = lax.axis_index("freq")
    dev = lax.axis_index("depth")

    first = col * own - halo
    both_ref[0] = cut_out(lambda c: slow_ref[:, c], first, wide, cells)
    both_ref[1] = cut_out(lambda c: refl_ref[:, c], first, wide, cells)
    lane = lax.broadcasted_iota(jnp.int32, (1, obsw), 1) % nf

    def spread(read):
        acc = jnp.zeros((1, obsw), jnp.float32)
        for f in range(nf):
            acc = jnp.where(lane == f, read(f), acc)
        return acc

    table = jnp.concatenate(
        [
            spread(lambda f: omega[f]),
            spread(lambda f: coef[f]),
            spread(lambda f: wave[f, 0]),
            spread(lambda f: wave[f, 1]),
            jnp.zeros((4, obsw), jnp.float32),
        ],
        axis=0,
    )
    def observed_rows(c):
        return jnp.concatenate([obs_ref[:, f, part, c] for f in range(nf) for part in range(2)], axis=0)

    for k, out in enumerate(outs):
        dest = peers(col, dev, k)
        out[0, : 2 * shots * nf] = cut_out(observed_rows, dest * own - edge, obsw, cells)
        out[0, 2 * shots * nf :] = table


def migrate(
    ray, cell, aper, recv, slow, refl, *refs, dims, srcs, zsrc,
):
    sr_refs, (out_mine, out_other, nat, rows_s, rows_b, cos_c, sin_c, wgt, mask_s, phase_s, src_h, sct, adj, obs_n, src_n, adj_n, prod, skew) = refs[: zsrc + srcs], refs[zsrc + srcs :]
    sr_refs, obs_refs = sr_refs[:zsrc], sr_refs[zsrc:]
    shots, nf, depth, zloc, cells, own, halo, edge, block, scale = dims
    half = HOFF // 2
    win = own + 2 * halo
    pairs = LANES // 2
    nfc = nf // 2
    per = pairs // shots
    zper = pairs // per
    span = own + HOFF
    f32 = jnp.float32
    group = pl.program_id(0)
    x_start = lax.axis_index("freq") * own - halo
    dev = lax.axis_index("depth")
    core = dev % 2
    z_first = (dev - core) * zloc
    slab = 2 * zloc

    lane = lax.broadcasted_iota(jnp.int32, (SUBS, LANES), 1)
    sub = lax.broadcasted_iota(jnp.int32, (SUBS, LANES), 0)
    upper = lane >= pairs
    pair = lane % pairs
    lane_src = pair // (shots * nfc)
    lane_shot = pair % shots
    lane_f2 = (pair // shots) % nfc
    lane_f = lane_src * nfc + lane_f2
    lane_own = core * nfc + lane_f2

    obs_rows = 2 * shots * nf
    table = jnp.zeros((SUBS, LANES), jnp.float32)
    for k in range(srcs):
        table = jnp.where(lane_src == k, obs_refs[k][obs_rows:, :LANES], table)

    table = pick(table, lane_src * (shots * nfc) + lane_own)

    def row(k):
        return jnp.broadcast_to(table[k : k + 1, :], (SUBS, LANES))

    omega, coef, wave_re, wave_im = row(0), row(1), row(2), row(3)
    damp = 0.26 - jnp.sqrt(0.0625 - coef * coef)
    comp_f = lane % per
    comp_z = pair // per
    first_lane = (comp_f // nfc) * (shots * nfc) + (comp_f % nfc) * shots
    omega_c, damp_c, coef_c = (pick(v, first_lane) for v in (omega, damp, coef))
    norm = damp * damp + coef * coef
    g_re, g_im = damp / norm - 2.0, -coef / norm

    def per_shot(ref, dtype):
        acc = jnp.zeros((SUBS, LANES), dtype)
        for s in range(shots):
            acc = jnp.where(lane_shot == s, ref[s], acc)
        return acc

    ray_l = per_shot(ray, f32)
    cell_l = per_shot(cell, jnp.int32)
    aper_l = per_shot(aper, jnp.int32)
    recv_l = per_shot(recv, jnp.int32)
    ntile = cells // LANES

    rows2 = 2 * depth
    wide = pl.cdiv(win, LANES) * LANES
    mine = [cut_out(lambda c: ref[:, c], x_start, wide, cells) for ref in (slow, refl)]
    for t in range(pl.cdiv(win, LANES)):
        cut = slice(t * LANES, (t + 1) * LANES)
        blk = sum(([mine[part][:, cut]] + [r[part, :, cut] for r in sr_refs] for part in range(2)), [])
        blk = jnp.concatenate(blk + [jnp.zeros((LANES - rows2, LANES), f32)], axis=0)
        nat[t * LANES : (t + 1) * LANES, :] = blk.T

    def halves(j):
        return pl.ds(j, SUBS, stride=block), pl.ds(win // 2 + j, SUBS, stride=block)

    def cell_of(j):
        return x_start + (sub + jnp.where(upper, SUBS, 0)) * block + j

    def compact(zg, _):
        z = zg * zper + comp_z
        zrow = ((z // zloc) ^ dev) * zloc + z % zloc + jnp.where(upper, pairs, 0)
        for j in range(block):
            c, s = sincos(omega_c * pick(rows_s[j], zrow))
            cos_c[zg, j] = c * damp_c - s * coef_c
            sin_c[zg, j] = c * coef_c + s * damp_c
        for i in range(0, zper, 2):
            z0 = zg * zper + i
            chosen = [depth + ((z // zloc) ^ dev) * zloc + z % zloc for z in (z0, z0 + 1)]
            col = lax.broadcasted_iota(jnp.int32, (1, 2 * LANES), 1)
            at = jnp.where(col >= LANES, chosen[1], chosen[0]) + jnp.where(col % LANES >= pairs, pairs, 0)
            hot = jnp.where(lax.broadcasted_iota(jnp.int32, (LANES, 2 * LANES), 0) == at, 1.0, 0.0)
            hot = hot.astype(jnp.bfloat16)
            value = jnp.dot(rows_b[...], jnp.concatenate([hot, hot], axis=0), preferred_element_type=f32)
            for k in range(2):
                wgt[z0 + k] = value[:, k * LANES : (k + 1) * LANES].reshape(block, SUBS, LANES) * omega
        return 0

    for j in range(block):
        low, high = (nat[rows, :] for rows in halves(j))
        rows_s[j] = jnp.where(upper, pltpu.roll(high, pairs, 1), low)
    rows_b[...] = jnp.concatenate(split(rows_s[...].reshape(block * SUBS, LANES)), axis=1)
    lax.fori_loop(0, depth // zper, compact, 0)

    for j in range(block):
        x = cell_of(j)
        tile = jnp.where(x < 0, -1, x // LANES)
        inside = (tile >= aper_l) & (tile < aper_l + ntile // 2) & (tile < ntile)
        m = inside.astype(f32)
        mask_s[j] = m
        dist = (x - cell_l).astype(f32)
        c, s = sincos(omega * ray_l * dist)
        src_h[0, 0, j] = (wave_re * c - wave_im * s) * m
        src_h[0, 1, j] = (wave_re * s + wave_im * c) * m
        sct[0, j] = jnp.zeros((SUBS, LANES), f32)
        sct[1, j] = jnp.zeros((SUBS, LANES), f32)

    def up_sub(v):
        v = pltpu.roll(v, 1, 0)
        return jnp.where(sub == 0, pltpu.roll(v, pairs, 1), v)

    def down_sub(v):
        v = pltpu.roll(v, SUBS - 1, 0)
        return jnp.where(sub == SUBS - 1, pltpu.roll(v, pairs, 1), v)

    def forward(z, _):
        zg = z // zper
        idx = (z % zper) * per + lane_f + jnp.where(upper, pairs, 0)

        def born(j):
            w = wgt[z, j]
            sr, si = src_h[z, 0, j], src_h[z, 1, j]
            return sr, si, sct[0, j] - w * si, sct[1, j] + w * sr

        first = born(0)
        last = born(block - 1)
        before = [up_sub(v) for v in last]
        after = [down_sub(v) for v in first]
        now = first
        for j in range(block):
            nxt = after if j == block - 1 else (last if j == block - 2 else born(j + 1))
            both = [a + b for a, b in zip(nxt, before)]
            m = mask_s[j]
            mc = m * pick(cos_c[zg, j], idx)
            ms = m * pick(sin_c[zg, j], idx)
            phase_s[z, 0, j] = mc
            phase_s[z, 1, j] = ms
            s_re = (g_re * now[0] - g_im * now[1]) + both[0]
            s_im = (g_re * now[1] + g_im * now[0]) + both[1]
            d_re = (g_re * now[2] - g_im * now[3]) + both[2]
            d_im = (g_re * now[3] + g_im * now[2]) + both[3]
            src_h[z + 1, 0, j] = s_re * mc - s_im * ms
            src_h[z + 1, 1, j] = s_re * ms + s_im * mc
            sct[0, j] = d_re * mc - d_im * ms
            sct[1, j] = d_re * ms + d_im * mc
            before, now = now, nxt
        return 0

    lax.fori_loop(0, depth, forward, 0)

    pad = halo - edge
    obs_n[: pad + SUBS, :] = jnp.zeros((pad + SUBS, LANES), f32)
    obs_n[win - pad - SUBS : win, :] = jnp.zeros((pad + SUBS, LANES), f32)
    for t in range(pl.cdiv(own + 2 * edge, LANES)):
        rows_t = min(LANES, own + 2 * edge - t * LANES)
        blk = [
            r[pl.ds(pl.multiple_of(((core * nfc + f) * 2 + part) * shots, SUBS), shots), t * LANES : (t + 1) * LANES]
            for part in range(2)
            for r in obs_refs
            for f in range(nfc)
        ]
        obs_n[pad + t * LANES : pad + t * LANES + rows_t, :] = jnp.concatenate(blk, axis=0).T[:rows_t]
    for j in range(block):
        x = cell_of(j)
        tile = jnp.where(x < 0, -1, x // LANES)
        inside = (tile >= recv_l) & (tile < recv_l + max(1, ntile // 4)) & (tile < ntile)
        m = inside.astype(f32)
        low, high = (obs_n[rows, :] for rows in halves(j))
        turn = pltpu.roll(jnp.where(upper, low, high), pairs, 1)
        adj[0, j] = m * (sct[0, j] - jnp.where(upper, turn, low))
        adj[1, j] = m * (sct[1, j] - jnp.where(upper, high, turn))

    @pl.when(group == 0)
    def _():
        out_mine[...] = jnp.zeros(out_mine.shape, f32)
        out_other[...] = jnp.zeros(out_other.shape, f32)

    weight = omega * scale
    nrow = span // 2
    ncol = pl.cdiv(nrow, LANES) * LANES
    lead = halo - half
    rows_in = slice(lead // 2, lead // 2 + nrow)

    def products(z, odd):
        zi = z - z_first
        for j in range(block):
            for out, a, b in (
                (src_n, src_h[z, 0, j] * weight, src_h[z, 1, j] * -weight),
                (adj_n, adj[1, j], adj[0, j]),
            ):
                turn = pltpu.roll(jnp.where(upper, a, b), pairs, 1)
                low = jnp.where(upper, turn, a)
                high = jnp.where(upper, b, turn)
                out[j % 2, pl.ds(j // 2, SUBS, stride=block // 2), :] = low
                out[j % 2, pl.ds(win // 4 + j // 2, SUBS, stride=block // 2), :] = high
        for p in range(2):
            y = lax.broadcasted_iota(jnp.int32, (nrow, LANES), 0) * 2 + (x_start + lead + p)
            left = src_n[p, rows_in, :]
            right = jnp.where((y >= 0) & (y < cells), adj_n[p, rows_in, :], 0.0)
            if ncol > nrow:
                right = jnp.concatenate([right, jnp.zeros((ncol - nrow, LANES), f32)], axis=0)
            if odd:
                cuts = [right[i : i + pairs] for i in range(0, ncol, pairs)]
                right = jnp.concatenate([cuts[i ^ 1] for i in range(len(cuts))], axis=0)
            lh, ll = split(left)
            rh, rl = split(right)
            dims_t = (((1,), (1,)), ((), ()))
            dot = functools.partial(lax.dot_general, dimension_numbers=dims_t, preferred_element_type=f32)
            prod[zi, p] = dot(lh, rl) + dot(
                jnp.concatenate([lh, ll], axis=1), jnp.concatenate([rh, rh], axis=1)
            )

    slots = LANES // HOFF

    def extract(zg, slab_at, out_ref):
        for b in range(nrow // SUBS):
            for p in range(2):
                rows = slice(b * SUBS, (b + 1) * SUBS)
                first = b * SUBS - half
                near = ((lane - first) & (LANES - 1)) < pairs
                index = (lane % HOFF + sub + first + (lane // HOFF) * pairs) & (LANES - 1)

                def window(z, start):
                    at = max(first, 0)
                    v = prod[z, p, rows, at // LANES * LANES : (at // LANES + 1) * LANES]
                    end = min(b * SUBS + SUBS + half - 1, nrow)
                    if at // LANES < (end - 1) // LANES:
                        v2 = prod[z, p, rows, (at // LANES + 1) * LANES : (at // LANES + 2) * LANES]
                        v = jnp.where(((lane - start) & (LANES - 1)) < at % LANES - SUBS, v2, v)
                    return v

                acc = None
                for q in range(0, slots, 2):
                    z = slab_at + zg * slots + q
                    v = jnp.where(near, window(z, 0), window(z + 1, pairs))
                    v = pick(v, index)
                    acc = v if acc is None else jnp.where(lane >= q * HOFF, v, acc)
                skew[pl.ds(2 * b * SUBS + p, SUBS, stride=2), :] = acc
        tiles = pl.cdiv(span, LANES)
        turned = [skew[t * LANES : (t + 1) * LANES, :].T for t in range(tiles)]
        for q in range(slots):
            for hq in range(HOFF // SUBS):
                rows = slice(q * HOFF + hq * SUBS, q * HOFF + (hq + 1) * SUBS)
                for t in range(pl.cdiv(own, LANES)):
                    v = turned[t][rows]
                    if t + 1 < tiles:
                        v = jnp.where(lane < HOFF - hq * SUBS - sub, turned[t + 1][rows], v)
                    v = pltpu.roll(v, (hq * SUBS - HOFF) % LANES, 1, stride=1, stride_axis=0)
                    width = min(LANES, own - t * LANES)
                    out_ref[zg * slots + q, hq * SUBS : (hq + 1) * SUBS, t * LANES : t * LANES + width] += v[:, :width]

    def backward(k, _):
        z = depth - 1 - k

        def turn(j):
            mc, ms = phase_s[z, 0, j], phase_s[z, 1, j]
            ar, ai = adj[0, j], adj[1, j]
            return ar * mc + ai * ms, ai * mc - ar * ms

        first = turn(0)
        last = turn(block - 1)
        before = [up_sub(v) for v in last]
        after = [down_sub(v) for v in first]
        now = first
        for j in range(block):
            nxt = after if j == block - 1 else (last if j == block - 2 else turn(j + 1))
            adj[0, j] = (g_re * now[0] + g_im * now[1]) + (nxt[0] + before[0])
            adj[1, j] = (g_re * now[1] - g_im * now[0]) + (nxt[1] + before[1])
            before, now = now, nxt

        return 0

    def backward_slab(k, i):
        backward(k, 0)
        products(depth - 1 - k, (i + 1) % 2)
        return 0

    ahead = depth - z_first - slab
    lax.fori_loop(0, ahead, backward, 0)

    def several(k, _):
        for i in range(UNROLL):
            backward_slab(ahead + UNROLL * k + i, i)
        return 0

    lax.fori_loop(0, slab // UNROLL, several, 0)

    @pl.loop(0, zloc // slots)
    def _(zg):
        extract(zg, core * zloc, out_mine)
        extract(zg, (1 - core) * zloc, out_other)


def local(
    slowness, reflect, omega, spread_coef, wavelet, ray_param, source_cell, aperture_tile, receiver_tile, observed,
):
    nd = lax.axis_size("depth")
    nq = lax.axis_size("freq")
    zloc, cells = slowness.shape
    depth = zloc * nd
    shots, nf, _, _ = observed.shape
    own = cells // nq
    halo = HOFF // 2 + 2 * depth
    win = own + 2 * halo
    block = win // (2 * SUBS)
    wide = pl.cdiv(win, LANES) * LANES
    per = LANES // (2 * shots)
    slot = shots * nf
    groups = nq * slot // LANES
    srcs = LANES // slot
    half = HOFF // 2
    edge = half + depth + half
    obsw = pl.cdiv(own + 2 * edge, LANES) * LANES
    direct = groups == 1 and nq == 8
    smem = pl.BlockSpec(memory_space=pltpu.SMEM)
    rows = 2 * slot + SUBS

    fetch = ((7, 4, 3, 0), (6, 5, 2, 1))
    if direct:
        count = nq // 2
        peers = lambda c, d, k: c ^ jnp.where(d % 2 == 0, fetch[0][k], fetch[1][k])
    else:
        count = nq
        peers = lambda c, d, k: k

    packed = pl.pallas_call(
        functools.partial(
            pack,
            dims=(shots, nf, depth, zloc, cells, own, halo, edge, wide, obsw),
            peers=peers,
        ),
        in_specs=[smem] * 3 + [pl.BlockSpec(memory_space=pltpu.VMEM)] * 3,
        out_shape=[jax.ShapeDtypeStruct((2, zloc, wide), jnp.float32)]
        + [jax.ShapeDtypeStruct((1, rows, obsw), jnp.float32)] * count,
    )(omega, spread_coef, wavelet, slowness, reflect, observed)
    both, parts = {0: packed[0]}, packed[1:]

    def swap(value, bit):
        return lax.ppermute(value, "depth", [(i, i ^ bit) for i in range(nd)])

    bit = nd // 2
    while bit > 1:
        both.update({k ^ bit: swap(v, bit) for k, v in list(both.items())})
        bit //= 2
    if direct:
        parts = [
            lax.ppermute(
                part,
                ("depth", "freq"),
                [(d * nq + i, d * nq + (i ^ fetch[d % 2][k])) for d in range(nd) for i in range(nq)],
            )
            for k, part in enumerate(parts)
        ]
        parts = parts + [swap(part, 1) for part in parts]
    else:
        parts = lax.all_to_all(jnp.stack(parts), "freq", 0, 0).reshape(groups, srcs, rows, obsw)
        parts = [parts[:, k] for k in range(srcs)]
    both.update({k ^ 1: swap(v, 1) for k, v in list(both.items())})
    both = [both[k] for k in range(1, nd)]

    dims = (shots, nf, depth, zloc, cells, own, halo, edge, block, 1.0 / math.sqrt(shots * nf * nq))
    natr = wide
    grid_spec = pltpu.PrefetchScalarGridSpec(
        num_scalar_prefetch=0,
        grid=(groups,),
        in_specs=[
            smem, smem, smem, smem,
        ]
        + [pl.BlockSpec((zloc, cells), lambda g: (0, 0))] * 2
        + [pl.BlockSpec((2, zloc, wide), lambda g: (0, 0, 0))] * (nd - 1)
        + [pl.BlockSpec((None, rows, obsw), lambda g: (g, 0, 0))] * srcs,
        out_specs=[pl.BlockSpec((zloc, HOFF, own), lambda g: (0, 0, 0))] * 2,
        scratch_shapes=[
            pltpu.VMEM((natr, LANES), jnp.float32),
            pltpu.VMEM((block, SUBS, LANES), jnp.float32),
            pltpu.VMEM((block * SUBS, 2 * LANES), jnp.bfloat16),
            pltpu.VMEM((2 * depth * per // LANES, block, SUBS, LANES), jnp.float32),
            pltpu.VMEM((2 * depth * per // LANES, block, SUBS, LANES), jnp.float32),
            pltpu.VMEM((depth, block, SUBS, LANES), jnp.float32),
            pltpu.VMEM((block, SUBS, LANES), jnp.float32),
            pltpu.VMEM((depth, 2, block, SUBS, LANES), jnp.float32),
            pltpu.VMEM((depth + 1, 2, block, SUBS, LANES), jnp.float32),
            pltpu.VMEM((2, block, SUBS, LANES), jnp.float32),
            pltpu.VMEM((2, block, SUBS, LANES), jnp.float32),
            pltpu.VMEM((natr, LANES), jnp.float32),
            pltpu.VMEM((2, win // 2, LANES), jnp.float32),
            pltpu.VMEM((2, win // 2, LANES), jnp.float32),
            pltpu.VMEM((2 * zloc, 2, (own + HOFF) // 2, pl.cdiv((own + HOFF) // 2, LANES) * LANES), jnp.float32),
            pltpu.VMEM((pl.cdiv(own + HOFF, LANES) * LANES, LANES), jnp.float32),
        ],
    )
    mine, other = pl.pallas_call(
        functools.partial(migrate, dims=dims, srcs=srcs, zsrc=nd - 1),
        out_shape=[jax.ShapeDtypeStruct((zloc, HOFF, own), jnp.float32)] * 2,
        grid_spec=grid_spec,
        compiler_params=pltpu.CompilerParams(vmem_limit_bytes=36 << 20),
    )(ray_param, source_cell, aperture_tile, receiver_tile, slowness, reflect, *both, *parts)
    return mine + swap(other, 1)


def solution(mesh):
    return jax.shard_map(
        local,
        mesh=mesh,
        in_specs=(
            P("depth", None), P("depth", None), P("freq"), P("freq"), P("freq", None),
            P(), P(), P(), P(), P(None, "freq", None, None),
        ),
        out_specs=P("depth", None, "freq"),
        check_vma=False,
    )
```

```python
import functools
import math

import jax
import jax.numpy as jnp
from jax import lax
from jax.experimental import pallas as pl
from jax.experimental.pallas import tpu as pltpu
from jax.sharding import PartitionSpec as P

HOFF = 32
LANES = 128
SUBS = 8
UNROLL = 16


def sincos(angle):
    turns = jnp.floor(angle * 0.6366197723675814 + 0.5)
    rem = angle - turns * 1.5703125
    rem = rem - turns * 4.837512969970703125e-4
    rem = rem - turns * 7.54978995489188216e-8
    sq = rem * rem
    sin_p = rem + rem * sq * (-1.6666654611e-1 + sq * (8.3321608736e-3 + sq * -1.9515295891e-4))
    cos_p = (1.0 - 0.5 * sq) + sq * sq * (
        4.166664568298827e-2 + sq * (-1.388731625493765e-3 + sq * 2.443315711809948e-5)
    )
    quad = turns.astype(jnp.int32)
    odd = (quad & 1) == 1
    sine = jnp.where(odd, cos_p, sin_p)
    cosine = jnp.where(odd, sin_p, cos_p)
    sine = jnp.where((quad & 2) == 2, -sine, sine)
    cosine = jnp.where(((quad + 1) & 2) == 2, -cosine, cosine)
    return cosine, sine


def pick(values, index):
    return jnp.take_along_axis(values, index, axis=1, mode="promise_in_bounds")


def split(values):
    high = values.astype(jnp.bfloat16)
    low = (values - high.astype(jnp.float32)).astype(jnp.bfloat16)
    return high, low


def cut_out(load, first, width, cells):
    tiles = pl.cdiv(width, LANES) + 1
    low = first + cells * LANES
    base = low // LANES - cells
    off = low % LANES
    cut = [
        load(pl.ds(pl.multiple_of(jnp.clip(base + t, 0, cells // LANES - 1) * LANES, LANES), LANES))
        for t in range(tiles)
    ]
    full = jnp.concatenate(cut, axis=1)
    return pltpu.roll(full, (tiles * LANES - off) % (tiles * LANES), 1)[:, :width]


def pack(omega, coef, wave, slow_ref, refl_ref, obs_ref, both_ref, *outs, dims, peers):
    shots, nf, depth, zloc, cells, own, halo, edge, wide, obsw = dims
    col = lax.axis_index("freq")
    dev = lax.axis_index("depth")

    first = col * own - halo
    both_ref[0] = cut_out(lambda c: slow_ref[:, c], first, wide, cells)
    both_ref[1] = cut_out(lambda c: refl_ref[:, c], first, wide, cells)
    lane = lax.broadcasted_iota(jnp.int32, (1, obsw), 1) % nf

    def spread(read):
        acc = jnp.zeros((1, obsw), jnp.float32)
        for f in range(nf):
            acc = jnp.where(lane == f, read(f), acc)
        return acc

    table = jnp.concatenate(
        [
            spread(lambda f: omega[f]),
            spread(lambda f: coef[f]),
            spread(lambda f: wave[f, 0]),
            spread(lambda f: wave[f, 1]),
            jnp.zeros((4, obsw), jnp.float32),
        ],
        axis=0,
    )
    def observed_rows(c):
        return jnp.concatenate([obs_ref[:, f, part, c] for f in range(nf) for part in range(2)], axis=0)

    for k, out in enumerate(outs):
        dest = peers(col, dev, k)
        out[0, : 2 * shots * nf] = cut_out(observed_rows, dest * own - edge, obsw, cells)
        out[0, 2 * shots * nf :] = table


def migrate(
    ray, cell, aper, recv, slow, refl, *refs, dims, srcs, zsrc,
):
    sr_refs, (out_mine, out_other, nat, rows_s, rows_b, cos_c, sin_c, wgt, mask_s, phase_s, src_h, sct, adj, obs_n, src_n, adj_n, prod, skew) = refs[: zsrc + srcs], refs[zsrc + srcs :]
    sr_refs, obs_refs = sr_refs[:zsrc], sr_refs[zsrc:]
    shots, nf, depth, zloc, cells, own, halo, edge, block, scale = dims
    half = HOFF // 2
    win = own + 2 * halo
    pairs = LANES // 2
    nfc = nf // 2
    per = pairs // shots
    zper = pairs // per
    span = own + HOFF
    f32 = jnp.float32
    group = pl.program_id(0)
    x_start = lax.axis_index("freq") * own - halo
    dev = lax.axis_index("depth")
    core = dev % 2
    z_first = (dev - core) * zloc
    slab = 2 * zloc

    lane = lax.broadcasted_iota(jnp.int32, (SUBS, LANES), 1)
    sub = lax.broadcasted_iota(jnp.int32, (SUBS, LANES), 0)
    upper = lane >= pairs
    pair = lane % pairs
    lane_src = pair // (shots * nfc)
    lane_shot = pair % shots
    lane_f2 = (pair // shots) % nfc
    lane_f = lane_src * nfc + lane_f2
    lane_own = core * nfc + lane_f2

    obs_rows = 2 * shots * nf
    table = jnp.zeros((SUBS, LANES), jnp.float32)
    for k in range(srcs):
        table = jnp.where(lane_src == k, obs_refs[k][obs_rows:, :LANES], table)

    table = pick(table, lane_src * (shots * nfc) + lane_own)

    def row(k):
        return jnp.broadcast_to(table[k : k + 1, :], (SUBS, LANES))

    omega, coef, wave_re, wave_im = row(0), row(1), row(2), row(3)
    damp = 0.26 - jnp.sqrt(0.0625 - coef * coef)
    comp_f = lane % per
    comp_z = pair // per
    first_lane = (comp_f // nfc) * (shots * nfc) + (comp_f % nfc) * shots
    omega_c, damp_c, coef_c = (pick(v, first_lane) for v in (omega, damp, coef))
    norm = damp * damp + coef * coef
    g_re, g_im = damp / norm - 2.0, -coef / norm

    def per_shot(ref, dtype):
        acc = jnp.zeros((SUBS, LANES), dtype)
        for s in range(shots):
            acc = jnp.where(lane_shot == s, ref[s], acc)
        return acc

    ray_l = per_shot(ray, f32)
    cell_l = per_shot(cell, jnp.int32)
    aper_l = per_shot(aper, jnp.int32)
    recv_l = per_shot(recv, jnp.int32)
    ntile = cells // LANES

    rows2 = 2 * depth
    wide = pl.cdiv(win, LANES) * LANES
    mine = [cut_out(lambda c: ref[:, c], x_start, wide, cells) for ref in (slow, refl)]
    for t in range(pl.cdiv(win, LANES)):
        cut = slice(t * LANES, (t + 1) * LANES)
        blk = sum(([mine[part][:, cut]] + [r[part, :, cut] for r in sr_refs] for part in range(2)), [])
        blk = jnp.concatenate(blk + [jnp.zeros((LANES - rows2, LANES), f32)], axis=0)
        nat[t * LANES : (t + 1) * LANES, :] = blk.T

    def halves(j):
        return pl.ds(j, SUBS, stride=block), pl.ds(win // 2 + j, SUBS, stride=block)

    def cell_of(j):
        return x_start + (sub + jnp.where(upper, SUBS, 0)) * block + j

    def compact(zg, _):
        z = zg * zper + comp_z
        zrow = ((z // zloc) ^ dev) * zloc + z % zloc + jnp.where(upper, pairs, 0)
        for j in range(block):
            c, s = sincos(omega_c * pick(rows_s[j], zrow))
            cos_c[zg, j] = c * damp_c - s * coef_c
            sin_c[zg, j] = c * coef_c + s * damp_c
        for i in range(0, zper, 2):
            z0 = zg * zper + i
            chosen = [depth + ((z // zloc) ^ dev) * zloc + z % zloc for z in (z0, z0 + 1)]
            col = lax.broadcasted_iota(jnp.int32, (1, 2 * LANES), 1)
            at = jnp.where(col >= LANES, chosen[1], chosen[0]) + jnp.where(col % LANES >= pairs, pairs, 0)
            hot = jnp.where(lax.broadcasted_iota(jnp.int32, (LANES, 2 * LANES), 0) == at, 1.0, 0.0)
            hot = hot.astype(jnp.bfloat16)
            value = jnp.dot(rows_b[...], jnp.concatenate([hot, hot], axis=0), preferred_element_type=f32)
            for k in range(2):
                wgt[z0 + k] = value[:, k * LANES : (k + 1) * LANES].reshape(block, SUBS, LANES) * omega
        return 0

    for j in range(block):
        low, high = (nat[rows, :] for rows in halves(j))
        rows_s[j] = jnp.where(upper, pltpu.roll(high, pairs, 1), low)
    rows_b[...] = jnp.concatenate(split(rows_s[...].reshape(block * SUBS, LANES)), axis=1)
    lax.fori_loop(0, depth // zper, compact, 0)

    for j in range(block):
        x = cell_of(j)
        tile = jnp.where(x < 0, -1, x // LANES)
        inside = (tile >= aper_l) & (tile < aper_l + ntile // 2) & (tile < ntile)
        m = inside.astype(f32)
        mask_s[j] = m
        dist = (x - cell_l).astype(f32)
        c, s = sincos(omega * ray_l * dist)
        src_h[0, 0, j] = (wave_re * c - wave_im * s) * m
        src_h[0, 1, j] = (wave_re * s + wave_im * c) * m
        sct[0, j] = jnp.zeros((SUBS, LANES), f32)
        sct[1, j] = jnp.zeros((SUBS, LANES), f32)

    def up_sub(v):
        v = pltpu.roll(v, 1, 0)
        return jnp.where(sub == 0, pltpu.roll(v, pairs, 1), v)

    def down_sub(v):
        v = pltpu.roll(v, SUBS - 1, 0)
        return jnp.where(sub == SUBS - 1, pltpu.roll(v, pairs, 1), v)

    def forward(z, _):
        zg = z // zper
        idx = (z % zper) * per + lane_f + jnp.where(upper, pairs, 0)

        def born(j):
            w = wgt[z, j]
            sr, si = src_h[z, 0, j], src_h[z, 1, j]
            return sr, si, sct[0, j] - w * si, sct[1, j] + w * sr

        first = born(0)
        last = born(block - 1)
        before = [up_sub(v) for v in last]
        after = [down_sub(v) for v in first]
        now = first
        for j in range(block):
            nxt = after if j == block - 1 else (last if j == block - 2 else born(j + 1))
            both = [a + b for a, b in zip(nxt, before)]
            m = mask_s[j]
            mc = m * pick(cos_c[zg, j], idx)
            ms = m * pick(sin_c[zg, j], idx)
            phase_s[z, 0, j] = mc
            phase_s[z, 1, j] = ms
            s_re = (g_re * now[0] - g_im * now[1]) + both[0]
            s_im = (g_re * now[1] + g_im * now[0]) + both[1]
            d_re = (g_re * now[2] - g_im * now[3]) + both[2]
            d_im = (g_re * now[3] + g_im * now[2]) + both[3]
            src_h[z + 1, 0, j] = s_re * mc - s_im * ms
            src_h[z + 1, 1, j] = s_re * ms + s_im * mc
            sct[0, j] = d_re * mc - d_im * ms
            sct[1, j] = d_re * ms + d_im * mc
            before, now = now, nxt
        return 0

    def forward_four(k, _):
        for i in range(4):
            forward(4 * k + i, 0)
        return 0

    lax.fori_loop(0, depth // 4, forward_four, 0)

    pad = halo - edge
    obs_n[: pad + SUBS, :] = jnp.zeros((pad + SUBS, LANES), f32)
    obs_n[win - pad - SUBS : win, :] = jnp.zeros((pad + SUBS, LANES), f32)
    for t in range(pl.cdiv(own + 2 * edge, LANES)):
        rows_t = min(LANES, own + 2 * edge - t * LANES)
        blk = [
            r[pl.ds(pl.multiple_of(((core * nfc + f) * 2 + part) * shots, SUBS), shots), t * LANES : (t + 1) * LANES]
            for part in range(2)
            for r in obs_refs
            for f in range(nfc)
        ]
        obs_n[pad + t * LANES : pad + t * LANES + rows_t, :] = jnp.concatenate(blk, axis=0).T[:rows_t]
    for j in range(block):
        x = cell_of(j)
        tile = jnp.where(x < 0, -1, x // LANES)
        inside = (tile >= recv_l) & (tile < recv_l + max(1, ntile // 4)) & (tile < ntile)
        m = inside.astype(f32)
        low, high = (obs_n[rows, :] for rows in halves(j))
        turn = pltpu.roll(jnp.where(upper, low, high), pairs, 1)
        adj[0, j] = m * (sct[0, j] - jnp.where(upper, turn, low))
        adj[1, j] = m * (sct[1, j] - jnp.where(upper, high, turn))

    @pl.when(group == 0)
    def _():
        out_mine[...] = jnp.zeros(out_mine.shape, f32)
        out_other[...] = jnp.zeros(out_other.shape, f32)

    weight = omega * scale
    nrow = span // 2
    ncol = pl.cdiv(nrow, LANES) * LANES
    lead = halo - half
    rows_in = slice(lead // 2, lead // 2 + nrow)

    def products(z, odd):
        zi = z - z_first
        for j in range(block):
            for out, a, b in (
                (src_n, src_h[z, 0, j] * weight, src_h[z, 1, j] * -weight),
                (adj_n, adj[1, j], adj[0, j]),
            ):
                turn = pltpu.roll(jnp.where(upper, a, b), pairs, 1)
                low = jnp.where(upper, turn, a)
                high = jnp.where(upper, b, turn)
                out[j % 2, pl.ds(j // 2, SUBS, stride=block // 2), :] = low
                out[j % 2, pl.ds(win // 4 + j // 2, SUBS, stride=block // 2), :] = high
        for p in range(2):
            y = lax.broadcasted_iota(jnp.int32, (nrow, LANES), 0) * 2 + (x_start + lead + p)
            left = src_n[p, rows_in, :]
            right = jnp.where((y >= 0) & (y < cells), adj_n[p, rows_in, :], 0.0)
            if ncol > nrow:
                right = jnp.concatenate([right, jnp.zeros((ncol - nrow, LANES), f32)], axis=0)
            if odd:
                cuts = [right[i : i + pairs] for i in range(0, ncol, pairs)]
                right = jnp.concatenate([cuts[i ^ 1] for i in range(len(cuts))], axis=0)
            lh, ll = split(left)
            rh, rl = split(right)
            dims_t = (((1,), (1,)), ((), ()))
            dot = functools.partial(lax.dot_general, dimension_numbers=dims_t, preferred_element_type=f32)
            prod[zi, p] = dot(lh, rl) + dot(
                jnp.concatenate([lh, ll], axis=1), jnp.concatenate([rh, rh], axis=1)
            )

    slots = LANES // HOFF

    def extract(zg, slab_at, out_ref):
        for b in range(nrow // SUBS):
            for p in range(2):
                rows = slice(b * SUBS, (b + 1) * SUBS)
                first = b * SUBS - half
                near = ((lane - first) & (LANES - 1)) < pairs
                index = (lane % HOFF + sub + first + (lane // HOFF) * pairs) & (LANES - 1)

                def window(z, start):
                    at = max(first, 0)
                    v = prod[z, p, rows, at // LANES * LANES : (at // LANES + 1) * LANES]
                    end = min(b * SUBS + SUBS + half - 1, nrow)
                    if at // LANES < (end - 1) // LANES:
                        v2 = prod[z, p, rows, (at // LANES + 1) * LANES : (at // LANES + 2) * LANES]
                        v = jnp.where(((lane - start) & (LANES - 1)) < at % LANES - SUBS, v2, v)
                    return v

                acc = None
                for q in range(0, slots, 2):
                    z = slab_at + zg * slots + q
                    v = jnp.where(near, window(z, 0), window(z + 1, pairs))
                    v = pick(v, index)
                    acc = v if acc is None else jnp.where(lane >= q * HOFF, v, acc)
                skew[pl.ds(2 * b * SUBS + p, SUBS, stride=2), :] = acc
        tiles = pl.cdiv(span, LANES)
        turned = [skew[t * LANES : (t + 1) * LANES, :].T for t in range(tiles)]
        for q in range(slots):
            for hq in range(HOFF // SUBS):
                rows = slice(q * HOFF + hq * SUBS, q * HOFF + (hq + 1) * SUBS)
                for t in range(pl.cdiv(own, LANES)):
                    v = turned[t][rows]
                    if t + 1 < tiles:
                        v = jnp.where(lane < HOFF - hq * SUBS - sub, turned[t + 1][rows], v)
                    v = pltpu.roll(v, (hq * SUBS - HOFF) % LANES, 1, stride=1, stride_axis=0)
                    width = min(LANES, own - t * LANES)
                    out_ref[zg * slots + q, hq * SUBS : (hq + 1) * SUBS, t * LANES : t * LANES + width] += v[:, :width]

    def backward(k, _):
        z = depth - 1 - k

        def turn(j):
            mc, ms = phase_s[z, 0, j], phase_s[z, 1, j]
            ar, ai = adj[0, j], adj[1, j]
            return ar * mc + ai * ms, ai * mc - ar * ms

        first = turn(0)
        last = turn(block - 1)
        before = [up_sub(v) for v in last]
        after = [down_sub(v) for v in first]
        now = first
        for j in range(block):
            nxt = after if j == block - 1 else (last if j == block - 2 else turn(j + 1))
            adj[0, j] = (g_re * now[0] + g_im * now[1]) + (nxt[0] + before[0])
            adj[1, j] = (g_re * now[1] - g_im * now[0]) + (nxt[1] + before[1])
            before, now = now, nxt

        return 0

    def backward_slab(k, i):
        backward(k, 0)
        products(depth - 1 - k, (i + 1) % 2)
        return 0

    ahead = depth - z_first - slab
    lax.fori_loop(0, ahead, backward, 0)

    def several(k, _):
        for i in range(UNROLL):
            backward_slab(ahead + UNROLL * k + i, i)
        return 0

    lax.fori_loop(0, slab // UNROLL, several, 0)

    for zg in range(zloc // slots):
        extract(zg, (1 - core) * zloc, out_other)
        extract(zg, core * zloc, out_mine)


def local(
    slowness, reflect, omega, spread_coef, wavelet, ray_param, source_cell, aperture_tile, receiver_tile, observed,
):
    nd = lax.axis_size("depth")
    nq = lax.axis_size("freq")
    zloc, cells = slowness.shape
    depth = zloc * nd
    shots, nf, _, _ = observed.shape
    own = cells // nq
    halo = HOFF // 2 + 2 * depth
    win = own + 2 * halo
    block = win // (2 * SUBS)
    wide = pl.cdiv(win, LANES) * LANES
    per = LANES // (2 * shots)
    slot = shots * nf
    groups = nq * slot // LANES
    srcs = LANES // slot
    half = HOFF // 2
    edge = half + depth + half
    obsw = pl.cdiv(own + 2 * edge, LANES) * LANES
    direct = groups == 1 and nq == 8
    smem = pl.BlockSpec(memory_space=pltpu.SMEM)
    rows = 2 * slot + SUBS

    fetch = ((7, 4, 3, 0), (6, 5, 2, 1))
    if direct:
        count = nq // 2
        peers = lambda c, d, k: c ^ jnp.where(d % 2 == 0, fetch[0][k], fetch[1][k])
    else:
        count = nq
        peers = lambda c, d, k: k

    packed = pl.pallas_call(
        functools.partial(
            pack,
            dims=(shots, nf, depth, zloc, cells, own, halo, edge, wide, obsw),
            peers=peers,
        ),
        in_specs=[smem] * 3 + [pl.BlockSpec(memory_space=pltpu.VMEM)] * 3,
        out_shape=[jax.ShapeDtypeStruct((2, zloc, wide), jnp.float32)]
        + [jax.ShapeDtypeStruct((1, rows, obsw), jnp.float32)] * count,
    )(omega, spread_coef, wavelet, slowness, reflect, observed)
    both, parts = {0: packed[0]}, packed[1:]

    def swap(value, bit):
        return lax.ppermute(value, "depth", [(i, i ^ bit) for i in range(nd)])

    bit = nd // 2
    while bit > 1:
        both.update({k ^ bit: swap(v, bit) for k, v in list(both.items())})
        bit //= 2
    if direct:
        parts = [
            lax.ppermute(
                part,
                ("depth", "freq"),
                [(d * nq + i, d * nq + (i ^ fetch[d % 2][k])) for d in range(nd) for i in range(nq)],
            )
            for k, part in enumerate(parts)
        ]
        parts = parts + [swap(part, 1) for part in parts]
    else:
        parts = lax.all_to_all(jnp.stack(parts), "freq", 0, 0).reshape(groups, srcs, rows, obsw)
        parts = [parts[:, k] for k in range(srcs)]
    both.update({k ^ 1: swap(v, 1) for k, v in list(both.items())})
    both = [both[k] for k in range(1, nd)]

    dims = (shots, nf, depth, zloc, cells, own, halo, edge, block, 1.0 / math.sqrt(shots * nf * nq))
    natr = wide
    grid_spec = pltpu.PrefetchScalarGridSpec(
        num_scalar_prefetch=0,
        grid=(groups,),
        in_specs=[
            smem, smem, smem, smem,
        ]
        + [pl.BlockSpec((zloc, cells), lambda g: (0, 0))] * 2
        + [pl.BlockSpec((2, zloc, wide), lambda g: (0, 0, 0))] * (nd - 1)
        + [pl.BlockSpec((None, rows, obsw), lambda g: (g, 0, 0))] * srcs,
        out_specs=[pl.BlockSpec((zloc, HOFF, own), lambda g: (0, 0, 0))] * 2,
        scratch_shapes=[
            pltpu.VMEM((natr, LANES), jnp.float32),
            pltpu.VMEM((block, SUBS, LANES), jnp.float32),
            pltpu.VMEM((block * SUBS, 2 * LANES), jnp.bfloat16),
            pltpu.VMEM((2 * depth * per // LANES, block, SUBS, LANES), jnp.float32),
            pltpu.VMEM((2 * depth * per // LANES, block, SUBS, LANES), jnp.float32),
            pltpu.VMEM((depth, block, SUBS, LANES), jnp.float32),
            pltpu.VMEM((block, SUBS, LANES), jnp.float32),
            pltpu.VMEM((depth, 2, block, SUBS, LANES), jnp.float32),
            pltpu.VMEM((depth + 1, 2, block, SUBS, LANES), jnp.float32),
            pltpu.VMEM((2, block, SUBS, LANES), jnp.float32),
            pltpu.VMEM((2, block, SUBS, LANES), jnp.float32),
            pltpu.VMEM((natr, LANES), jnp.float32),
            pltpu.VMEM((2, win // 2, LANES), jnp.float32),
            pltpu.VMEM((2, win // 2, LANES), jnp.float32),
            pltpu.VMEM((2 * zloc, 2, (own + HOFF) // 2, pl.cdiv((own + HOFF) // 2, LANES) * LANES), jnp.float32),
            pltpu.VMEM((pl.cdiv(own + HOFF, LANES) * LANES, LANES), jnp.float32),
        ],
    )
    mine, other = pl.pallas_call(
        functools.partial(migrate, dims=dims, srcs=srcs, zsrc=nd - 1),
        out_shape=[jax.ShapeDtypeStruct((zloc, HOFF, own), jnp.float32)] * 2,
        grid_spec=grid_spec,
        compiler_params=pltpu.CompilerParams(vmem_limit_bytes=36 << 20),
    )(ray_param, source_cell, aperture_tile, receiver_tile, slowness, reflect, *both, *parts)
    return mine + swap(other, 1)


def solution(mesh):
    return jax.shard_map(
        local,
        mesh=mesh,
        in_specs=(
            P("depth", None), P("depth", None), P("freq"), P("freq"), P("freq", None),
            P(), P(), P(), P(), P(None, "freq", None, None),
        ),
        out_specs=P("depth", None, "freq"),
        check_vma=False,
    )
```

```python
import functools
import math

import jax
import jax.numpy as jnp
from jax import lax
from jax.experimental import pallas as pl
from jax.experimental.pallas import tpu as pltpu
from jax.sharding import PartitionSpec as P

HOFF = 32
LANES = 128
SUBS = 8
UNROLL = 16


def sincos(angle):
    turns = jnp.floor(angle * 0.6366197723675814 + 0.5)
    rem = angle - turns * 1.5703125
    rem = rem - turns * 4.837512969970703125e-4
    rem = rem - turns * 7.54978995489188216e-8
    sq = rem * rem
    sin_p = rem + rem * sq * (-1.6666654611e-1 + sq * (8.3321608736e-3 + sq * -1.9515295891e-4))
    cos_p = (1.0 - 0.5 * sq) + sq * sq * (
        4.166664568298827e-2 + sq * (-1.388731625493765e-3 + sq * 2.443315711809948e-5)
    )
    quad = turns.astype(jnp.int32)
    odd = (quad & 1) == 1
    sine = jnp.where(odd, cos_p, sin_p)
    cosine = jnp.where(odd, sin_p, cos_p)
    sine = jnp.where((quad & 2) == 2, -sine, sine)
    cosine = jnp.where(((quad + 1) & 2) == 2, -cosine, cosine)
    return cosine, sine


def pick(values, index):
    return jnp.take_along_axis(values, index, axis=1, mode="promise_in_bounds")


def split(values):
    high = values.astype(jnp.bfloat16)
    low = (values - high.astype(jnp.float32)).astype(jnp.bfloat16)
    return high, low


def cut_out(load, first, width, cells):
    tiles = pl.cdiv(width, LANES) + 1
    low = first + cells * LANES
    base = low // LANES - cells
    off = low % LANES
    cut = [
        load(pl.ds(pl.multiple_of(jnp.clip(base + t, 0, cells // LANES - 1) * LANES, LANES), LANES))
        for t in range(tiles)
    ]
    full = jnp.concatenate(cut, axis=1)
    return pltpu.roll(full, (tiles * LANES - off) % (tiles * LANES), 1)[:, :width]


def pack(omega, coef, wave, slow_ref, refl_ref, obs_ref, both_ref, *outs, dims, peers):
    shots, nf, depth, zloc, cells, own, halo, edge, wide, obsw = dims
    col = lax.axis_index("freq")
    dev = lax.axis_index("depth")

    first = col * own - halo
    both_ref[0] = cut_out(lambda c: slow_ref[:, c], first, wide, cells)
    both_ref[1] = cut_out(lambda c: refl_ref[:, c], first, wide, cells)
    lane = lax.broadcasted_iota(jnp.int32, (1, obsw), 1) % nf

    def spread(read):
        acc = jnp.zeros((1, obsw), jnp.float32)
        for f in range(nf):
            acc = jnp.where(lane == f, read(f), acc)
        return acc

    table = jnp.concatenate(
        [
            spread(lambda f: omega[f]),
            spread(lambda f: coef[f]),
            spread(lambda f: wave[f, 0]),
            spread(lambda f: wave[f, 1]),
            jnp.zeros((4, obsw), jnp.float32),
        ],
        axis=0,
    )
    def observed_rows(c):
        return jnp.concatenate([obs_ref[:, f, part, c] for f in range(nf) for part in range(2)], axis=0)

    for k, out in enumerate(outs):
        dest = peers(col, dev, k)
        out[0, : 2 * shots * nf] = cut_out(observed_rows, dest * own - edge, obsw, cells)
        out[0, 2 * shots * nf :] = table


def migrate(
    ray, cell, aper, recv, slow, refl, *refs, dims, srcs, zsrc,
):
    sr_refs, (out_mine, out_other, nat, rows_s, rows_b, cos_c, sin_c, wgt, mask_s, phase_s, src_h, sct, adj, obs_n, src_n, adj_n, prod, skew) = refs[: zsrc + srcs], refs[zsrc + srcs :]
    sr_refs, obs_refs = sr_refs[:zsrc], sr_refs[zsrc:]
    shots, nf, depth, zloc, cells, own, halo, edge, block, scale = dims
    half = HOFF // 2
    win = own + 2 * halo
    pairs = LANES // 2
    nfc = nf // 2
    per = pairs // shots
    zper = pairs // per
    span = own + HOFF
    f32 = jnp.float32
    group = pl.program_id(0)
    x_start = lax.axis_index("freq") * own - halo
    dev = lax.axis_index("depth")
    core = dev % 2
    z_first = (dev - core) * zloc
    slab = 2 * zloc

    lane = lax.broadcasted_iota(jnp.int32, (SUBS, LANES), 1)
    sub = lax.broadcasted_iota(jnp.int32, (SUBS, LANES), 0)
    upper = lane >= pairs
    pair = lane % pairs
    lane_src = pair // (shots * nfc)
    lane_shot = pair % shots
    lane_f2 = (pair // shots) % nfc
    lane_f = lane_src * nfc + lane_f2
    lane_own = core * nfc + lane_f2

    obs_rows = 2 * shots * nf
    table = jnp.zeros((SUBS, LANES), jnp.float32)
    for k in range(srcs):
        table = jnp.where(lane_src == k, obs_refs[k][obs_rows:, :LANES], table)

    table = pick(table, lane_src * (shots * nfc) + lane_own)

    def row(k):
        return jnp.broadcast_to(table[k : k + 1, :], (SUBS, LANES))

    omega, coef, wave_re, wave_im = row(0), row(1), row(2), row(3)
    damp = 0.26 - jnp.sqrt(0.0625 - coef * coef)
    comp_f = lane % per
    comp_z = pair // per
    first_lane = (comp_f // nfc) * (shots * nfc) + (comp_f % nfc) * shots
    omega_c, damp_c, coef_c = (pick(v, first_lane) for v in (omega, damp, coef))
    norm = damp * damp + coef * coef
    g_re, g_im = damp / norm - 2.0, -coef / norm

    def per_shot(ref, dtype):
        acc = jnp.zeros((SUBS, LANES), dtype)
        for s in range(shots):
            acc = jnp.where(lane_shot == s, ref[s], acc)
        return acc

    ray_l = per_shot(ray, f32)
    cell_l = per_shot(cell, jnp.int32)
    aper_l = per_shot(aper, jnp.int32)
    recv_l = per_shot(recv, jnp.int32)
    ntile = cells // LANES

    rows2 = 2 * depth
    wide = pl.cdiv(win, LANES) * LANES
    mine = [cut_out(lambda c: ref[:, c], x_start, wide, cells) for ref in (slow, refl)]
    for t in range(pl.cdiv(win, LANES)):
        cut = slice(t * LANES, (t + 1) * LANES)
        blk = sum(([mine[part][:, cut]] + [r[part, :, cut] for r in sr_refs] for part in range(2)), [])
        blk = jnp.concatenate(blk + [jnp.zeros((LANES - rows2, LANES), f32)], axis=0)
        nat[t * LANES : (t + 1) * LANES, :] = blk.T

    def halves(j):
        return pl.ds(j, SUBS, stride=block), pl.ds(win // 2 + j, SUBS, stride=block)

    def cell_of(j):
        return x_start + (sub + jnp.where(upper, SUBS, 0)) * block + j

    def compact(zg, _):
        z = zg * zper + comp_z
        zrow = ((z // zloc) ^ dev) * zloc + z % zloc + jnp.where(upper, pairs, 0)
        for j in range(block):
            c, s = sincos(omega_c * pick(rows_s[j], zrow))
            cos_c[zg, j] = c * damp_c - s * coef_c
            sin_c[zg, j] = c * coef_c + s * damp_c
        for i in range(0, zper, 2):
            z0 = zg * zper + i
            chosen = [depth + ((z // zloc) ^ dev) * zloc + z % zloc for z in (z0, z0 + 1)]
            col = lax.broadcasted_iota(jnp.int32, (1, 2 * LANES), 1)
            at = jnp.where(col >= LANES, chosen[1], chosen[0]) + jnp.where(col % LANES >= pairs, pairs, 0)
            hot = jnp.where(lax.broadcasted_iota(jnp.int32, (LANES, 2 * LANES), 0) == at, 1.0, 0.0)
            hot = hot.astype(jnp.bfloat16)
            value = jnp.dot(rows_b[...], jnp.concatenate([hot, hot], axis=0), preferred_element_type=f32)
            for k in range(2):
                wgt[z0 + k] = value[:, k * LANES : (k + 1) * LANES].reshape(block, SUBS, LANES) * omega
        return 0

    for j in range(block):
        low, high = (nat[rows, :] for rows in halves(j))
        rows_s[j] = jnp.where(upper, pltpu.roll(high, pairs, 1), low)
    rows_b[...] = jnp.concatenate(split(rows_s[...].reshape(block * SUBS, LANES)), axis=1)
    def compact_two(k, _):
        compact(2 * k, 0)
        compact(2 * k + 1, 0)
        return 0

    lax.fori_loop(0, depth // (2 * zper), compact_two, 0)

    for j in range(block):
        x = cell_of(j)
        tile = jnp.where(x < 0, -1, x // LANES)
        inside = (tile >= aper_l) & (tile < aper_l + ntile // 2) & (tile < ntile)
        m = inside.astype(f32)
        mask_s[j] = m
        dist = (x - cell_l).astype(f32)
        c, s = sincos(omega * ray_l * dist)
        src_h[0, 0, j] = (wave_re * c - wave_im * s) * m
        src_h[0, 1, j] = (wave_re * s + wave_im * c) * m
        sct[0, j] = jnp.zeros((SUBS, LANES), f32)
        sct[1, j] = jnp.zeros((SUBS, LANES), f32)

    def up_sub(v):
        v = pltpu.roll(v, 1, 0)
        return jnp.where(sub == 0, pltpu.roll(v, pairs, 1), v)

    def down_sub(v):
        v = pltpu.roll(v, SUBS - 1, 0)
        return jnp.where(sub == SUBS - 1, pltpu.roll(v, pairs, 1), v)

    def forward(z, _):
        zg = z // zper
        idx = (z % zper) * per + lane_f + jnp.where(upper, pairs, 0)

        def born(j):
            w = wgt[z, j]
            sr, si = src_h[z, 0, j], src_h[z, 1, j]
            return sr, si, sct[0, j] - w * si, sct[1, j] + w * sr

        first = born(0)
        last = born(block - 1)
        before = [up_sub(v) for v in last]
        after = [down_sub(v) for v in first]
        now = first
        for j in range(block):
            nxt = after if j == block - 1 else (last if j == block - 2 else born(j + 1))
            both = [a + b for a, b in zip(nxt, before)]
            m = mask_s[j]
            mc = m * pick(cos_c[zg, j], idx)
            ms = m * pick(sin_c[zg, j], idx)
            phase_s[z, 0, j] = mc
            phase_s[z, 1, j] = ms
            s_re = (g_re * now[0] - g_im * now[1]) + both[0]
            s_im = (g_re * now[1] + g_im * now[0]) + both[1]
            d_re = (g_re * now[2] - g_im * now[3]) + both[2]
            d_im = (g_re * now[3] + g_im * now[2]) + both[3]
            src_h[z + 1, 0, j] = s_re * mc - s_im * ms
            src_h[z + 1, 1, j] = s_re * ms + s_im * mc
            sct[0, j] = d_re * mc - d_im * ms
            sct[1, j] = d_re * ms + d_im * mc
            before, now = now, nxt
        return 0

    def forward_four(k, _):
        for i in range(4):
            forward(4 * k + i, 0)
        return 0

    lax.fori_loop(0, depth // 4, forward_four, 0)

    pad = halo - edge
    obs_n[: pad + SUBS, :] = jnp.zeros((pad + SUBS, LANES), f32)
    obs_n[win - pad - SUBS : win, :] = jnp.zeros((pad + SUBS, LANES), f32)
    for t in range(pl.cdiv(own + 2 * edge, LANES)):
        rows_t = min(LANES, own + 2 * edge - t * LANES)
        blk = [
            r[pl.ds(pl.multiple_of(((core * nfc + f) * 2 + part) * shots, SUBS), shots), t * LANES : (t + 1) * LANES]
            for part in range(2)
            for r in obs_refs
            for f in range(nfc)
        ]
        obs_n[pad + t * LANES : pad + t * LANES + rows_t, :] = jnp.concatenate(blk, axis=0).T[:rows_t]
    for j in range(block):
        x = cell_of(j)
        tile = jnp.where(x < 0, -1, x // LANES)
        inside = (tile >= recv_l) & (tile < recv_l + max(1, ntile // 4)) & (tile < ntile)
        m = inside.astype(f32)
        low, high = (obs_n[rows, :] for rows in halves(j))
        turn = pltpu.roll(jnp.where(upper, low, high), pairs, 1)
        adj[0, j] = m * (sct[0, j] - jnp.where(upper, turn, low))
        adj[1, j] = m * (sct[1, j] - jnp.where(upper, high, turn))

    @pl.when(group == 0)
    def _():
        out_mine[...] = jnp.zeros(out_mine.shape, f32)
        out_other[...] = jnp.zeros(out_other.shape, f32)

    weight = omega * scale
    nrow = span // 2
    ncol = pl.cdiv(nrow, LANES) * LANES
    lead = halo - half
    rows_in = slice(lead // 2, lead // 2 + nrow)

    def products(z, odd):
        zi = z - z_first
        for j in range(block):
            for out, a, b in (
                (src_n, src_h[z, 0, j] * weight, src_h[z, 1, j] * -weight),
                (adj_n, adj[1, j], adj[0, j]),
            ):
                turn = pltpu.roll(jnp.where(upper, a, b), pairs, 1)
                low = jnp.where(upper, turn, a)
                high = jnp.where(upper, b, turn)
                out[j % 2, pl.ds(j // 2, SUBS, stride=block // 2), :] = low
                out[j % 2, pl.ds(win // 4 + j // 2, SUBS, stride=block // 2), :] = high
        for p in range(2):
            y = lax.broadcasted_iota(jnp.int32, (nrow, LANES), 0) * 2 + (x_start + lead + p)
            left = src_n[p, rows_in, :]
            right = jnp.where((y >= 0) & (y < cells), adj_n[p, rows_in, :], 0.0)
            if ncol > nrow:
                right = jnp.concatenate([right, jnp.zeros((ncol - nrow, LANES), f32)], axis=0)
            if odd:
                cuts = [right[i : i + pairs] for i in range(0, ncol, pairs)]
                right = jnp.concatenate([cuts[i ^ 1] for i in range(len(cuts))], axis=0)
            lh, ll = split(left)
            rh, rl = split(right)
            dims_t = (((1,), (1,)), ((), ()))
            dot = functools.partial(lax.dot_general, dimension_numbers=dims_t, preferred_element_type=f32)
            prod[zi, p] = dot(lh, rl) + dot(
                jnp.concatenate([lh, ll], axis=1), jnp.concatenate([rh, rh], axis=1)
            )

    slots = LANES // HOFF

    def extract(zg, slab_at, out_ref):
        for b in range(nrow // SUBS):
            for p in range(2):
                rows = slice(b * SUBS, (b + 1) * SUBS)
                first = b * SUBS - half
                near = ((lane - first) & (LANES - 1)) < pairs
                index = (lane % HOFF + sub + first + (lane // HOFF) * pairs) & (LANES - 1)

                def window(z, start):
                    at = max(first, 0)
                    v = prod[z, p, rows, at // LANES * LANES : (at // LANES + 1) * LANES]
                    end = min(b * SUBS + SUBS + half - 1, nrow)
                    if at // LANES < (end - 1) // LANES:
                        v2 = prod[z, p, rows, (at // LANES + 1) * LANES : (at // LANES + 2) * LANES]
                        v = jnp.where(((lane - start) & (LANES - 1)) < at % LANES - SUBS, v2, v)
                    return v

                acc = None
                for q in range(0, slots, 2):
                    z = slab_at + zg * slots + q
                    v = jnp.where(near, window(z, 0), window(z + 1, pairs))
                    v = pick(v, index)
                    acc = v if acc is None else jnp.where(lane >= q * HOFF, v, acc)
                skew[pl.ds(2 * b * SUBS + p, SUBS, stride=2), :] = acc
        tiles = pl.cdiv(span, LANES)
        turned = [skew[t * LANES : (t + 1) * LANES, :].T for t in range(tiles)]
        for q in range(slots):
            for hq in range(HOFF // SUBS):
                rows = slice(q * HOFF + hq * SUBS, q * HOFF + (hq + 1) * SUBS)
                for t in range(pl.cdiv(own, LANES)):
                    v = turned[t][rows]
                    if t + 1 < tiles:
                        v = jnp.where(lane < HOFF - hq * SUBS - sub, turned[t + 1][rows], v)
                    v = pltpu.roll(v, (hq * SUBS - HOFF) % LANES, 1, stride=1, stride_axis=0)
                    width = min(LANES, own - t * LANES)
                    out_ref[zg * slots + q, hq * SUBS : (hq + 1) * SUBS, t * LANES : t * LANES + width] += v[:, :width]

    def backward(k, _):
        z = depth - 1 - k

        def turn(j):
            mc, ms = phase_s[z, 0, j], phase_s[z, 1, j]
            ar, ai = adj[0, j], adj[1, j]
            return ar * mc + ai * ms, ai * mc - ar * ms

        first = turn(0)
        last = turn(block - 1)
        before = [up_sub(v) for v in last]
        after = [down_sub(v) for v in first]
        now = first
        for j in range(block):
            nxt = after if j == block - 1 else (last if j == block - 2 else turn(j + 1))
            adj[0, j] = (g_re * now[0] + g_im * now[1]) + (nxt[0] + before[0])
            adj[1, j] = (g_re * now[1] - g_im * now[0]) + (nxt[1] + before[1])
            before, now = now, nxt

        return 0

    def backward_slab(k, i):
        backward(k, 0)
        products(depth - 1 - k, (i + 1) % 2)
        return 0

    ahead = depth - z_first - slab
    lax.fori_loop(0, ahead, backward, 0)

    def several(k, _):
        for i in range(UNROLL):
            backward_slab(ahead + UNROLL * k + i, i)
        return 0

    lax.fori_loop(0, slab // UNROLL, several, 0)

    for zg in range(zloc // slots):
        extract(zg, (1 - core) * zloc, out_other)
        extract(zg, core * zloc, out_mine)


def local(
    slowness, reflect, omega, spread_coef, wavelet, ray_param, source_cell, aperture_tile, receiver_tile, observed,
):
    nd = lax.axis_size("depth")
    nq = lax.axis_size("freq")
    zloc, cells = slowness.shape
    depth = zloc * nd
    shots, nf, _, _ = observed.shape
    own = cells // nq
    halo = HOFF // 2 + 2 * depth
    win = own + 2 * halo
    block = win // (2 * SUBS)
    wide = pl.cdiv(win, LANES) * LANES
    per = LANES // (2 * shots)
    slot = shots * nf
    groups = nq * slot // LANES
    srcs = LANES // slot
    half = HOFF // 2
    edge = half + depth + half
    obsw = pl.cdiv(own + 2 * edge, LANES) * LANES
    direct = groups == 1 and nq == 8
    smem = pl.BlockSpec(memory_space=pltpu.SMEM)
    rows = 2 * slot + SUBS

    fetch = ((7, 4, 3, 0), (6, 5, 2, 1))
    if direct:
        count = nq // 2
        peers = lambda c, d, k: c ^ jnp.where(d % 2 == 0, fetch[0][k], fetch[1][k])
    else:
        count = nq
        peers = lambda c, d, k: k

    packed = pl.pallas_call(
        functools.partial(
            pack,
            dims=(shots, nf, depth, zloc, cells, own, halo, edge, wide, obsw),
            peers=peers,
        ),
        in_specs=[smem] * 3 + [pl.BlockSpec(memory_space=pltpu.VMEM)] * 3,
        out_shape=[jax.ShapeDtypeStruct((2, zloc, wide), jnp.float32)]
        + [jax.ShapeDtypeStruct((1, rows, obsw), jnp.float32)] * count,
    )(omega, spread_coef, wavelet, slowness, reflect, observed)
    both, parts = {0: packed[0]}, packed[1:]

    def swap(value, bit):
        return lax.ppermute(value, "depth", [(i, i ^ bit) for i in range(nd)])

    bit = nd // 2
    while bit > 1:
        both.update({k ^ bit: swap(v, bit) for k, v in list(both.items())})
        bit //= 2
    if direct:
        parts = [
            lax.ppermute(
                part,
                ("depth", "freq"),
                [(d * nq + i, d * nq + (i ^ fetch[d % 2][k])) for d in range(nd) for i in range(nq)],
            )
            for k, part in enumerate(parts)
        ]
        parts = parts + [swap(part, 1) for part in parts]
    else:
        parts = lax.all_to_all(jnp.stack(parts), "freq", 0, 0).reshape(groups, srcs, rows, obsw)
        parts = [parts[:, k] for k in range(srcs)]
    both.update({k ^ 1: swap(v, 1) for k, v in list(both.items())})
    both = [both[k] for k in range(1, nd)]

    dims = (shots, nf, depth, zloc, cells, own, halo, edge, block, 1.0 / math.sqrt(shots * nf * nq))
    natr = wide
    grid_spec = pltpu.PrefetchScalarGridSpec(
        num_scalar_prefetch=0,
        grid=(groups,),
        in_specs=[
            smem, smem, smem, smem,
        ]
        + [pl.BlockSpec((zloc, cells), lambda g: (0, 0))] * 2
        + [pl.BlockSpec((2, zloc, wide), lambda g: (0, 0, 0))] * (nd - 1)
        + [pl.BlockSpec((None, rows, obsw), lambda g: (g, 0, 0))] * srcs,
        out_specs=[pl.BlockSpec((zloc, HOFF, own), lambda g: (0, 0, 0))] * 2,
        scratch_shapes=[
            pltpu.VMEM((natr, LANES), jnp.float32),
            pltpu.VMEM((block, SUBS, LANES), jnp.float32),
            pltpu.VMEM((block * SUBS, 2 * LANES), jnp.bfloat16),
            pltpu.VMEM((2 * depth * per // LANES, block, SUBS, LANES), jnp.float32),
            pltpu.VMEM((2 * depth * per // LANES, block, SUBS, LANES), jnp.float32),
            pltpu.VMEM((depth, block, SUBS, LANES), jnp.float32),
            pltpu.VMEM((block, SUBS, LANES), jnp.float32),
            pltpu.VMEM((depth, 2, block, SUBS, LANES), jnp.float32),
            pltpu.VMEM((depth + 1, 2, block, SUBS, LANES), jnp.float32),
            pltpu.VMEM((2, block, SUBS, LANES), jnp.float32),
            pltpu.VMEM((2, block, SUBS, LANES), jnp.float32),
            pltpu.VMEM((natr, LANES), jnp.float32),
            pltpu.VMEM((2, win // 2, LANES), jnp.float32),
            pltpu.VMEM((2, win // 2, LANES), jnp.float32),
            pltpu.VMEM((2 * zloc, 2, (own + HOFF) // 2, pl.cdiv((own + HOFF) // 2, LANES) * LANES), jnp.float32),
            pltpu.VMEM((pl.cdiv(own + HOFF, LANES) * LANES, LANES), jnp.float32),
        ],
    )
    mine, other = pl.pallas_call(
        functools.partial(migrate, dims=dims, srcs=srcs, zsrc=nd - 1),
        out_shape=[jax.ShapeDtypeStruct((zloc, HOFF, own), jnp.float32)] * 2,
        grid_spec=grid_spec,
        compiler_params=pltpu.CompilerParams(vmem_limit_bytes=36 << 20),
    )(ray_param, source_cell, aperture_tile, receiver_tile, slowness, reflect, *both, *parts)
    return mine + swap(other, 1)


def solution(mesh):
    return jax.shard_map(
        local,
        mesh=mesh,
        in_specs=(
            P("depth", None), P("depth", None), P("freq"), P("freq"), P("freq", None),
            P(), P(), P(), P(), P(None, "freq", None, None),
        ),
        out_specs=P("depth", None, "freq"),
        check_vma=False,
    )
```
